256 devices in a mesh: replica: 16 (over z, core), ctx: 16 (over x, y).
Axes of the slice: x: 4, y: 4, z: 8, core: 2. Of those that a mesh axis runs over, the one named last changes fastest.
Arguments:
- queries: bfloat16 [64, 128, 3584], P('replica', 'ctx'), may hold values from -128 to 128
- key_cache: bfloat16 [16384, 512], P('ctx'), may hold values from -6 to 6
- value_cache: bfloat16 [16384, 512], P('ctx'), may hold values from -6 to 6
- key_scale: float32 [128, 4], P('ctx'), may hold values from 0.7 to 1.4
- value_scale: float32 [128, 4], P('ctx'), may hold values from 0.5 to 2
- pattern: int32 [28, 64, 32], replicated, may hold values from 0 to 127
- target: int32 [64], replicated, may hold values from 0 to 15, as said below
Outputs:
- landed: bfloat16 [64, 128, 3584], P('replica', 'ctx')
The draws below stay inside these ranges and needn't reach their ends.
Inputs may be any that keep to these rules, and one draw needn't show every extreme that they name: `target`: query block j belongs to group j // 4. The blocks of one group go to distinct groups, and every group receives exactly 4 blocks.
All inputs are finite; a program needn't handle non-finite values.
Results may differ from the reference program's by a relative error of at most 0.018.
Values may be sent and summed in bfloat16 or wider, within the bound.
A program may use at most 64 MiB of HBM per device.

```python
import math
import jax
import jax.numpy as jnp
from jax import lax

HEADS = 28
KV_HEADS = 4
HEAD_DIM = 128
BLOCK = 128
SELECTED = 32
CTX_DEV = 1024
QBLK_DEV = 4
GROUPS = 16
SHARDS = 16
QBLOCKS = 64
KVBLOCKS = 128


def paired_draw(key):
    folded = jax.random.fold_in(key, 5)
    query_key, cache_key = jax.random.split(folded, 2)
    row_width = HEADS * HEAD_DIM
    query_base = jax.random.truncated_normal(query_key, -6.0, 6.0, (QBLOCKS, BLOCK, row_width), jnp.float32)
    cache_base = jax.random.truncated_normal(cache_key, -6.0, 6.0, (KVBLOCKS * BLOCK, KV_HEADS * HEAD_DIM), jnp.float32)
    return (query_base, cache_base)


def draw_queries(key, part):
    return paired_draw(key)[0].astype(jnp.bfloat16)


def draw_key_cache(key, part):
    return paired_draw(key)[1].astype(jnp.bfloat16)


def draw_target(key, part):
    first_key, second_key = jax.random.split(jax.random.fold_in(key, 11))
    ordering = jax.random.permutation(first_key, GROUPS)
    shifts = jax.random.permutation(second_key, GROUPS)[:QBLK_DEV]
    inverse = jnp.argsort(ordering)
    return ordering[(inverse[:, None] + shifts[None, :]) % GROUPS].reshape(QBLOCKS).astype(jnp.int32)


def set_ends(array, own_key, smallest, top_value):
    extent = array.shape
    index_at = [jax.random.randint(jax.random.fold_in(own_key, axis), (), 0, extent[axis]) for axis in range(len(extent))]
    array = array.at[tuple(index_at)].set(smallest)
    longest = extent.index(max(extent))
    index_at[longest] = (index_at[longest] + 1) % extent[longest]
    return array.at[tuple(index_at)].set(top_value)


def block_scale(rng, dims, pieces, least, top_value):
    level, own = 1.0, jax.random.fold_in(rng, 6)
    for position, parts in pieces:
        draws = jnp.exp(jax.random.uniform(jax.random.fold_in(own, position), (parts,), jnp.float32, least / len(pieces), top_value / len(pieces)))
        level = level * jnp.repeat(draws, dims[position] // parts).reshape([-1 if axis == position else 1 for axis in range(len(dims))])
    return level


def bell_draw(own_key, extent, scale, limit, cuts=(), kind=jnp.bfloat16):
    result = jax.random.normal(own_key, extent, jnp.float32) * scale
    if len(cuts) > 0:
        result = block_scale(own_key, extent, cuts, -0.22, 0.18) * result
    return jnp.clip(result, min=-limit, max=limit).astype(kind)


def setup_inputs(seed: int = 0) -> dict:
    splits = jax.random.split(jax.random.key(seed), 8)
    queries = draw_queries(jax.random.fold_in(splits[7], 71), 0)
    key_cache = draw_key_cache(jax.random.fold_in(splits[7], 71), 0)
    value_cache = bell_draw(splits[2], (KVBLOCKS * BLOCK, KV_HEADS * HEAD_DIM), 1.0, 6.0, ((0, 16),))
    key_scale = jnp.clip(jnp.exp(math.log(1.4) - 0.6931472 * jax.random.uniform(splits[3], (KVBLOCKS, KV_HEADS), jnp.float32) ** block_scale(splits[3], (KVBLOCKS, KV_HEADS), ((0, 16),), -0.2, 0.2)), 0.7, 1.4)
    value_scale = jnp.clip(jnp.exp(math.log(2.0) - 1.3862944 * jax.random.uniform(splits[4], (KVBLOCKS, KV_HEADS), jnp.float32) ** block_scale(splits[4], (KVBLOCKS, KV_HEADS), ((0, 16),), -0.2, 0.2)), 0.5, 2.0)
    pattern = set_ends(jax.random.randint(splits[5], (HEADS, QBLOCKS, SELECTED), 0, KVBLOCKS), jax.random.fold_in(splits[5], 1), 0, KVBLOCKS - 1).astype(jnp.int32)
    target = draw_target(jax.random.fold_in(splits[7], 71), 0)
    return dict(queries=queries, key_cache=key_cache, value_cache=value_cache, key_scale=key_scale, value_scale=value_scale, pattern=pattern, target=target)


def reference(queries, key_cache, value_cache, key_scale, value_scale, pattern, target):
    group_size = HEADS // KV_HEADS
    local_blocks = CTX_DEV // BLOCK
    first_block = KVBLOCKS - QBLOCKS
    inv_root = 1.0 / math.sqrt(HEAD_DIM)
    keys_all = key_cache.astype(jnp.float32).reshape(SHARDS, local_blocks, BLOCK, KV_HEADS, HEAD_DIM)
    values_all = value_cache.astype(jnp.float32).reshape(SHARDS, local_blocks, BLOCK, KV_HEADS, HEAD_DIM)
    key_factor = jnp.transpose(key_scale.reshape(SHARDS, local_blocks, KV_HEADS), (2, 0, 1)) * inv_root
    value_factor = jnp.transpose(value_scale.reshape(SHARDS, local_blocks, KV_HEADS), (2, 0, 1))
    block_ids = jnp.arange(KVBLOCKS, dtype=jnp.int32)
    key_pos = jnp.arange(KVBLOCKS * BLOCK, dtype=jnp.int32).reshape(SHARDS, local_blocks, BLOCK)
    row_ids = jnp.arange(BLOCK, dtype=jnp.int32)

    def one_block(operands):
        query_block, listed, block_index = operands
        diagonal = first_block + block_index
        chosen = jnp.any(listed[:, :, None] == block_ids[None, None, :], axis=1) | (block_ids == diagonal)[None, :]
        chosen = chosen.reshape(KV_HEADS, group_size, SHARDS, local_blocks)
        query_pos = diagonal * BLOCK + row_ids
        causal = key_pos[None] <= query_pos[:, None, None, None]
        allowed = chosen[:, :, None, :, :, None] & causal[None, None]
        query_f = query_block.astype(jnp.float32).reshape(BLOCK, KV_HEADS, group_size, HEAD_DIM)
        scores = jnp.einsum('rgkd,sbtgd->gkrsbt', query_f, keys_all) * key_factor[:, None, None, :, :, None]
        local_top = lax.optimization_barrier(jnp.max(jnp.where(allowed, scores, -jnp.inf), axis=(4, 5), keepdims=True))
        top_score = lax.optimization_barrier(jnp.max(local_top, axis=3, keepdims=True))
        rescale = jnp.exp(local_top - top_score)
        expo = jnp.where(allowed, jnp.exp(scores - local_top), 0.0)
        weight = (expo * value_factor[:, None, None, :, :, None]).astype(jnp.bfloat16)
        weight = lax.optimization_barrier(weight).astype(jnp.float32)
        rescale_t = jnp.transpose(rescale[:, :, :, :, 0, 0], (3, 2, 0, 1))
        numer_part = (jnp.einsum('gkrsbt,sbtgd->srgkd', weight, values_all) * rescale_t[..., None]).astype(jnp.bfloat16)
        denom_part = (jnp.transpose(lax.optimization_barrier(jnp.sum(expo, axis=(4, 5))), (3, 2, 0, 1)) * rescale_t).astype(jnp.bfloat16)
        numer_part = lax.optimization_barrier(numer_part)
        denom_part = lax.optimization_barrier(denom_part)
        numer_sum = lax.optimization_barrier(jnp.sum(numer_part.astype(jnp.float32), axis=0))
        denom_sum = lax.optimization_barrier(jnp.sum(denom_part.astype(jnp.float32), axis=0))
        attended = numer_sum / denom_sum[..., None]
        return attended.reshape(BLOCK, HEADS * HEAD_DIM).astype(jnp.bfloat16)
    attended_all = lax.map(one_block, (queries, jnp.transpose(pattern, (1, 0, 2)), jnp.arange(QBLOCKS, dtype=jnp.int32)))
    arrival_order = jnp.argsort(target, stable=True).astype(jnp.int32)
    return jnp.take(attended_all, arrival_order, axis=0)
```

```python
import functools
import math

import jax
import jax.numpy as jnp
from jax import lax
from jax.experimental import pallas as pl
from jax.experimental.pallas import tpu as pltpu
from jax.sharding import PartitionSpec as P

MESH = pl.DeviceIdType.MESH
BF16 = jnp.bfloat16
F32 = jnp.float32

NX = 4
NY = 4
NZ = 8
HEADS = 7
D = 128
B = 128
QB = 4
KB = 32
SLICE = HEADS * D
WIDE = SLICE + 128
ROWS = B // (NX * NY)
SUM_LANE = 64
NEG = -(2.0**100)
STEP = 2
FIRST = 64


def place():
    rep = lax.axis_index("replica")
    ctx = lax.axis_index("ctx")
    return rep, rep // 2, rep % 2, ctx // NY, ctx % NY


def greet(partners):
    barrier = pltpu.get_barrier_semaphore()
    for who in partners:
        pl.semaphore_signal(barrier, inc=1, device_id=who, device_id_type=MESH)
    pl.semaphore_wait(barrier, len(partners))


def remote(src, dst, send, recv, who):
    return pltpu.make_async_remote_copy(
        src_ref=src, dst_ref=dst, send_sem=send, recv_sem=recv, device_id=who, device_id_type=MESH
    )


def spread_kernel(
    q, k, v, sc, q_all, k_all, v_all, s_all,
    q_send, q_recv, k_send, k_recv, v_send, v_recv, s_send, s_recv,
    up_send, up_recv, dn_send, dn_recv, f_send, f_recv, kc_send, kc_recv, vc_send, vc_recv, own,
):
    rep, z, c, x, y = place()
    sib = (rep + 1 - 2 * c, x * NY + y)
    xs = [(x + d) % NX for d in range(NX)]
    back = [(x + NX - d) % NX for d in range(NX)]
    at_x = [(rep, xs[d] * NY + y) for d in range(NX)]
    up = (rep, x * NY + (y + 1) % NY)
    down = (rep, x * NY + (y + NY - 1) % NY)
    below, above = (y + NY - 1) % NY, (y + 1) % NY
    half = pl.ds(c * 512, 512)
    greet([at_x[1], at_x[2], at_x[3], up, down, sib])

    def cols(d, n):
        return pl.ds(pl.multiple_of(xs[d] * n, n), n)

    qx = [None] * NX
    kx = [None] * NX
    vx = [None] * NX
    sx = [None] * NX
    order = (1, 3, 2)
    for d in order:
        qx[d] = remote(q.at[:, :, cols(d, SLICE)], q_all.at[y, x], q_send.at[d], q_recv.at[d], at_x[d])
        qx[d].start()
    own_q = q.at[:, :, cols(0, SLICE)]
    ups = [None] * NX
    dns = [None] * NX
    ups[0] = remote(own_q, q_all.at[y, x], up_send.at[0], up_recv.at[0], up)
    dns[0] = remote(own_q, q_all.at[y, x], dn_send.at[0], dn_recv.at[0], down)
    ups[0].start()
    dns[0].start()
    for d in order:
        kx[d] = remote(k.at[half, cols(d, D)], k_all.at[x, half], k_send.at[d], k_recv.at[d], at_x[d])
        vx[d] = remote(v.at[half, cols(d, D)], v_all.at[x, half], v_send.at[d], v_recv.at[d], at_x[d])
        sx[d] = remote(sc, s_all.at[x], s_send.at[d], s_recv.at[d], at_x[d])
        kx[d].start()
        vx[d].start()
        sx[d].start()
    stay = [
        pltpu.make_async_copy(own_q, q_all.at[y, x], own.at[0]),
        pltpu.make_async_copy(k.at[:, cols(0, D)], k_all.at[x], own.at[1]),
        pltpu.make_async_copy(v.at[:, cols(0, D)], v_all.at[x], own.at[2]),
        pltpu.make_async_copy(sc, s_all.at[x], own.at[3]),
    ]
    for copy in stay:
        copy.start()
    for d in order:
        qx[d].wait_recv()
        piece = q_all.at[y, back[d]]
        ups[d] = remote(piece, piece, up_send.at[d], up_recv.at[d], up)
        dns[d] = remote(piece, piece, dn_send.at[d], dn_recv.at[d], down)
        ups[d].start()
        dns[d].start()
    on = [None] * NX
    for d in (0, 1):
        ups[d].wait_recv()
        piece = q_all.at[below, back[d]]
        on[d] = remote(piece, piece, f_send.at[d], f_recv.at[d], up)
        on[d].start()
    for d in (3, 2):
        dns[d].wait_recv()
        piece = q_all.at[above, back[d]]
        on[d] = remote(piece, piece, f_send.at[d], f_recv.at[d], down)
        on[d].start()
    kc = [None] * NX
    vc = [None] * NX
    for d in order:
        kx[d].wait_recv()
        piece = k_all.at[back[d], half]
        kc[d] = remote(piece, piece, kc_send.at[d], kc_recv.at[d], sib)
        kc[d].start()
        vx[d].wait_recv()
        piece = v_all.at[back[d], half]
        vc[d] = remote(piece, piece, vc_send.at[d], vc_recv.at[d], sib)
        vc[d].start()
        sx[d].wait_recv()
    for d in (2, 3):
        ups[d].wait_recv()
    for d in (0, 1):
        dns[d].wait_recv()
    for d in range(NX):
        on[d].wait_recv()
        on[d].wait_send()
        ups[d].wait_send()
        dns[d].wait_send()
    for d in order:
        kc[d].wait_recv()
        vc[d].wait_recv()
        kc[d].wait_send()
        vc[d].wait_send()
        qx[d].wait_send()
        kx[d].wait_send()
        vx[d].wait_send()
        sx[d].wait_send()
    for copy in stay:
        copy.wait()


def spread(q, k, v, sc):
    dma = pltpu.SemaphoreType.DMA((NX,))
    any_space = pl.BlockSpec(memory_space=pl.ANY)
    return pl.pallas_call(
        spread_kernel,
        out_shape=[
            jax.ShapeDtypeStruct((NY, NX, QB, ROWS, SLICE), BF16),
            jax.ShapeDtypeStruct((NX, 1024, D), BF16),
            jax.ShapeDtypeStruct((NX, 1024, D), BF16),
            jax.ShapeDtypeStruct((NX, 8, 128), F32),
        ],
        in_specs=[any_space] * 4,
        out_specs=[any_space] * 4,
        scratch_shapes=[dma] * 19,
        compiler_params=pltpu.CompilerParams(collective_id=0, has_side_effects=True),
        name="spread",
    )(q, k, v, sc)


def attend_kernel(
    ints, steps, where_x, q_ref, k_ref, v_ref, s_ref, out_ref, vs, qs, sc, mx, acc, su
):
    qb = pl.program_id(0)
    hx = where_x[0]

    @pl.when(qb == 0)
    def _():
        @pl.loop(0, KB)
        def _(kb):
            factor = s_ref[kb // 8, kb % 8, 4 + hx]
            vs[kb] = (v_ref[kb].astype(F32) * factor).astype(BF16)

    qs[...] = q_ref[:, :, 0].astype(F32).reshape(B, SLICE).astype(BF16)
    mx[...] = jnp.full(mx.shape, NEG, F32)
    acc[...] = jnp.zeros(acc.shape, F32)
    su[...] = jnp.zeros(su.shape, F32)
    row = lax.broadcasted_iota(jnp.int32, (B, B), 0)
    row = ((row // 8) % 4) * 32 + (row // 32) * 8 + row % 8
    ahead = lax.broadcasted_iota(jnp.int32, (B, B), 1) - row
    count = steps[qb]
    to_log2 = math.log2(math.e) / math.sqrt(D)

    @pl.loop(0, count)
    def _(t):
        for h in range(HEADS):
            top = mx[h]
            for u in range(STEP):
                code = ints[(qb * HEADS + h) * KB + t * STEP + u]
                kb = code & (KB - 1)
                reach = (code >> 5) * B
                factor = s_ref[kb // 8, kb % 8, hx] * to_log2
                score = lax.dot_general(
                    qs[:, h * D : (h + 1) * D],
                    k_ref[kb],
                    (((1,), (1,)), ((), ())),
                    preferred_element_type=F32,
                )
                score = jnp.where(ahead <= reach, score * factor, NEG)
                sc[h, t * STEP + u] = score
                top = jnp.maximum(top, score)
            mx[h] = top

    for h in range(HEADS):
        top = jnp.max(mx[h], axis=1, keepdims=True)
        mx[h] = jnp.broadcast_to(top, (B, B)).astype(BF16).astype(F32)

    @pl.loop(0, count)
    def _(t):
        for h in range(HEADS):
            top = mx[h]
            total = su[h]
            weights = []
            values = []
            for u in range(STEP):
                code = ints[(qb * HEADS + h) * KB + t * STEP + u]
                weight = jnp.exp2(sc[h, t * STEP + u] - top)
                total = total + weight
                weights.append(weight.astype(BF16))
                values.append(vs[code & (KB - 1)])
            su[h] = total
            acc[h] += jnp.dot(
                jnp.concatenate(weights, axis=1),
                jnp.concatenate(values, axis=0),
                preferred_element_type=F32,
            )

    lane = lax.broadcasted_iota(jnp.int32, (B, 128), 1)
    extra = jnp.zeros((B, 128), F32)
    for h in range(HEADS):
        extra = jnp.where(lane == h, mx[h], extra)
        total = jnp.sum(su[h], axis=1, keepdims=True)
        extra = jnp.where(lane == SUM_LANE + h, jnp.broadcast_to(total, (B, 128)), extra)
        part = acc[h].astype(BF16)
        for d in range(NY):
            out_ref[d, 0, :, h * D : (h + 1) * D] = part[d * 32 : (d + 1) * 32]
    extra = extra.astype(BF16)
    for d in range(NY):
        out_ref[d, 0, :, SLICE:WIDE] = extra[d * 32 : (d + 1) * 32]


def attend(ints, steps, where_x, q_all, k_all, v_all, s_all):
    whole = lambda qb, *_: (0, 0, 0)
    once = pl.Buffered(1)
    return pl.pallas_call(
        attend_kernel,
        out_shape=jax.ShapeDtypeStruct((NY, QB, 32, WIDE), BF16),
        grid_spec=pltpu.PrefetchScalarGridSpec(
            num_scalar_prefetch=3,
            grid=(QB,),
            in_specs=[
                pl.BlockSpec((NY, NX, 1, ROWS, SLICE), lambda qb, *_: (0, 0, qb, 0, 0)),
                pl.BlockSpec((KB, B, D), whole, pipeline_mode=once),
                pl.BlockSpec((KB, B, D), whole, pipeline_mode=once),
                pl.BlockSpec(memory_space=pltpu.SMEM),
            ],
            out_specs=pl.BlockSpec((NY, 1, 32, WIDE), lambda qb, *_: (0, qb, 0, 0)),
            scratch_shapes=[
                pltpu.VMEM((KB, B, D), BF16),
                pltpu.VMEM((B, SLICE), BF16),
                pltpu.VMEM((HEADS, KB, B, B), F32),
                pltpu.VMEM((HEADS, B, B), F32),
                pltpu.VMEM((HEADS, B, D), F32),
                pltpu.VMEM((HEADS, B, B), F32),
            ],
        ),
        compiler_params=pltpu.CompilerParams(vmem_limit_bytes=40 << 20),
        name="attend",
    )(ints, steps, where_x, q_all, k_all.reshape(KB, B, D), v_all.reshape(KB, B, D), s_all)


def gather_kernel(
    p, got, parts, att,
    up_send, up_recv, dn_send, dn_recv, far_send, far_recv,
    x_send, x_recv, zu_send, zu_recv, zd_send, zd_recv, c_send, c_recv, own, own_x,
):
    rep, z, c, x, y = place()
    group = rep
    other = rep + 1 - 2 * c
    here = x * NY + y
    sib = (other, here)
    xs = [(x + d) % NX for d in range(NX)]
    at_x = [(rep, xs[d] * NY + y) for d in range(NX)]
    ys = [(y + d) % NY for d in range(NY)]
    at_y = [(rep, x * NY + ys[d]) for d in range(NY)]
    zup = (((z + 1) % NZ) * 2 + c, here)
    zdn = (((z + NZ - 1) % NZ) * 2 + c, here)
    greet([at_x[1], at_x[2], at_x[3], at_y[1], at_y[2], at_y[3], zup, zdn, sib])

    py = [[None] * NY for _ in range(QB)]
    sems = {1: (up_send, up_recv), 3: (dn_send, dn_recv), 2: (far_send, far_recv)}
    for b in range(QB):
        for d in (1, 3, 2):
            s, r = sems[d]
            py[b][d] = remote(p.at[ys[d], b], parts.at[y, b], s.at[b], r.at[b], at_y[d])
            py[b][d].start()
        py[b][0] = pltpu.make_async_copy(p.at[y, b], parts.at[y, b], own.at[b])
        py[b][0].start()

    px = [[None] * NX for _ in range(QB)]
    lane = lax.broadcasted_iota(jnp.int32, (32, 128), 1)

    def combine(b):
        for d in (1, 3, 2):
            py[b][d].wait_recv()
        py[b][0].wait()
        extra = [parts[s, b, :, SLICE:WIDE].astype(F32) for s in range(NY)]
        top = functools.reduce(jnp.maximum, extra)
        shift = [jnp.exp2(e - top) for e in extra]
        total = sum(w * pltpu.roll(e, SUM_LANE, 1) for w, e in zip(shift, extra))
        total = jnp.where(lane < HEADS, total, 1.0)
        ratio = [w / total for w in shift]
        for h in range(HEADS):
            cols = slice(h * D, (h + 1) * D)
            value = sum(
                jnp.broadcast_to(ratio[s][:, h : h + 1], (32, D)) * parts[s, b, :, cols].astype(F32)
                for s in range(NY)
            )
            value = value.reshape(NX, ROWS, D).astype(BF16)
            for d in range(NX):
                att[b, d, :, cols] = value[d]
        mine = pl.ds(pl.multiple_of(x * SLICE, SLICE), SLICE)
        for d in (1, 3, 2):
            px[b][d] = remote(
                att.at[b, xs[d]], got.at[group, b, :, mine], x_send.at[b, d], x_recv.at[b, d], at_x[d]
            )
            px[b][d].start()
        px[b][0] = pltpu.make_async_copy(att.at[b, x], got.at[group, b, :, mine], own_x.at[b])
        px[b][0].start()

    def across(src, b, k):
        piece = got.at[src, b]
        copy = remote(piece, piece, c_send.at[b, k], c_recv.at[b, k], sib)
        copy.start()
        return copy

    zu = [[None] * 5 for _ in range(QB)]
    zd = [[None] * 5 for _ in range(QB)]
    cs = [[None] * NZ for _ in range(QB)]

    def upward(src, b, k):
        piece = got.at[src, b]
        zu[b][k] = remote(piece, piece, zu_send.at[b, k], zu_recv.at[b, k], zup)
        zu[b][k].start()

    def downward(src, b, k):
        piece = got.at[src, b]
        zd[b][k] = remote(piece, piece, zd_send.at[b, k], zd_recv.at[b, k], zdn)
        zd[b][k].start()

    def land(b):
        for d in (1, 3, 2):
            px[b][d].wait_recv()
        px[b][0].wait()
        upward(group, b, 1)
        downward(group, b, 1)
        cs[b][0] = across(group, b, 0)

    def hop(b, k):
        if zu[b][k] is not None:
            src = ((z + NZ - k) % NZ) * 2 + c
            zu[b][k].wait_recv()
            if k < 3 or (k == 3 and b % 2 == 0):
                upward(src, b, k + 1)
            cs[b][k] = across(src, b, k)
        if zd[b][k] is not None:
            src = ((z + k) % NZ) * 2 + c
            zd[b][k].wait_recv()
            if k < 3 or (k == 3 and b % 2 == 1):
                downward(src, b, k + 1)
            cs[b][NZ - k] = across(src, b, NZ - k)

    for wave in range(QB + 5):
        for b in range(QB):
            stage = wave - b
            if stage == 0:
                combine(b)
            elif stage == 1:
                land(b)
            elif 2 <= stage <= 5:
                hop(b, stage - 1)

    for b in range(QB):
        for d in (1, 2, 3):
            py[b][d].wait_send()
            px[b][d].wait_send()
        for k in range(1, 5):
            for copy in (zu[b][k], zd[b][k]):
                if copy is not None:
                    copy.wait_send()
        for k in range(NZ):
            cs[b][k].wait_send()
            cs[b][k].wait_recv()


def gather(p):
    dma = pltpu.SemaphoreType.DMA
    return pl.pallas_call(
        gather_kernel,
        out_shape=jax.ShapeDtypeStruct((2 * NZ, QB, ROWS, NX * SLICE), BF16),
        in_specs=[pl.BlockSpec(memory_space=pl.ANY)],
        out_specs=pl.BlockSpec(memory_space=pl.ANY),
        scratch_shapes=[
            pltpu.VMEM((NY, QB, 32, WIDE), BF16),
            pltpu.VMEM((QB, NX, ROWS, SLICE), BF16),
        ]
        + [dma((QB,))] * 6
        + [dma((QB, NX))] * 2
        + [dma((QB, 5))] * 4
        + [dma((QB, NZ))] * 2
        + [dma((QB,))] * 2,
        compiler_params=pltpu.CompilerParams(
            collective_id=1, has_side_effects=True, vmem_limit_bytes=16 << 20
        ),
        name="gather",
    )(p)


def pick_kernel(target, me, got, out, sem):
    def look(j, found):
        hit = target[j] == me[0]

        @pl.when(hit)
        def _():
            pltpu.make_async_copy(got.at[j], out.at[found], sem.at[found]).start()

        return found + hit.astype(jnp.int32)

    lax.fori_loop(0, 2 * NZ * QB, look, jnp.int32(0))
    for s in range(QB):
        pltpu.make_async_copy(got.at[s], out.at[s], sem.at[s]).wait()


def pick(target, me, got):
    smem = pl.BlockSpec(memory_space=pltpu.SMEM)
    return pl.pallas_call(
        pick_kernel,
        out_shape=jax.ShapeDtypeStruct((QB, ROWS, NX * SLICE), BF16),
        in_specs=[smem, smem, pl.BlockSpec(memory_space=pl.ANY)],
        out_specs=pl.BlockSpec(memory_space=pl.ANY),
        scratch_shapes=[pltpu.SemaphoreType.DMA((QB,))],
        name="pick",
    )(target, me, got.reshape(2 * NZ * QB, ROWS, NX * SLICE))


def block_lists(pattern, group, x, y):
    mine = lax.dynamic_slice(pattern, (x * HEADS, group * QB, 0), (HEADS, QB, pattern.shape[2]))
    mine = jnp.transpose(mine, (1, 0, 2))
    kb = jnp.arange(KB, dtype=jnp.int32)
    block = ((kb // 8) * NY + y) * 8 + kb % 8
    diagonal = (FIRST + group * QB + jnp.arange(QB, dtype=jnp.int32))[:, None, None]
    chosen = jnp.any(mine[:, :, None, :] == block[None, None, :, None], axis=3)
    chosen = (chosen | (block == diagonal)) & (block <= diagonal)
    ones = chosen.astype(jnp.int32)
    rank = jnp.sum(jnp.where(kb[None, :] < kb[:, None], ones[:, :, None, :], 0), axis=3)
    code = kb + KB * (diagonal - block)
    empty = -KB * 1024
    hit = chosen[:, :, None, :] & (rank[:, :, None, :] == kb[:, None])
    ints = jnp.sum(jnp.where(hit, code[:, :, None, :] - empty, 0), axis=3) + empty
    most = jnp.max(jnp.sum(ones, axis=2), axis=1)
    return ints.reshape(-1), (most + STEP - 1) // STEP


def per_device(queries, key_cache, value_cache, key_scale, value_scale, pattern, target):
    rep, z, c, x, y = place()
    scales = jnp.pad(jnp.concatenate([key_scale, value_scale], axis=1), ((0, 0), (0, 120)))
    ints, steps = block_lists(pattern, rep, x, y)
    q_all, k_all, v_all, s_all = spread(queries, key_cache, value_cache, scales)
    partial = attend(ints, steps, x.reshape(1), q_all, k_all, v_all, s_all)
    got = gather(partial)
    return pick(target, rep.reshape(1), got)


def solution(mesh):
    return jax.shard_map(
        per_device,
        mesh=mesh,
        in_specs=(
            P("replica", "ctx", None),
            P("ctx", None),
            P("ctx", None),
            P("ctx", None),
            P("ctx", None),
            P(),
            P(),
        ),
        out_specs=P("replica", "ctx", None),
        check_vma=False,
    )
```

```python
import functools
import math

import jax
import jax.numpy as jnp
from jax import lax
from jax.experimental import pallas as pl
from jax.experimental.pallas import tpu as pltpu
from jax.sharding import PartitionSpec as P

MESH = pl.DeviceIdType.MESH
BF16 = jnp.bfloat16
F32 = jnp.float32
I32 = jnp.int32

NX = 4
NY = 4
NZ = 8
HEADS = 7
D = 128
B = 128
QB = 4
KB = 32
SHARD = 8
SLICE = HEADS * D
ROWS = B // (NX * NY)
PART = NX * ROWS
KEYS = SHARD * B
PAIRS = 32
SUM_LANE = 64
NEG = -(2.0**100)
STEP = 4
FIRST = 64
FAR = (1, 3, 2)
TO_LOG2 = math.log2(math.e) / math.sqrt(D)

DMA = pltpu.SemaphoreType.DMA
ANY = pl.BlockSpec(memory_space=pl.ANY)
VMEM = pl.BlockSpec(memory_space=pltpu.VMEM)
SMEM = pl.BlockSpec(memory_space=pltpu.SMEM)


def place():
    rep = lax.axis_index("replica")
    ctx = lax.axis_index("ctx")
    return rep, rep // 2, rep % 2, ctx // NY, ctx % NY


def greet(partners):
    barrier = pltpu.get_barrier_semaphore()
    for who in partners:
        pl.semaphore_signal(barrier, inc=1, device_id=who, device_id_type=MESH)
    pl.semaphore_wait(barrier, len(partners))


def remote(src, dst, send, recv, who):
    return pltpu.make_async_remote_copy(
        src_ref=src, dst_ref=dst, send_sem=send, recv_sem=recv, device_id=who, device_id_type=MESH
    )


def iota(shape, dim):
    return lax.broadcasted_iota(I32, shape, dim)


def block_lists(mine, rep, y):
    shape = (PAIRS, 128)
    lane, row = iota(shape, 1), iota(shape, 0)
    of_pair = sum((row >= n * HEADS).astype(I32) for n in range(1, QB))
    below = FIRST + rep * QB + of_pair - ((lane >> 3) * (SHARD * NY) + y * SHARD + (lane & 7))
    block = (lane >> 3) * (SHARD * NY) + y * SHARD + (lane & 7)
    hits = (below == 0).astype(I32)
    for e in range(mine.shape[1]):
        hits = hits | (jnp.broadcast_to(mine[:, e : e + 1], shape) == block).astype(I32)
    hits = jnp.where((below >= 0) & (lane < KB), hits, 0)
    upto = hits
    for s in (1, 2, 4, 8, 16):
        upto = upto + jnp.where(lane >= s, pltpu.roll(upto, s, 1), 0)
    slot = jnp.where(hits > 0, upto - 1, -1)
    code = lane + KB * below
    packed = jnp.full(shape, -KB * 1024, I32)
    for b in range(KB):
        at = jnp.broadcast_to(slot[:, b : b + 1], shape) == lane
        packed = jnp.where(at, jnp.broadcast_to(code[:, b : b + 1], shape), packed)
    number = jnp.broadcast_to(upto[:, KB - 1 : KB], shape)
    return jnp.where(lane == KB, number, packed)


def spread_kernel(
    q, k, v, ks, vs, mine,
    q_all, keys, values, factors, lists,
    k_land, v_land, scales, k_loc, v_loc,
    q_send, q_recv, y_send, y_recv, k_send, k_recv, v_send, v_recv, s_send, s_recv,
    kc_send, kc_recv, vc_send, vc_recv, own,
):
    rep, z, c, x, y = place()
    sib = (rep + 1 - 2 * c, x * NY + y)
    xs = [(x + d) % NX for d in range(NX)]
    back = [(x + NX - d) % NX for d in range(NX)]
    at_x = [(rep, xs[d] * NY + y) for d in range(NX)]
    at_y = [(rep, x * NY + (y + d) % NY) for d in range(NY)]
    half = pl.ds(pl.multiple_of(c * (KEYS // 2), KEYS // 2), KEYS // 2)

    def cols(d, n):
        return pl.ds(pl.multiple_of(xs[d] * n, n), n)

    own_q = q.at[:, :, cols(0, SLICE)]
    stay = [
        pltpu.make_async_copy(ks, k_loc, own.at[0]),
        pltpu.make_async_copy(vs, v_loc, own.at[1]),
        pltpu.make_async_copy(own_q, q_all.at[y, x], own.at[2]),
        pltpu.make_async_copy(k.at[:, cols(0, D)], k_land.at[0], own.at[3]),
        pltpu.make_async_copy(v.at[:, cols(0, D)], v_land.at[0], own.at[4]),
    ]
    for copy in stay:
        copy.start()
    greet([at_x[1], at_x[2], at_x[3], at_y[1], at_y[2], at_y[3], sib])

    qx, kx, vx, sx, kc, vc = ([None] * NX for _ in range(6))
    qy = [[None] * NY for _ in range(NX)]

    def over_y(d, src):
        for e in FAR:
            qy[d][e] = remote(src, q_all.at[y, back[d]], y_send.at[d, e], y_recv.at[d, e], at_y[e])
            qy[d][e].start()

    for d in FAR:
        qx[d] = remote(q.at[:, :, cols(d, SLICE)], q_all.at[y, x], q_send.at[d], q_recv.at[d], at_x[d])
        qx[d].start()
    over_y(0, own_q)
    for d in FAR:
        kx[d] = remote(k.at[half, cols(d, D)], k_land.at[d, half], k_send.at[d], k_recv.at[d], at_x[d])
        vx[d] = remote(v.at[half, cols(d, D)], v_land.at[d, half], v_send.at[d], v_recv.at[d], at_x[d])
        kx[d].start()
        vx[d].start()
    stay[0].wait()
    stay[1].wait()
    scales[0] = jnp.zeros((SHARD, 128), F32)
    scales[0, :, 0:NX] = k_loc[...]
    scales[0, :, NX : 2 * NX] = v_loc[...]
    for d in FAR:
        sx[d] = remote(scales.at[0], scales.at[d], s_send.at[d], s_recv.at[d], at_x[d])
        sx[d].start()
    for d in FAR:
        qx[d].wait_recv()
        over_y(d, q_all.at[y, back[d]])

    lists[...] = block_lists(mine[...], rep, y)

    lane = iota((SHARD, 128), 1)

    def column(tile, n):
        return jnp.sum(jnp.where(lane == n, tile, 0.0), axis=1, keepdims=True)

    def finish(d):
        tile = scales[d]
        for_keys = jnp.broadcast_to(column(tile, x) * TO_LOG2, (SHARD, 128))
        for_values = jnp.broadcast_to(column(tile, NX + x), (SHARD, 128))
        for b in range(SHARD):
            at = back[d] * SHARD + b
            factors[at] = jnp.broadcast_to(for_keys[b : b + 1], (8, 128))
            rows = slice(b * B, (b + 1) * B)
            keys[at] = k_land[d, rows].T
            values[at] = (v_land[d, rows].astype(F32) * for_values[b : b + 1]).astype(BF16)

    def hand_over(d):
        kx[d].wait_recv()
        kc[d] = remote(k_land.at[d, half], k_land.at[d, half], kc_send.at[d], kc_recv.at[d], sib)
        kc[d].start()
        vx[d].wait_recv()
        vc[d] = remote(v_land.at[d, half], v_land.at[d, half], vc_send.at[d], vc_recv.at[d], sib)
        vc[d].start()
        sx[d].wait_recv()

    def whole(d):
        kc[d].wait_recv()
        vc[d].wait_recv()

    for copy in stay[2:]:
        copy.wait()
    finish(0)
    hand_over(1)
    hand_over(3)
    whole(1)
    finish(1)
    hand_over(2)
    whole(3)
    finish(3)
    whole(2)
    finish(2)
    for d in range(NX):
        for e in FAR:
            qy[d][e].wait_recv()
            qy[d][e].wait_send()
    for d in FAR:
        for copy in (qx[d], kx[d], vx[d], sx[d], kc[d], vc[d]):
            copy.wait_send()


def spread(q, k, v, ks, vs, mine):
    return pl.pallas_call(
        spread_kernel,
        out_shape=[
            jax.ShapeDtypeStruct((NY, NX, QB, ROWS, SLICE), BF16),
            jax.ShapeDtypeStruct((KB, D, B), BF16),
            jax.ShapeDtypeStruct((KB, B, D), BF16),
            jax.ShapeDtypeStruct((KB, 8, 128), F32),
            jax.ShapeDtypeStruct((PAIRS, 128), I32),
        ],
        in_specs=[ANY] * 5 + [VMEM],
        out_specs=[VMEM] * 5,
        scratch_shapes=[
            pltpu.VMEM((NX, KEYS, D), BF16),
            pltpu.VMEM((NX, KEYS, D), BF16),
            pltpu.VMEM((NX, SHARD, 128), F32),
            pltpu.VMEM((SHARD, NX), F32),
            pltpu.VMEM((SHARD, NX), F32),
        ]
        + [DMA((NX,))] * 2
        + [DMA((NX, NY))] * 2
        + [DMA((NX,))] * 10
        + [DMA((5,))],
        compiler_params=pltpu.CompilerParams(
            collective_id=0, has_side_effects=True, vmem_limit_bytes=24 << 20
        ),
        name="spread",
    )(q, k, v, ks, vs, mine)


def attend_kernel(ints, q_ref, keys, values, factors, out, extra_out, qs, sc, mx, acc, su, extra):
    row = iota((B, B), 0)
    row = ((row >> 3) & 3) * PART + (row >> 5) * ROWS + (row & 7)
    lane = iota((B, B), 1)
    ahead = lane - row
    extra[...] = jnp.zeros((B, B), F32)

    @pl.loop(0, QB)
    def _(qb):
        qs[...] = q_ref[:, :, qb].astype(F32).reshape(B, SLICE).astype(BF16)
        mx[...] = jnp.full(mx.shape, NEG, F32)
        acc[...] = jnp.zeros(acc.shape, F32)
        su[...] = jnp.zeros(su.shape, F32)
        most = ints[qb * HEADS, KB]
        for h in range(1, HEADS):
            most = jnp.maximum(most, ints[qb * HEADS + h, KB])
        count = (most + STEP - 1) // STEP

        @pl.loop(0, count)
        def _(t):
            for h in range(HEADS):
                head = qs[:, h * D : (h + 1) * D]
                top = mx[h]
                for u in range(STEP):
                    code = ints[qb * HEADS + h, t * STEP + u]
                    kb = code & (KB - 1)
                    score = jnp.dot(head, keys[kb], preferred_element_type=F32)
                    factor = jnp.broadcast_to(factors[kb][None], (B // 8, 8, B)).reshape(B, B)
                    score = jnp.where(ahead <= (code >> 5) * B, score * factor, NEG)
                    sc[h, t * STEP + u] = score
                    top = jnp.maximum(top, score)
                mx[h] = top

        for h in range(HEADS):
            top = jnp.max(mx[h], axis=1, keepdims=True)
            mx[h] = jnp.broadcast_to(top, (B, B)).astype(BF16).astype(F32)

        @pl.loop(0, count)
        def _(t):
            for h in range(HEADS):
                top = mx[h]
                total = su[h]
                weights, columns = [], []
                for u in range(STEP):
                    code = ints[qb * HEADS + h, t * STEP + u]
                    weight = jnp.exp2(sc[h, t * STEP + u] - top)
                    total = total + weight
                    weights.append(weight.astype(BF16))
                    columns.append(values[code & (KB - 1)])
                su[h] = total
                for u in range(0, STEP, 2):
                    acc[h] += jnp.dot(
                        jnp.concatenate(weights[u : u + 2], axis=1),
                        jnp.concatenate(columns[u : u + 2], axis=0),
                        preferred_element_type=F32,
                    )

        tile = extra[...]
        for h in range(HEADS):
            tile = jnp.where(lane == qb * 8 + h, mx[h], tile)
            total = jnp.broadcast_to(jnp.sum(su[h], axis=1, keepdims=True), (B, B))
            tile = jnp.where(lane == SUM_LANE + qb * 8 + h, total, tile)
            part = acc[h].astype(BF16)
            for d in range(NY):
                out[d, qb, :, h * D : (h + 1) * D] = part[d * PART : (d + 1) * PART]
        extra[...] = tile

    for d in range(NY):
        extra_out[d] = extra[d * PART : (d + 1) * PART].astype(BF16)


def attend(lists, q_all, keys, values, factors):
    return pl.pallas_call(
        attend_kernel,
        out_shape=[
            jax.ShapeDtypeStruct((NY, QB, PART, SLICE), BF16),
            jax.ShapeDtypeStruct((NY, PART, 128), BF16),
        ],
        in_specs=[SMEM] + [VMEM] * 4,
        out_specs=[VMEM] * 2,
        scratch_shapes=[
            pltpu.VMEM((B, SLICE), BF16),
            pltpu.VMEM((HEADS, KB, B, B), F32),
            pltpu.VMEM((HEADS, B, B), F32),
            pltpu.VMEM((HEADS, B, D), F32),
            pltpu.VMEM((HEADS, B, B), F32),
            pltpu.VMEM((B, B), F32),
        ],
        compiler_params=pltpu.CompilerParams(vmem_limit_bytes=36 << 20),
        name="attend",
    )(lists, q_all, keys, values, factors)


def gather_kernel(
    target, p, extra_in, out, parts, extra, att, got, swap_out, swap_in,
    e_send, e_recv, y_send, y_recv, x_send, x_recv, z_send, z_recv, c_send, c_recv, own,
):
    rep, z, c, x, y = place()
    other = rep + 1 - 2 * c
    here = x * NY + y
    sib = (other, here)
    xs = [(x + d) % NX for d in range(NX)]
    ys = [(y + d) % NY for d in range(NY)]
    at_x = [(rep, xs[d] * NY + y) for d in range(NX)]
    at_y = [(rep, x * NY + ys[d]) for d in range(NY)]
    at_z = [(((z + d) % NZ) * 2 + c, here) for d in range(NZ)]
    greet(at_x[1:] + at_y[1:] + at_z[1:] + [sib])

    ex = [None] * NY
    py = [[None] * NY for _ in range(QB)]
    px = [[None] * NX for _ in range(QB)]
    pz = [[None] * NZ for _ in range(QB)]
    for d in FAR:
        ex[d] = remote(extra_in.at[ys[d]], extra.at[d], e_send.at[d], e_recv.at[d], at_y[d])
        ex[d].start()
    for b in range(QB):
        for d in FAR:
            py[b][d] = remote(p.at[ys[d], b], parts.at[d, b], y_send.at[b, d], y_recv.at[b, d], at_y[d])
            py[b][d].start()

    def look(j, state):
        code = target[j]
        mine = code == rep
        theirs = code == other
        found, passed, *at = state
        at = [
            jnp.where(hit & (n == s), j, a)
            for a, (hit, n, s) in zip(
                at,
                [(mine, found, s) for s in range(QB)] + [(theirs, passed, s) for s in range(QB)],
            )
        ]
        return (found + mine.astype(I32), passed + theirs.astype(I32), *at)

    _, _, *at = lax.fori_loop(0, 2 * NZ * QB, look, (jnp.int32(0),) * (2 + 2 * QB))
    to_keep, to_pass = at[:QB], at[QB:]

    for d in FAR:
        ex[d].wait_recv()
    marks = [extra_in[y].astype(F32)] + [extra[d].astype(F32) for d in range(1, NY)]
    top = functools.reduce(jnp.maximum, marks)
    shift = [jnp.exp2(e - top) for e in marks]
    total = sum(w * pltpu.roll(e, SUM_LANE, 1) for w, e in zip(shift, marks))
    lane = iota((PART, 128), 1)
    total = jnp.where((lane < QB * 8) & ((lane & 7) < HEADS), total, 1.0)
    ratio = [w / total for w in shift]
    mine = pl.ds(pl.multiple_of(x * SLICE, SLICE), SLICE)

    def combine(b):
        for d in FAR:
            py[b][d].wait_recv()
        for h in range(HEADS):
            cols = slice(h * D, (h + 1) * D)
            at = b * 8 + h
            value = sum(
                jnp.broadcast_to(ratio[d][:, at : at + 1], (PART, D))
                * (parts[d, b, :, cols] if d else p[y, b, :, cols]).astype(F32)
                for d in range(NY)
            )
            value = value.reshape(NX, ROWS, D).astype(BF16)
            for d in range(NX):
                att[b, d, :, cols] = value[d]
        for d in FAR:
            px[b][d] = remote(
                att.at[b, xs[d]], got.at[z, b, :, mine], x_send.at[b, d], x_recv.at[b, d], at_x[d]
            )
            px[b][d].start()
        px[b][0] = pltpu.make_async_copy(att.at[b, x], got.at[z, b, :, mine], own.at[b])
        px[b][0].start()

    def land(b):
        for d in FAR:
            px[b][d].wait_recv()
        px[b][0].wait()
        for d in (4, 3, 5, 2, 6, 1, 7):
            pz[b][d] = remote(got.at[z, b], got.at[z, b], z_send.at[b, d], z_recv.at[b, d], at_z[d])
            pz[b][d].start()

    for b in range(QB):
        combine(b)
        if b:
            land(b - 1)
    land(QB - 1)
    for b in range(QB):
        for d in range(1, NZ):
            pz[b][d].wait_recv()

    def where(j):
        return j >> 3, j & 3

    for s in range(QB):
        from_z, b = where(to_pass[s])
        swap_out[s] = got[from_z, b]
    cross = remote(swap_out, swap_in, c_send, c_recv, sib)
    cross.start()
    for s in range(QB):
        from_z, b = where(to_keep[s])
        out[s] = got[from_z, b]
    cross.wait_recv()
    for s in range(QB):
        here_too = ((to_keep[s] >> 2) & 1) == c
        out[s] = jnp.where(here_too, out[s], swap_in[s])

    cross.wait_send()
    for d in FAR:
        ex[d].wait_send()
    for b in range(QB):
        for d in FAR:
            py[b][d].wait_send()
            px[b][d].wait_send()
        for d in range(1, NZ):
            pz[b][d].wait_send()


def gather(target, p, extra):
    return pl.pallas_call(
        gather_kernel,
        out_shape=jax.ShapeDtypeStruct((QB, ROWS, NX * SLICE), BF16),
        in_specs=[SMEM, VMEM, VMEM],
        out_specs=VMEM,
        scratch_shapes=[
            pltpu.VMEM((NY, QB, PART, SLICE), BF16),
            pltpu.VMEM((NY, PART, 128), BF16),
            pltpu.VMEM((QB, NX, ROWS, SLICE), BF16),
            pltpu.VMEM((NZ, QB, ROWS, NX * SLICE), BF16),
            pltpu.VMEM((QB, ROWS, NX * SLICE), BF16),
            pltpu.VMEM((QB, ROWS, NX * SLICE), BF16),
        ]
        + [DMA((NY,))] * 2
        + [DMA((QB, NY))] * 2
        + [DMA((QB, NX))] * 2
        + [DMA((QB, NZ))] * 2
        + [DMA] * 2
        + [DMA((QB,))],
        compiler_params=pltpu.CompilerParams(
            collective_id=1, has_side_effects=True, vmem_limit_bytes=24 << 20
        ),
        name="gather",
    )(target, p, extra)


def per_device(queries, key_cache, value_cache, key_scale, value_scale, pattern, target):
    rep, z, c, x, y = place()
    listed = pattern.shape[2]
    mine = lax.dynamic_slice(pattern, (x * HEADS, rep * QB, 0), (HEADS, QB, listed))
    mine = jnp.transpose(mine, (1, 0, 2)).reshape(HEADS * QB, listed)
    mine = jnp.pad(mine, ((0, PAIRS - HEADS * QB), (0, 0)))
    q_all, keys, values, factors, lists = spread(
        queries, key_cache, value_cache, key_scale, value_scale, mine
    )
    part, extra = attend(lists, q_all, keys, values, factors)
    return gather(target, part, extra)


def solution(mesh):
    return jax.shard_map(
        per_device,
        mesh=mesh,
        in_specs=(
            P("replica", "ctx", None),
            P("ctx", None),
            P("ctx", None),
            P("ctx", None),
            P("ctx", None),
            P(),
            P(),
        ),
        out_specs=P("replica", "ctx", None),
        check_vma=False,
    )
```

```python
import functools
import math

import jax
import jax.numpy as jnp
from jax import lax
from jax.experimental import pallas as pl
from jax.experimental.pallas import tpu as pltpu
from jax.sharding import PartitionSpec as P

MESH = pl.DeviceIdType.MESH
BF16 = jnp.bfloat16
F32 = jnp.float32
I32 = jnp.int32

NX = 4
NY = 4
NZ = 8
HEADS = 7
D = 128
B = 128
QB = 4
KB = 32
SHARD = 8
SLICE = HEADS * D
ROWS = B // (NX * NY)
PART = NX * ROWS
KEYS = SHARD * B
PAIRS = 32
SUM_LANE = 64
NEG = -(2.0**100)
STEP = 4
FIRST = 64
FAR = (1, 3, 2)
CHUNKS = ((2, 1), (3, 0))
ORDER = (8, 9, 6, 7, 10, 11, 4, 5, 12, 13, 2, 3, 14, 15, 1, 0)
TO_LOG2 = math.log2(math.e) / math.sqrt(D)

DMA = pltpu.SemaphoreType.DMA
HBM = pl.BlockSpec(memory_space=pltpu.HBM)
VMEM = pl.BlockSpec(memory_space=pltpu.VMEM)
SMEM = pl.BlockSpec(memory_space=pltpu.SMEM)


def place():
    rep = lax.axis_index("replica")
    ctx = lax.axis_index("ctx")
    return rep, rep // 2, rep % 2, ctx // NY, ctx % NY


def greet(partners):
    barrier = pltpu.get_barrier_semaphore()
    for who in partners:
        pl.semaphore_signal(barrier, inc=1, device_id=who, device_id_type=MESH)
    pl.semaphore_wait(barrier, len(partners))


def remote(src, dst, send, recv, who):
    return pltpu.make_async_remote_copy(
        src_ref=src, dst_ref=dst, send_sem=send, recv_sem=recv, device_id=who, device_id_type=MESH
    )


def iota(shape, dim):
    return lax.broadcasted_iota(I32, shape, dim)


def block_lists(listed, blocks, y):
    shape = (PAIRS, 128)
    lane, row = iota(shape, 1), iota(shape, 0)
    block = (lane >> 3) * (SHARD * NY) + y * SHARD + (lane & 7)
    hits = jnp.zeros(shape, I32)
    own = jnp.zeros(shape, I32)
    column = iota(listed.shape[1:], 1)
    for s in range(QB):
        own = jnp.where(row >> 3 == s, blocks[s], own)
        for h in range(HEADS):
            entry = jnp.max(jnp.where(column == blocks[s], listed[h], -1), axis=1, keepdims=True)
            found = (jnp.broadcast_to(entry, shape) == block).astype(I32)
            found = jnp.max(found, axis=0, keepdims=True)
            hits = jnp.where(row == s * 8 + h, found, hits)
    below = FIRST + own - block
    hits = jnp.where(below == 0, 1, hits)
    hits = jnp.where((below >= 0) & (lane < KB) & ((row & 7) < HEADS), hits, 0)
    upto = hits
    for s in (1, 2, 4, 8, 16):
        upto = upto + jnp.where(lane >= s, pltpu.roll(upto, s, 1), 0)
    slot = jnp.where(hits > 0, upto - 1, -1)
    code = lane + KB * below
    packed = jnp.full(shape, -KB * 1024, I32)
    for b in range(KB):
        at = jnp.broadcast_to(slot[:, b : b + 1], shape) == lane
        packed = jnp.where(at, jnp.broadcast_to(code[:, b : b + 1], shape), packed)
    number = jnp.broadcast_to(upto[:, KB - 1 : KB], shape)
    return jnp.where(lane == KB, number, packed)


def spread_kernel(
    target, q, k, v, ks, vs, pattern,
    q_all, keys, values, factors, lists,
    q_loc, packed, first, second, chosen, k_land, v_land, scales, k_loc, v_loc, listed,
    z_send, z_recv, q_send, q_recv, y_send, y_recv, k_send, k_recv, v_send, v_recv, s_send, s_recv,
    kc_send, kc_recv, vc_send, vc_recv, own,
):
    rep, z, c, x, y = place()
    sib = (rep + 1 - 2 * c, x * NY + y)
    xs = [(x + d) % NX for d in range(NX)]
    back = [(x + NX - d) % NX for d in range(NX)]
    at_x = [(rep, xs[d] * NY + y) for d in range(NX)]
    at_y = [(rep, x * NY + (y + d) % NY) for d in range(NY)]
    half = pl.ds(pl.multiple_of(c * (KEYS // 2), KEYS // 2), KEYS // 2)
    groups = [((z + d) % NZ) * 2 + (c + e) % 2 for d in range(NZ) for e in range(2)]
    at_group = [(g, x * NY + y) for g in groups]

    arrived = (first, second)

    def cols(d, n):
        return pl.ds(pl.multiple_of(xs[d] * n, n), n)

    stay = [
        pltpu.make_async_copy(q, q_loc, own.at[0]),
        pltpu.make_async_copy(ks, k_loc, own.at[1]),
        pltpu.make_async_copy(vs, v_loc, own.at[2]),
        pltpu.make_async_copy(pattern.at[pl.ds(x * HEADS, HEADS)], listed, own.at[3]),
        pltpu.make_async_copy(k.at[:, cols(0, D)], k_land.at[0], own.at[4]),
        pltpu.make_async_copy(v.at[:, cols(0, D)], v_land.at[0], own.at[5]),
    ]
    for copy in stay:
        copy.start()
    greet(at_group[1:] + at_x[1:] + at_y[1:])

    qx, kx, vx, sx, kc, vc = ([None] * NX for _ in range(6))
    qy = [[None] * NY for _ in range(NX)]
    qz = [[None] * len(groups) for _ in CHUNKS]

    for d in FAR:
        kx[d] = remote(k.at[half, cols(d, D)], k_land.at[d, half], k_send.at[d], k_recv.at[d], at_x[d])
        vx[d] = remote(v.at[half, cols(d, D)], v_land.at[d, half], v_send.at[d], v_recv.at[d], at_x[d])
        kx[d].start()
        vx[d].start()

    goes_to = [target[rep * QB + b] for b in range(QB)]
    stay[0].wait()
    for i, chunk in enumerate(CHUNKS):
        for n in ORDER:
            b = jnp.int32(0)
            for other in range(1, QB):
                b = jnp.where(goes_to[other] == groups[n], other, b)
            for j, d in enumerate(chunk):
                block = q_loc[b, :, cols(d, SLICE)]
                if n == 0:
                    arrived[i][n, j] = block
                else:
                    packed[i, n, j] = block
            if n > 0:
                qz[i][n] = remote(
                    packed.at[i, n], arrived[i].at[n], z_send.at[i, n], z_recv.at[i, n], at_group[n]
                )
                qz[i][n].start()

    stay[1].wait()
    stay[2].wait()
    scales[0] = jnp.zeros((2 * NX, 128), F32)
    scales[0, 0:NX, 0:SHARD] = k_loc[...]
    scales[0, NX : 2 * NX, 0:SHARD] = v_loc[...]
    for d in FAR:
        sx[d] = remote(scales.at[0], scales.at[d], s_send.at[d], s_recv.at[d], at_x[d])
        sx[d].start()

    def look(j, state):
        found, *at = state
        hit = target[j] == rep
        at = [jnp.where(hit & (found == s), j, a) for s, a in enumerate(at)]
        return (found + hit.astype(I32), *at)

    _, *blocks = lax.fori_loop(0, 2 * NZ * QB, look, (jnp.int32(0),) * (1 + QB))
    stay[3].wait()
    lists[...] = block_lists(listed, blocks, y)

    scale_row = iota((2 * NX, 128), 0)

    def pick_row(tile, n):
        return jnp.sum(jnp.where(scale_row == n, tile, 0.0), axis=0, keepdims=True)

    def finish(d):
        tile = scales[d]
        for_keys = pick_row(tile, x) * TO_LOG2
        for_values = pick_row(tile, NX + x)
        for b in range(SHARD):
            at = back[d] * SHARD + b
            factors[at] = jnp.broadcast_to(for_keys[:, b : b + 1], (8, 128))
            rows = slice(b * B, (b + 1) * B)
            keys[at] = k_land[d, rows].T
            scaled = v_land[d, rows].astype(F32) * jnp.broadcast_to(for_values[:, b : b + 1], (B, D))
            values[at] = scaled.astype(BF16)

    def hand_over(d):
        kx[d].wait_recv()
        kc[d] = remote(k_land.at[d, half], k_land.at[d, half], kc_send.at[d], kc_recv.at[d], sib)
        kc[d].start()
        vx[d].wait_recv()
        vc[d] = remote(v_land.at[d, half], v_land.at[d, half], vc_send.at[d], vc_recv.at[d], sib)
        vc[d].start()
        sx[d].wait_recv()

    def whole(d):
        kc[d].wait_recv()
        vc[d].wait_recv()

    def over_y(d):
        for e in FAR:
            piece = q_all.at[y, back[d]]
            qy[d][e] = remote(piece, piece, y_send.at[d, e], y_recv.at[d, e], at_y[e])
            qy[d][e].start()

    def over_x(i):
        for n in range(1, len(groups)):
            qz[i][n].wait_recv()
        for j, d in enumerate(CHUNKS[i]):
            for s in range(QB):
                source = blocks[s] >> 2
                n = (((z + NZ - (source >> 1)) & (NZ - 1)) << 1) + ((source & 1) ^ c)
                block = arrived[i][n, j]
                if d == 0:
                    q_all[y, x, s] = block
                else:
                    chosen[d, s] = block
            if d == 0:
                over_y(0)
            else:
                qx[d] = remote(chosen.at[d], q_all.at[y, x], q_send.at[d], q_recv.at[d], at_x[d])
                qx[d].start()

    def from_x(i):
        for d in CHUNKS[i]:
            if d:
                qx[d].wait_recv()
                over_y(d)

    for copy in stay[4:]:
        copy.wait()
    finish(0)
    hand_over(1)
    hand_over(3)
    whole(1)
    finish(1)
    over_x(0)
    hand_over(2)
    from_x(0)
    whole(3)
    finish(3)
    whole(2)
    finish(2)
    over_x(1)
    from_x(1)
    for d in range(NX):
        for e in FAR:
            qy[d][e].wait_recv()
            qy[d][e].wait_send()
    for d in FAR:
        for copy in (qx[d], kx[d], vx[d], sx[d], kc[d], vc[d]):
            copy.wait_send()
    for copies in qz:
        for copy in copies[1:]:
            copy.wait_send()


def spread(target, q, k, v, ks, vs, pattern):
    pieces = (len(CHUNKS), 2 * NZ, len(CHUNKS[0]), ROWS, SLICE)
    return pl.pallas_call(
        spread_kernel,
        out_shape=[
            jax.ShapeDtypeStruct((NY, NX, QB, ROWS, SLICE), BF16),
            jax.ShapeDtypeStruct((KB, D, B), BF16),
            jax.ShapeDtypeStruct((KB, B, D), BF16),
            jax.ShapeDtypeStruct((KB, 8, 128), F32),
            jax.ShapeDtypeStruct((PAIRS, 128), I32),
        ],
        in_specs=[SMEM] + [HBM] * 6,
        out_specs=[VMEM] * 5,
        scratch_shapes=[
            pltpu.VMEM((QB, ROWS, NX * SLICE), BF16),
            pltpu.VMEM(pieces, BF16),
            pltpu.VMEM(pieces[1:], BF16),
            pltpu.VMEM(pieces[1:], BF16),
            pltpu.VMEM((NX, QB, ROWS, SLICE), BF16),
            pltpu.VMEM((NX, KEYS, D), BF16),
            pltpu.VMEM((NX, KEYS, D), BF16),
            pltpu.VMEM((NX, 2 * NX, 128), F32),
            pltpu.VMEM((NX, SHARD), F32),
            pltpu.VMEM((NX, SHARD), F32),
            pltpu.VMEM((HEADS, *pattern.shape[1:]), I32),
        ]
        + [DMA((len(CHUNKS), 2 * NZ))] * 2
        + [DMA((NX,))] * 2
        + [DMA((NX, NY))] * 2
        + [DMA((NX,))] * 10
        + [DMA((6,))],
        compiler_params=pltpu.CompilerParams(
            collective_id=0, has_side_effects=True, vmem_limit_bytes=50 << 20
        ),
        name="spread",
    )(target, q, k, v, ks, vs, pattern)


def attend_kernel(ints, q_ref, keys, values, factors, out, extra_out, qs, sc, mx, acc, su, extra):
    row = iota((B, B), 0)
    row = ((row >> 3) & 3) * PART + (row >> 5) * ROWS + (row & 7)
    lane = iota((B, B), 1)
    ahead = lane - row
    extra[...] = jnp.zeros((B, B), F32)

    @pl.loop(0, QB)
    def _(qb):
        qs[...] = q_ref[:, :, qb].astype(F32).reshape(B, SLICE).astype(BF16)
        mx[...] = jnp.full(mx.shape, NEG, F32)
        acc[...] = jnp.zeros(acc.shape, F32)
        su[...] = jnp.zeros(su.shape, F32)
        most = ints[qb * 8, KB]
        for h in range(1, HEADS):
            most = jnp.maximum(most, ints[qb * 8 + h, KB])
        count = (most + STEP - 1) // STEP

        @pl.loop(0, count)
        def _(t):
            for h in range(HEADS):
                head = qs[:, h * D : (h + 1) * D]
                top = mx[h]
                for u in range(STEP):
                    code = ints[qb * 8 + h, t * STEP + u]
                    kb = code & (KB - 1)
                    score = jnp.dot(head, keys[kb], preferred_element_type=F32)
                    factor = jnp.broadcast_to(factors[kb][None], (B // 8, 8, B)).reshape(B, B)
                    score = jnp.where(ahead <= (code >> 5) * B, score * factor, NEG)
                    sc[h, t * STEP + u] = score
                    top = jnp.maximum(top, score)
                mx[h] = top

        for h in range(HEADS):
            top = jnp.max(mx[h], axis=1, keepdims=True)
            mx[h] = jnp.broadcast_to(top, (B, B)).astype(BF16).astype(F32)

        @pl.loop(0, count)
        def _(t):
            for h in range(HEADS):
                top = mx[h]
                total = su[h]
                weights, columns = [], []
                for u in range(STEP):
                    code = ints[qb * 8 + h, t * STEP + u]
                    weight = jnp.exp2(sc[h, t * STEP + u] - top)
                    total = total + weight
                    weights.append(weight.astype(BF16))
                    columns.append(values[code & (KB - 1)])
                su[h] = total
                for u in range(0, STEP, 2):
                    acc[h] += jnp.dot(
                        jnp.concatenate(weights[u : u + 2], axis=1),
                        jnp.concatenate(columns[u : u + 2], axis=0),
                        preferred_element_type=F32,
                    )

        tile = extra[...]
        for h in range(HEADS):
            tile = jnp.where(lane == qb * 8 + h, mx[h], tile)
            total = jnp.broadcast_to(jnp.sum(su[h], axis=1, keepdims=True), (B, B))
            tile = jnp.where(lane == SUM_LANE + qb * 8 + h, total, tile)
            part = acc[h].astype(BF16)
            for d in range(NY):
                out[d, qb, :, h * D : (h + 1) * D] = part[d * PART : (d + 1) * PART]
        extra[...] = tile

    for d in range(NY):
        extra_out[d] = extra[d * PART : (d + 1) * PART].astype(BF16)


def attend(lists, q_all, keys, values, factors):
    return pl.pallas_call(
        attend_kernel,
        out_shape=[
            jax.ShapeDtypeStruct((NY, QB, PART, SLICE), BF16),
            jax.ShapeDtypeStruct((NY, PART, 128), BF16),
        ],
        in_specs=[SMEM] + [VMEM] * 4,
        out_specs=[VMEM] * 2,
        scratch_shapes=[
            pltpu.VMEM((B, SLICE), BF16),
            pltpu.VMEM((HEADS, KB, B, B), F32),
            pltpu.VMEM((HEADS, B, B), F32),
            pltpu.VMEM((HEADS, B, D), F32),
            pltpu.VMEM((HEADS, B, B), F32),
            pltpu.VMEM((B, B), F32),
        ],
        compiler_params=pltpu.CompilerParams(vmem_limit_bytes=36 << 20),
        name="attend",
    )(lists, q_all, keys, values, factors)


def gather_kernel(
    p, extra_in, out, parts, extra, att, e_send, e_recv, y_send, y_recv, x_send, x_recv, own
):
    rep, z, c, x, y = place()
    xs = [(x + d) % NX for d in range(NX)]
    ys = [(y + d) % NY for d in range(NY)]
    at_x = [(rep, xs[d] * NY + y) for d in range(NX)]
    at_y = [(rep, x * NY + ys[d]) for d in range(NY)]
    greet(at_x[1:] + at_y[1:])

    ex = [None] * NY
    py = [[None] * NY for _ in range(QB)]
    px = [[None] * NX for _ in range(QB)]
    for d in FAR:
        ex[d] = remote(extra_in.at[ys[d]], extra.at[d], e_send.at[d], e_recv.at[d], at_y[d])
        ex[d].start()
    for b in range(QB):
        for d in FAR:
            py[b][d] = remote(p.at[ys[d], b], parts.at[d, b], y_send.at[b, d], y_recv.at[b, d], at_y[d])
            py[b][d].start()
    for d in FAR:
        ex[d].wait_recv()
    marks = [extra_in[y].astype(F32)] + [extra[d].astype(F32) for d in range(1, NY)]
    top = functools.reduce(jnp.maximum, marks)
    shift = [jnp.exp2(e - top) for e in marks]
    total = sum(w * pltpu.roll(e, SUM_LANE, 1) for w, e in zip(shift, marks))
    lane = iota((PART, 128), 1)
    total = jnp.where((lane < QB * 8) & ((lane & 7) < HEADS), total, 1.0)
    ratio = [w / total for w in shift]
    mine = pl.ds(pl.multiple_of(x * SLICE, SLICE), SLICE)

    for b in range(QB):
        for d in FAR:
            py[b][d].wait_recv()
        for h in range(HEADS):
            cols = slice(h * D, (h + 1) * D)
            at = b * 8 + h
            value = sum(
                jnp.broadcast_to(ratio[d][:, at : at + 1], (PART, D))
                * (parts[d, b, :, cols] if d else p[y, b, :, cols]).astype(F32)
                for d in range(NY)
            )
            value = value.reshape(NX, ROWS, D).astype(BF16)
            for d in range(NX):
                att[b, d, :, cols] = value[d]
        for d in FAR:
            px[b][d] = remote(
                att.at[b, xs[d]], out.at[b, :, mine], x_send.at[b, d], x_recv.at[b, d], at_x[d]
            )
            px[b][d].start()
        px[b][0] = pltpu.make_async_copy(att.at[b, x], out.at[b, :, mine], own.at[b])
        px[b][0].start()

    for d in FAR:
        ex[d].wait_send()
    for b in range(QB):
        px[b][0].wait()
        for d in FAR:
            px[b][d].wait_recv()
            px[b][d].wait_send()
            py[b][d].wait_send()


def gather(p, extra):
    return pl.pallas_call(
        gather_kernel,
        out_shape=jax.ShapeDtypeStruct((QB, ROWS, NX * SLICE), BF16),
        in_specs=[VMEM, VMEM],
        out_specs=VMEM,
        scratch_shapes=[
            pltpu.VMEM((NY, QB, PART, SLICE), BF16),
            pltpu.VMEM((NY, PART, 128), BF16),
            pltpu.VMEM((QB, NX, ROWS, SLICE), BF16),
        ]
        + [DMA((NY,))] * 2
        + [DMA((QB, NY))] * 2
        + [DMA((QB, NX))] * 2
        + [DMA((QB,))],
        compiler_params=pltpu.CompilerParams(
            collective_id=1, has_side_effects=True, vmem_limit_bytes=16 << 20
        ),
        name="gather",
    )(p, extra)


def per_device(queries, key_cache, value_cache, key_scale, value_scale, pattern, target):
    q_all, keys, values, factors, lists = spread(
        target,
        queries,
        key_cache,
        value_cache,
        key_scale.T,
        value_scale.T,
        jnp.swapaxes(pattern, 1, 2),
    )
    part, extra = attend(lists, q_all, keys, values, factors)
    return gather(part, extra)


def solution(mesh):
    return jax.shard_map(
        per_device,
        mesh=mesh,
        in_specs=(
            P("replica", "ctx", None),
            P("ctx", None),
            P("ctx", None),
            P("ctx", None),
            P("ctx", None),
            P(),
            P(),
        ),
        out_specs=P("replica", "ctx", None),
        check_vma=False,
    )
```

```python
import functools
import math

import jax
import jax.numpy as jnp
from jax import lax
from jax.experimental import pallas as pl
from jax.experimental.pallas import tpu as pltpu
from jax.sharding import PartitionSpec as P

MESH = pl.DeviceIdType.MESH
BF16 = jnp.bfloat16
F32 = jnp.float32
I32 = jnp.int32

NX = 4
NY = 4
NZ = 8
HEADS = 7
D = 128
B = 128
QB = 4
KB = 32
SHARD = 8
SLICE = HEADS * D
ROWS = B // (NX * NY)
PART = NX * ROWS
KEYS = SHARD * B
PAIRS = 32
SUM_LANE = 64
NEG = -(2.0**100)
STEP = 4
FIRST = 64
FAR = (1, 3, 2)
ORDER = (8, 9, 6, 7, 10, 11, 4, 5, 12, 13, 2, 3, 14, 15, 1, 0)
TO_LOG2 = math.log2(math.e) / math.sqrt(D)

DMA = pltpu.SemaphoreType.DMA
HBM = pl.BlockSpec(memory_space=pltpu.HBM)
VMEM = pl.BlockSpec(memory_space=pltpu.VMEM)
SMEM = pl.BlockSpec(memory_space=pltpu.SMEM)


def place():
    rep = lax.axis_index("replica")
    ctx = lax.axis_index("ctx")
    return rep, rep // 2, rep % 2, ctx // NY, ctx % NY


def greet(partners):
    barrier = pltpu.get_barrier_semaphore()
    for who in partners:
        pl.semaphore_signal(barrier, inc=1, device_id=who, device_id_type=MESH)
    pl.semaphore_wait(barrier, len(partners))


def remote(src, dst, send, recv, who):
    return pltpu.make_async_remote_copy(
        src_ref=src, dst_ref=dst, send_sem=send, recv_sem=recv, device_id=who, device_id_type=MESH
    )


def iota(shape, dim):
    return lax.broadcasted_iota(I32, shape, dim)


def block_lists(listed, blocks, y):
    shape = (PAIRS, 128)
    lane, row = iota(shape, 1), iota(shape, 0)
    block = (lane >> 3) * (SHARD * NY) + y * SHARD + (lane & 7)
    hits = jnp.zeros(shape, I32)
    own = jnp.zeros(shape, I32)
    column = iota(listed.shape[1:], 1)
    for s in range(QB):
        own = jnp.where(row >> 3 == s, blocks[s], own)
        for h in range(HEADS):
            entry = jnp.max(jnp.where(column == blocks[s], listed[h], -1), axis=1, keepdims=True)
            found = (jnp.broadcast_to(entry, shape) == block).astype(I32)
            found = jnp.max(found, axis=0, keepdims=True)
            hits = jnp.where(row == s * 8 + h, found, hits)
    below = FIRST + own - block
    hits = jnp.where(below == 0, 1, hits)
    hits = jnp.where((below >= 0) & (lane < KB) & ((row & 7) < HEADS), hits, 0)
    upto = hits
    for s in (1, 2, 4, 8, 16):
        upto = upto + jnp.where(lane >= s, pltpu.roll(upto, s, 1), 0)
    slot = jnp.where(hits > 0, upto - 1, -1)
    code = lane + KB * below
    packed = jnp.full(shape, -KB * 1024, I32)
    for b in range(KB):
        at = jnp.broadcast_to(slot[:, b : b + 1], shape) == lane
        packed = jnp.where(at, jnp.broadcast_to(code[:, b : b + 1], shape), packed)
    number = jnp.broadcast_to(upto[:, KB - 1 : KB], shape)
    return jnp.where(lane == KB, number, packed)


def spread_kernel(
    target, q, k, v, ks, vs, pattern,
    q_all, keys, values, factors, lists,
    held0, held1, held2, held3, packed, came0, came1, came2, came3,
    k_land, v_land, scales, k_loc, v_loc, listed, goes,
    z_send, z_recv, q_send, q_recv, y_send, y_recv, k_send, k_recv, v_send, v_recv, s_send, s_recv,
    kc_send, kc_recv, vc_send, vc_recv, own,
):
    rep, z, c, x, y = place()
    sib = (rep + 1 - 2 * c, x * NY + y)
    xs = [(x + d) % NX for d in range(NX)]
    back = [(x + NX - d) % NX for d in range(NX)]
    at_x = [(rep, xs[d] * NY + y) for d in range(NX)]
    at_y = [(rep, x * NY + (y + d) % NY) for d in range(NY)]
    half = pl.ds(pl.multiple_of(c * (KEYS // 2), KEYS // 2), KEYS // 2)
    groups = [((z + d) % NZ) * 2 + (c + e) % 2 for d in range(NZ) for e in range(2)]
    at_group = [(g, x * NY + y) for g in groups]
    held = (held0, held1, held2, held3)
    came = (came0, came1, came2, came3)

    def cols(d, n):
        return pl.ds(pl.multiple_of(xs[d] * n, n), n)

    partners = at_group[1:] + at_x[1:] + at_y[1:]
    barrier = pltpu.get_barrier_semaphore()
    for who in partners:
        pl.semaphore_signal(barrier, inc=1, device_id=who, device_id_type=MESH)
    stay = [
        pltpu.make_async_copy(target, goes, own.at[0]),
        pltpu.make_async_copy(q.at[:, :, cols(0, SLICE)], held[0], own.at[1]),
        pltpu.make_async_copy(ks, k_loc, own.at[2]),
        pltpu.make_async_copy(vs, v_loc, own.at[3]),
        pltpu.make_async_copy(pattern.at[pl.ds(x * HEADS, HEADS)], listed, own.at[4]),
        pltpu.make_async_copy(k.at[:, cols(0, D)], k_land.at[0], own.at[5]),
        pltpu.make_async_copy(v.at[:, cols(0, D)], v_land.at[0], own.at[6]),
    ]
    for copy in stay:
        copy.start()

    qx, kx, vx, sx, kc, vc = ([None] * NX for _ in range(6))
    qy = [[None] * NY for _ in range(NX)]
    qz = [[None] * len(groups) for _ in range(NX)]

    stay[0].wait()
    goes_to = [goes[rep * QB + b] for b in range(QB)]
    leaving = []
    for group in groups:
        b = jnp.int32(0)
        for other in range(1, QB):
            b = jnp.where(goes_to[other] == group, other, b)
        leaving.append(b)

    def pack(d):
        for n in ORDER:
            block = held[d][leaving[n]]
            if n == 0:
                came[d][n] = block
            else:
                packed[d, n] = block

    def over_z(d):
        for n in ORDER[:-1]:
            qz[d][n] = remote(packed.at[d, n], came[d].at[n], z_send.at[d, n], z_recv.at[d, n], at_group[n])
            qz[d][n].start()

    stay[1].wait()
    pack(0)
    scales[0] = jnp.zeros((2 * NX, 128), F32)
    stay[2].wait()
    stay[3].wait()
    scales[0, 0:NX, 0:SHARD] = k_loc[...]
    scales[0, NX : 2 * NX, 0:SHARD] = v_loc[...]

    pl.semaphore_wait(barrier, len(partners))
    for d in FAR:
        qx[d] = remote(q.at[:, :, cols(d, SLICE)], held[d], q_send.at[d], q_recv.at[d], at_x[d])
        qx[d].start()
    over_z(0)
    for d in FAR:
        sx[d] = remote(scales.at[0], scales.at[d], s_send.at[d], s_recv.at[d], at_x[d])
        sx[d].start()
    for d in FAR:
        kx[d] = remote(k.at[half, cols(d, D)], k_land.at[d, half], k_send.at[d], k_recv.at[d], at_x[d])
        vx[d] = remote(v.at[half, cols(d, D)], v_land.at[d, half], v_send.at[d], v_recv.at[d], at_x[d])
        kx[d].start()
        vx[d].start()

    def look(j, state):
        found, *at = state
        hit = goes[j] == rep
        at = [jnp.where(hit & (found == s), j, a) for s, a in enumerate(at)]
        return (found + hit.astype(I32), *at)

    _, *blocks = lax.fori_loop(0, 2 * NZ * QB, look, (jnp.int32(0),) * (1 + QB))

    for d in FAR:
        qx[d].wait_recv()
        pack(d)
        over_z(d)

    stay[4].wait()
    lists[...] = block_lists(listed, blocks, y)

    scale_row = iota((2 * NX, 128), 0)

    def pick_row(tile, n):
        return jnp.sum(jnp.where(scale_row == n, tile, 0.0), axis=0, keepdims=True)

    def finish(d):
        tile = scales[d]
        for_keys = pick_row(tile, x) * TO_LOG2
        for_values = pick_row(tile, NX + x)
        for b in range(SHARD):
            at = back[d] * SHARD + b
            factors[at] = jnp.broadcast_to(for_keys[:, b : b + 1], (8, 128))
            rows = slice(b * B, (b + 1) * B)
            keys[at] = k_land[d, rows].T
            scaled = v_land[d, rows].astype(F32) * jnp.broadcast_to(for_values[:, b : b + 1], (B, D))
            values[at] = scaled.astype(BF16)

    def hand_over(d):
        kx[d].wait_recv()
        kc[d] = remote(k_land.at[d, half], k_land.at[d, half], kc_send.at[d], kc_recv.at[d], sib)
        kc[d].start()
        vx[d].wait_recv()
        vc[d] = remote(v_land.at[d, half], v_land.at[d, half], vc_send.at[d], vc_recv.at[d], sib)
        vc[d].start()
        sx[d].wait_recv()

    def whole(d):
        kc[d].wait_recv()
        vc[d].wait_recv()
        finish(d)

    def over_y(d):
        for n in range(1, len(groups)):
            qz[d][n].wait_recv()
        for s in range(QB):
            source = blocks[s] >> 2
            n = (((z + NZ - (source >> 1)) & (NZ - 1)) << 1) + ((source & 1) ^ c)
            q_all[y, back[d], s] = came[d][n]
        for e in FAR:
            piece = q_all.at[y, back[d]]
            qy[d][e] = remote(piece, piece, y_send.at[d, e], y_recv.at[d, e], at_y[e])
            qy[d][e].start()

    for copy in stay[5:]:
        copy.wait()
    finish(0)
    hand_over(1)
    hand_over(3)
    over_y(0)
    whole(1)
    whole(3)
    over_y(1)
    hand_over(2)
    whole(2)
    over_y(3)
    over_y(2)
    for d in range(NX):
        for e in FAR:
            qy[d][e].wait_recv()
            qy[d][e].wait_send()
    for d in FAR:
        for copy in (qx[d], kx[d], vx[d], sx[d], kc[d], vc[d]):
            copy.wait_send()
    for copies in qz:
        for copy in copies[1:]:
            copy.wait_send()


def spread(target, q, k, v, ks, vs, pattern):
    slots = pltpu.VMEM((2 * NZ, ROWS, SLICE), BF16)
    return pl.pallas_call(
        spread_kernel,
        out_shape=[
            jax.ShapeDtypeStruct((NY, NX, QB, ROWS, SLICE), BF16),
            jax.ShapeDtypeStruct((KB, D, B), BF16),
            jax.ShapeDtypeStruct((KB, B, D), BF16),
            jax.ShapeDtypeStruct((KB, 8, 128), F32),
            jax.ShapeDtypeStruct((PAIRS, 128), I32),
        ],
        in_specs=[HBM] * 7,
        out_specs=[VMEM] * 5,
        scratch_shapes=[pltpu.VMEM((QB, ROWS, SLICE), BF16)] * NX
        + [pltpu.VMEM((NX, 2 * NZ, ROWS, SLICE), BF16)]
        + [slots] * NX
        + [
            pltpu.VMEM((NX, KEYS, D), BF16),
            pltpu.VMEM((NX, KEYS, D), BF16),
            pltpu.VMEM((NX, 2 * NX, 128), F32),
            pltpu.VMEM((NX, SHARD), F32),
            pltpu.VMEM((NX, SHARD), F32),
            pltpu.VMEM((HEADS, *pattern.shape[1:]), I32),
            pltpu.SMEM(target.shape, I32),
        ]
        + [DMA((NX, 2 * NZ))] * 2
        + [DMA((NX,))] * 2
        + [DMA((NX, NY))] * 2
        + [DMA((NX,))] * 10
        + [DMA((7,))],
        compiler_params=pltpu.CompilerParams(
            collective_id=0, has_side_effects=True, vmem_limit_bytes=24 << 20
        ),
        name="spread",
    )(target, q, k, v, ks, vs, pattern)


def attend_kernel(ints, q_ref, keys, values, factors, out, extra_out, qs, sc, mx, acc, su, extra):
    row = iota((B, B), 0)
    row = ((row >> 3) & 3) * PART + (row >> 5) * ROWS + (row & 7)
    lane = iota((B, B), 1)
    ahead = lane - row
    extra[...] = jnp.zeros((B, B), F32)

    @pl.loop(0, QB)
    def _(qb):
        qs[...] = q_ref[:, :, qb].astype(F32).reshape(B, SLICE).astype(BF16)
        mx[...] = jnp.full(mx.shape, NEG, F32)
        acc[...] = jnp.zeros(acc.shape, F32)
        su[...] = jnp.zeros(su.shape, F32)
        most = ints[qb * 8, KB]
        for h in range(1, HEADS):
            most = jnp.maximum(most, ints[qb * 8 + h, KB])
        count = (most + STEP - 1) // STEP

        @pl.loop(0, count)
        def _(t):
            for h in range(HEADS):
                head = qs[:, h * D : (h + 1) * D]
                top = mx[h]
                for u in range(STEP):
                    code = ints[qb * 8 + h, t * STEP + u]
                    kb = code & (KB - 1)
                    score = jnp.dot(head, keys[kb], preferred_element_type=F32)
                    factor = jnp.broadcast_to(factors[kb][None], (B // 8, 8, B)).reshape(B, B)
                    score = jnp.where(ahead <= (code >> 5) * B, score * factor, NEG)
                    sc[h, t * STEP + u] = score
                    top = jnp.maximum(top, score)
                mx[h] = top

        for h in range(HEADS):
            top = jnp.max(mx[h], axis=1, keepdims=True)
            mx[h] = jnp.broadcast_to(top, (B, B)).astype(BF16).astype(F32)

        @pl.loop(0, count)
        def _(t):
            for h in range(HEADS):
                top = mx[h]
                total = su[h]
                weights, columns = [], []
                for u in range(STEP):
                    code = ints[qb * 8 + h, t * STEP + u]
                    weight = jnp.exp2(sc[h, t * STEP + u] - top)
                    total = total + weight
                    weights.append(weight.astype(BF16))
                    columns.append(values[code & (KB - 1)])
                su[h] = total
                for u in range(0, STEP, 2):
                    acc[h] += jnp.dot(
                        jnp.concatenate(weights[u : u + 2], axis=1),
                        jnp.concatenate(columns[u : u + 2], axis=0),
                        preferred_element_type=F32,
                    )

        tile = extra[...]
        for h in range(HEADS):
            tile = jnp.where(lane == qb * 8 + h, mx[h], tile)
            total = jnp.broadcast_to(jnp.sum(su[h], axis=1, keepdims=True), (B, B))
            tile = jnp.where(lane == SUM_LANE + qb * 8 + h, total, tile)
            part = acc[h].astype(BF16)
            for d in range(NY):
                out[d, qb, :, h * D : (h + 1) * D] = part[d * PART : (d + 1) * PART]
        extra[...] = tile

    for d in range(NY):
        extra_out[d] = extra[d * PART : (d + 1) * PART].astype(BF16)


def attend(lists, q_all, keys, values, factors):
    return pl.pallas_call(
        attend_kernel,
        out_shape=[
            jax.ShapeDtypeStruct((NY, QB, PART, SLICE), BF16),
            jax.ShapeDtypeStruct((NY, PART, 128), BF16),
        ],
        in_specs=[SMEM] + [VMEM] * 4,
        out_specs=[VMEM] * 2,
        scratch_shapes=[
            pltpu.VMEM((B, SLICE), BF16),
            pltpu.VMEM((HEADS, KB, B, B), F32),
            pltpu.VMEM((HEADS, B, B), F32),
            pltpu.VMEM((HEADS, B, D), F32),
            pltpu.VMEM((HEADS, B, B), F32),
            pltpu.VMEM((B, B), F32),
        ],
        compiler_params=pltpu.CompilerParams(vmem_limit_bytes=36 << 20),
        name="attend",
    )(lists, q_all, keys, values, factors)


def gather_kernel(
    p, extra_in, out, parts, extra, att, e_send, e_recv, y_send, y_recv, x_send, x_recv, own
):
    rep, z, c, x, y = place()
    xs = [(x + d) % NX for d in range(NX)]
    ys = [(y + d) % NY for d in range(NY)]
    at_x = [(rep, xs[d] * NY + y) for d in range(NX)]
    at_y = [(rep, x * NY + ys[d]) for d in range(NY)]
    greet(at_x[1:] + at_y[1:])

    ex = [None] * NY
    py = [[None] * NY for _ in range(QB)]
    px = [[None] * NX for _ in range(QB)]
    for d in FAR:
        ex[d] = remote(extra_in.at[ys[d]], extra.at[d], e_send.at[d], e_recv.at[d], at_y[d])
        ex[d].start()
    for b in range(QB):
        for d in FAR:
            py[b][d] = remote(p.at[ys[d], b], parts.at[d, b], y_send.at[b, d], y_recv.at[b, d], at_y[d])
            py[b][d].start()
    for d in FAR:
        ex[d].wait_recv()
    marks = [extra_in[y].astype(F32)] + [extra[d].astype(F32) for d in range(1, NY)]
    top = functools.reduce(jnp.maximum, marks)
    shift = [jnp.exp2(e - top) for e in marks]
    total = sum(w * pltpu.roll(e, SUM_LANE, 1) for w, e in zip(shift, marks))
    lane = iota((PART, 128), 1)
    total = jnp.where((lane < QB * 8) & ((lane & 7) < HEADS), total, 1.0)
    ratio = [w / total for w in shift]
    mine = pl.ds(pl.multiple_of(x * SLICE, SLICE), SLICE)

    for b in range(QB):
        for d in FAR:
            py[b][d].wait_recv()
        for h in range(HEADS):
            cols = slice(h * D, (h + 1) * D)
            at = b * 8 + h
            value = sum(
                jnp.broadcast_to(ratio[d][:, at : at + 1], (PART, D))
                * (parts[d, b, :, cols] if d else p[y, b, :, cols]).astype(F32)
                for d in range(NY)
            )
            value = value.reshape(NX, ROWS, D).astype(BF16)
            for d in range(NX):
                att[b, d, :, cols] = value[d]
        for d in FAR:
            px[b][d] = remote(
                att.at[b, xs[d]], out.at[b, :, mine], x_send.at[b, d], x_recv.at[b, d], at_x[d]
            )
            px[b][d].start()
        px[b][0] = pltpu.make_async_copy(att.at[b, x], out.at[b, :, mine], own.at[b])
        px[b][0].start()

    for d in FAR:
        ex[d].wait_send()
    for b in range(QB):
        px[b][0].wait()
        for d in FAR:
            px[b][d].wait_recv()
            px[b][d].wait_send()
            py[b][d].wait_send()


def gather(p, extra):
    return pl.pallas_call(
        gather_kernel,
        out_shape=jax.ShapeDtypeStruct((QB, ROWS, NX * SLICE), BF16),
        in_specs=[VMEM, VMEM],
        out_specs=VMEM,
        scratch_shapes=[
            pltpu.VMEM((NY, QB, PART, SLICE), BF16),
            pltpu.VMEM((NY, PART, 128), BF16),
            pltpu.VMEM((QB, NX, ROWS, SLICE), BF16),
        ]
        + [DMA((NY,))] * 2
        + [DMA((QB, NY))] * 2
        + [DMA((QB, NX))] * 2
        + [DMA((QB,))],
        compiler_params=pltpu.CompilerParams(
            collective_id=1, has_side_effects=True, vmem_limit_bytes=16 << 20
        ),
        name="gather",
    )(p, extra)


def hbm(array):
    return pltpu.with_memory_space_constraint(array, pltpu.HBM)


def per_device(queries, key_cache, value_cache, key_scale, value_scale, pattern, target):
    q_all, keys, values, factors, lists = spread(
        hbm(target),
        hbm(queries),
        hbm(key_cache),
        hbm(value_cache),
        hbm(key_scale.T),
        hbm(value_scale.T),
        hbm(jnp.swapaxes(pattern, 1, 2)),
    )
    part, extra = attend(lists, q_all, keys, values, factors)
    return gather(part, extra)


def solution(mesh):
    return jax.shard_map(
        per_device,
        mesh=mesh,
        in_specs=(
            P("replica", "ctx", None),
            P("ctx", None),
            P("ctx", None),
            P("ctx", None),
            P("ctx", None),
            P(),
            P(),
        ),
        out_specs=P("replica", "ctx", None),
        check_vma=False,
    )
```

```python
import functools
import math

import jax
import jax.numpy as jnp
from jax import lax
from jax.experimental import pallas as pl
from jax.experimental.pallas import tpu as pltpu
from jax.sharding import PartitionSpec as P

MESH = pl.DeviceIdType.MESH
BF16 = jnp.bfloat16
F32 = jnp.float32
I32 = jnp.int32

NX = 4
NY = 4
NZ = 8
HEADS = 7
D = 128
B = 128
QB = 4
KB = 32
SHARD = 8
SLICE = HEADS * D
ROWS = B // (NX * NY)
PART = NX * ROWS
KEYS = SHARD * B
PAIRS = 32
SUM_LANE = 64
NEG = -(2.0**100)
STEP = 4
FIRST = 64
FAR = (1, 3, 2)
TO_LOG2 = math.log2(math.e) / math.sqrt(D)

DMA = pltpu.SemaphoreType.DMA
HBM = pl.BlockSpec(memory_space=pltpu.HBM)
VMEM = pl.BlockSpec(memory_space=pltpu.VMEM)
SMEM = pl.BlockSpec(memory_space=pltpu.SMEM)


def place():
    rep = lax.axis_index("replica")
    ctx = lax.axis_index("ctx")
    return rep, rep // 2, rep % 2, ctx // NY, ctx % NY


def greet(partners):
    barrier = pltpu.get_barrier_semaphore()
    for who in partners:
        pl.semaphore_signal(barrier, inc=1, device_id=who, device_id_type=MESH)
    pl.semaphore_wait(barrier, len(partners))


def remote(src, dst, send, recv, who):
    return pltpu.make_async_remote_copy(
        src_ref=src, dst_ref=dst, send_sem=send, recv_sem=recv, device_id=who, device_id_type=MESH
    )


def iota(shape, dim):
    return lax.broadcasted_iota(I32, shape, dim)


def block_lists(listed, blocks, y):
    shape = (PAIRS, 128)
    lane, row = iota(shape, 1), iota(shape, 0)
    block = (lane >> 3) * (SHARD * NY) + y * SHARD + (lane & 7)
    hits = jnp.zeros(shape, I32)
    own = jnp.zeros(shape, I32)
    column = iota(listed.shape[1:], 1)
    for s in range(QB):
        own = jnp.where(row >> 3 == s, blocks[s], own)
        for h in range(HEADS):
            entry = jnp.max(jnp.where(column == blocks[s], listed[h], -1), axis=1, keepdims=True)
            found = (jnp.broadcast_to(entry, shape) == block).astype(I32)
            found = jnp.max(found, axis=0, keepdims=True)
            hits = jnp.where(row == s * 8 + h, found, hits)
    below = FIRST + own - block
    hits = jnp.where(below == 0, 1, hits)
    hits = jnp.where((below >= 0) & (lane < KB) & ((row & 7) < HEADS), hits, 0)
    upto = hits
    for s in (1, 2, 4, 8, 16):
        upto = upto + jnp.where(lane >= s, pltpu.roll(upto, s, 1), 0)
    slot = jnp.where(hits > 0, upto - 1, -1)
    code = lane + KB * below
    packed = jnp.full(shape, -KB * 1024, I32)
    for b in range(KB):
        at = jnp.broadcast_to(slot[:, b : b + 1], shape) == lane
        packed = jnp.where(at, jnp.broadcast_to(code[:, b : b + 1], shape), packed)
    number = jnp.broadcast_to(upto[:, KB - 1 : KB], shape)
    return jnp.where(lane == KB, number, packed)


def spread_kernel(
    target, q, k, v, ks, vs, pattern,
    q_all, keys, values, factors, lists,
    ring0, ring1, ring2, ring3, give, take,
    k_land, v_land, scales, k_loc, v_loc, listed, goes,
    up_send, up_recv, dn_send, dn_recv, g_send, g_recv,
    q_send, q_recv, y_send, y_recv, k_send, k_recv, v_send, v_recv, s_send, s_recv,
    kc_send, kc_recv, vc_send, vc_recv, own,
):
    rep, z, c, x, y = place()
    other = rep + 1 - 2 * c
    here = x * NY + y
    sib = (other, here)
    xs = [(x + d) % NX for d in range(NX)]
    back = [(x + NX - d) % NX for d in range(NX)]
    at_x = [(rep, xs[d] * NY + y) for d in range(NX)]
    at_y = [(rep, x * NY + (y + d) % NY) for d in range(NY)]
    half = pl.ds(pl.multiple_of(c * (KEYS // 2), KEYS // 2), KEYS // 2)
    at_zup = (((z + 1) % NZ) * 2 + c, here)
    at_zdn = (((z + NZ - 1) % NZ) * 2 + c, here)
    ring = (ring0, ring1, ring2, ring3)

    def cols(d, n):
        return pl.ds(pl.multiple_of(xs[d] * n, n), n)

    partners = [at_zup, at_zdn, sib] + at_x[1:] + at_y[1:]
    barrier = pltpu.get_barrier_semaphore()
    for who in partners:
        pl.semaphore_signal(barrier, inc=1, device_id=who, device_id_type=MESH)
    stay = [
        pltpu.make_async_copy(target, goes, own.at[0]),
        pltpu.make_async_copy(q.at[:, :, cols(0, SLICE)], ring[0].at[0], own.at[1]),
        pltpu.make_async_copy(ks, k_loc, own.at[2]),
        pltpu.make_async_copy(vs, v_loc, own.at[3]),
        pltpu.make_async_copy(pattern.at[pl.ds(x * HEADS, HEADS)], listed, own.at[4]),
        pltpu.make_async_copy(k.at[:, cols(0, D)], k_land.at[0], own.at[5]),
        pltpu.make_async_copy(v.at[:, cols(0, D)], v_land.at[0], own.at[6]),
    ]
    for copy in stay:
        copy.start()

    qx, kx, vx, sx, kc, vc = ([None] * NX for _ in range(6))
    qy = [[None] * NY for _ in range(NX)]
    zu, zd = ([[None] * 5 for _ in range(NX)] for _ in range(2))
    handed = [None] * NX

    scales[0] = jnp.zeros((2 * NX, 128), F32)
    stay[2].wait()
    stay[3].wait()
    scales[0, 0:NX, 0:SHARD] = k_loc[...]
    scales[0, NX : 2 * NX, 0:SHARD] = v_loc[...]

    stay[0].wait()

    def look(j, state):
        mine = goes[j] == rep
        theirs = goes[j] == other
        found, passed, *at = state
        tests = [(mine, found, s) for s in range(QB)] + [(theirs, passed, s) for s in range(QB)]
        at = [jnp.where(hit & (n == s), j, old) for old, (hit, n, s) in zip(at, tests)]
        return (found + mine.astype(I32), passed + theirs.astype(I32), *at)

    _, _, *at = lax.fori_loop(0, 2 * NZ * QB, look, (jnp.int32(0),) * (2 + 2 * QB))
    blocks, to_give = at[:QB], at[QB:]

    def over_z(d, k):
        low, high = (pl.ds(0, QB // 2), pl.ds(QB // 2, QB // 2)) if k == 4 else (pl.ds(0, QB),) * 2
        zu[d][k] = remote(
            ring[d].at[k - 1, low], ring[d].at[k, low], up_send.at[d, k], up_recv.at[d, k], at_zup
        )
        zd[d][k] = remote(
            ring[d].at[(NZ + 1 - k) % NZ, high], ring[d].at[NZ - k, high],
            dn_send.at[d, k], dn_recv.at[d, k], at_zdn,
        )
        zu[d][k].start()
        zd[d][k].start()

    def onward(d, k):
        zu[d][k].wait_recv()
        zd[d][k].wait_recv()
        if k < 4:
            over_z(d, k + 1)
        else:
            for s in range(QB):
                give[d, s] = ring[d][(z + NZ - (to_give[s] >> 3)) & (NZ - 1), to_give[s] & (QB - 1)]
            handed[d] = remote(give.at[d], take.at[d], g_send.at[d], g_recv.at[d], sib)
            handed[d].start()

    stay[1].wait()
    pl.semaphore_wait(barrier, len(partners))
    for d in FAR:
        qx[d] = remote(q.at[:, :, cols(d, SLICE)], ring[d].at[0], q_send.at[d], q_recv.at[d], at_x[d])
        qx[d].start()
    over_z(0, 1)
    for d in FAR:
        sx[d] = remote(scales.at[0], scales.at[d], s_send.at[d], s_recv.at[d], at_x[d])
        sx[d].start()
    for d in FAR:
        kx[d] = remote(k.at[half, cols(d, D)], k_land.at[d, half], k_send.at[d], k_recv.at[d], at_x[d])
        vx[d] = remote(v.at[half, cols(d, D)], v_land.at[d, half], v_send.at[d], v_recv.at[d], at_x[d])
        kx[d].start()
        vx[d].start()

    def from_x(d):
        qx[d].wait_recv()
        over_z(d, 1)

    scale_row = iota((2 * NX, 128), 0)

    def pick_row(tile, n):
        return jnp.sum(jnp.where(scale_row == n, tile, 0.0), axis=0, keepdims=True)

    def finish(d):
        tile = scales[d]
        for_keys = pick_row(tile, x) * TO_LOG2
        for_values = pick_row(tile, NX + x)
        for b in range(SHARD):
            at = back[d] * SHARD + b
            factors[at] = jnp.broadcast_to(for_keys[:, b : b + 1], (8, 128))
            rows = slice(b * B, (b + 1) * B)
            keys[at] = k_land[d, rows].T
            scaled = v_land[d, rows].astype(F32) * jnp.broadcast_to(for_values[:, b : b + 1], (B, D))
            values[at] = scaled.astype(BF16)

    def hand_over(d):
        kx[d].wait_recv()
        kc[d] = remote(k_land.at[d, half], k_land.at[d, half], kc_send.at[d], kc_recv.at[d], sib)
        kc[d].start()
        vx[d].wait_recv()
        vc[d] = remote(v_land.at[d, half], v_land.at[d, half], vc_send.at[d], vc_recv.at[d], sib)
        vc[d].start()
        sx[d].wait_recv()

    def whole(d):
        kc[d].wait_recv()
        vc[d].wait_recv()
        finish(d)

    def over_y(d):
        handed[d].wait_recv()
        for s in range(QB):
            near = ring[d][(z + NZ - (blocks[s] >> 3)) & (NZ - 1), blocks[s] & (QB - 1)]
            q_all[y, back[d], s] = jnp.where(((blocks[s] >> 2) & 1) == c, near, take[d, s])
        for e in FAR:
            piece = q_all.at[y, back[d]]
            qy[d][e] = remote(piece, piece, y_send.at[d, e], y_recv.at[d, e], at_y[e])
            qy[d][e].start()

    from_x(1)
    onward(0, 1)
    from_x(3)
    onward(1, 1)
    onward(0, 2)
    from_x(2)
    stay[4].wait()
    lists[...] = block_lists(listed, blocks, y)
    onward(3, 1)
    onward(1, 2)
    onward(0, 3)
    onward(2, 1)
    for copy in stay[5:]:
        copy.wait()
    finish(0)
    onward(3, 2)
    onward(1, 3)
    onward(0, 4)
    hand_over(1)
    onward(2, 2)
    onward(3, 3)
    over_y(0)
    hand_over(3)
    whole(1)
    onward(1, 4)
    onward(2, 3)
    over_y(1)
    hand_over(2)
    onward(3, 4)
    whole(3)
    over_y(3)
    onward(2, 4)
    whole(2)
    over_y(2)
    for d in range(NX):
        for e in FAR:
            qy[d][e].wait_recv()
            qy[d][e].wait_send()
    for d in FAR:
        for copy in (qx[d], kx[d], vx[d], sx[d], kc[d], vc[d]):
            copy.wait_send()
    for d in range(NX):
        handed[d].wait_send()
        for k in range(1, 5):
            zu[d][k].wait_send()
            zd[d][k].wait_send()


def spread(target, q, k, v, ks, vs, pattern):
    return pl.pallas_call(
        spread_kernel,
        out_shape=[
            jax.ShapeDtypeStruct((NY, NX, QB, ROWS, SLICE), BF16),
            jax.ShapeDtypeStruct((KB, D, B), BF16),
            jax.ShapeDtypeStruct((KB, B, D), BF16),
            jax.ShapeDtypeStruct((KB, 8, 128), F32),
            jax.ShapeDtypeStruct((PAIRS, 128), I32),
        ],
        in_specs=[HBM] * 7,
        out_specs=[VMEM] * 5,
        scratch_shapes=[pltpu.VMEM((NZ, QB, ROWS, SLICE), BF16)] * NX
        + [pltpu.VMEM((NX, QB, ROWS, SLICE), BF16)] * 2
        + [
            pltpu.VMEM((NX, KEYS, D), BF16),
            pltpu.VMEM((NX, KEYS, D), BF16),
            pltpu.VMEM((NX, 2 * NX, 128), F32),
            pltpu.VMEM((NX, SHARD), F32),
            pltpu.VMEM((NX, SHARD), F32),
            pltpu.VMEM((HEADS, *pattern.shape[1:]), I32),
            pltpu.SMEM(target.shape, I32),
        ]
        + [DMA((NX, 5))] * 4
        + [DMA((NX,))] * 4
        + [DMA((NX, NY))] * 2
        + [DMA((NX,))] * 10
        + [DMA((7,))],
        compiler_params=pltpu.CompilerParams(
            collective_id=0, has_side_effects=True, vmem_limit_bytes=24 << 20
        ),
        name="spread",
    )(target, q, k, v, ks, vs, pattern)


def attend_kernel(ints, q_ref, keys, values, factors, out, extra_out, qs, sc, mx, acc, su, extra):
    row = iota((B, B), 0)
    row = ((row >> 3) & 3) * PART + (row >> 5) * ROWS + (row & 7)
    lane = iota((B, B), 1)
    ahead = lane - row
    extra[...] = jnp.zeros((B, B), F32)

    @pl.loop(0, QB)
    def _(qb):
        qs[...] = q_ref[:, :, qb].astype(F32).reshape(B, SLICE).astype(BF16)
        mx[...] = jnp.full(mx.shape, NEG, F32)
        acc[...] = jnp.zeros(acc.shape, F32)
        su[...] = jnp.zeros(su.shape, F32)
        most = ints[qb * 8, KB]
        for h in range(1, HEADS):
            most = jnp.maximum(most, ints[qb * 8 + h, KB])
        count = (most + STEP - 1) // STEP

        @pl.loop(0, count)
        def _(t):
            for h in range(HEADS):
                head = qs[:, h * D : (h + 1) * D]
                top = mx[h]
                for u in range(STEP):
                    code = ints[qb * 8 + h, t * STEP + u]
                    kb = code & (KB - 1)
                    score = jnp.dot(head, keys[kb], preferred_element_type=F32)
                    factor = jnp.broadcast_to(factors[kb][None], (B // 8, 8, B)).reshape(B, B)
                    score = jnp.where(ahead <= (code >> 5) * B, score * factor, NEG)
                    sc[h, t * STEP + u] = score
                    top = jnp.maximum(top, score)
                mx[h] = top

        for h in range(HEADS):
            top = jnp.max(mx[h], axis=1, keepdims=True)
            mx[h] = jnp.broadcast_to(top, (B, B)).astype(BF16).astype(F32)

        @pl.loop(0, count)
        def _(t):
            for h in range(HEADS):
                top = mx[h]
                total = su[h]
                weights, columns = [], []
                for u in range(STEP):
                    code = ints[qb * 8 + h, t * STEP + u]
                    weight = jnp.exp2(sc[h, t * STEP + u] - top)
                    total = total + weight
                    weights.append(weight.astype(BF16))
                    columns.append(values[code & (KB - 1)])
                su[h] = total
                for u in range(0, STEP, 2):
                    acc[h] += jnp.dot(
                        jnp.concatenate(weights[u : u + 2], axis=1),
                        jnp.concatenate(columns[u : u + 2], axis=0),
                        preferred_element_type=F32,
                    )

        tile = extra[...]
        for h in range(HEADS):
            tile = jnp.where(lane == qb * 8 + h, mx[h], tile)
            total = jnp.broadcast_to(jnp.sum(su[h], axis=1, keepdims=True), (B, B))
            tile = jnp.where(lane == SUM_LANE + qb * 8 + h, total, tile)
            part = acc[h].astype(BF16)
            for d in range(NY):
                out[d, qb, :, h * D : (h + 1) * D] = part[d * PART : (d + 1) * PART]
        extra[...] = tile

    for d in range(NY):
        extra_out[d] = extra[d * PART : (d + 1) * PART].astype(BF16)


def attend(lists, q_all, keys, values, factors):
    return pl.pallas_call(
        attend_kernel,
        out_shape=[
            jax.ShapeDtypeStruct((NY, QB, PART, SLICE), BF16),
            jax.ShapeDtypeStruct((NY, PART, 128), BF16),
        ],
        in_specs=[SMEM] + [VMEM] * 4,
        out_specs=[VMEM] * 2,
        scratch_shapes=[
            pltpu.VMEM((B, SLICE), BF16),
            pltpu.VMEM((HEADS, KB, B, B), F32),
            pltpu.VMEM((HEADS, B, B), F32),
            pltpu.VMEM((HEADS, B, D), F32),
            pltpu.VMEM((HEADS, B, B), F32),
            pltpu.VMEM((B, B), F32),
        ],
        compiler_params=pltpu.CompilerParams(vmem_limit_bytes=36 << 20),
        name="attend",
    )(lists, q_all, keys, values, factors)


def gather_kernel(
    p, extra_in, out, parts, extra, att, e_send, e_recv, y_send, y_recv, x_send, x_recv, own
):
    rep, z, c, x, y = place()
    xs = [(x + d) % NX for d in range(NX)]
    ys = [(y + d) % NY for d in range(NY)]
    at_x = [(rep, xs[d] * NY + y) for d in range(NX)]
    at_y = [(rep, x * NY + ys[d]) for d in range(NY)]
    greet(at_x[1:] + at_y[1:])

    ex = [None] * NY
    py = [[None] * NY for _ in range(QB)]
    px = [[None] * NX for _ in range(QB)]
    for d in FAR:
        ex[d] = remote(extra_in.at[ys[d]], extra.at[d], e_send.at[d], e_recv.at[d], at_y[d])
        ex[d].start()
    for b in range(QB):
        for d in FAR:
            py[b][d] = remote(p.at[ys[d], b], parts.at[d, b], y_send.at[b, d], y_recv.at[b, d], at_y[d])
            py[b][d].start()
    for d in FAR:
        ex[d].wait_recv()
    marks = [extra_in[y].astype(F32)] + [extra[d].astype(F32) for d in range(1, NY)]
    top = functools.reduce(jnp.maximum, marks)
    shift = [jnp.exp2(e - top) for e in marks]
    total = sum(w * pltpu.roll(e, SUM_LANE, 1) for w, e in zip(shift, marks))
    lane = iota((PART, 128), 1)
    total = jnp.where((lane < QB * 8) & ((lane & 7) < HEADS), total, 1.0)
    ratio = [w / total for w in shift]
    mine = pl.ds(pl.multiple_of(x * SLICE, SLICE), SLICE)

    for b in range(QB):
        for d in FAR:
            py[b][d].wait_recv()
        for h in range(HEADS):
            cols = slice(h * D, (h + 1) * D)
            at = b * 8 + h
            value = sum(
                jnp.broadcast_to(ratio[d][:, at : at + 1], (PART, D))
                * (parts[d, b, :, cols] if d else p[y, b, :, cols]).astype(F32)
                for d in range(NY)
            )
            value = value.reshape(NX, ROWS, D).astype(BF16)
            for d in range(NX):
                att[b, d, :, cols] = value[d]
        for d in FAR:
            px[b][d] = remote(
                att.at[b, xs[d]], out.at[b, :, mine], x_send.at[b, d], x_recv.at[b, d], at_x[d]
            )
            px[b][d].start()
        px[b][0] = pltpu.make_async_copy(att.at[b, x], out.at[b, :, mine], own.at[b])
        px[b][0].start()

    for d in FAR:
        ex[d].wait_send()
    for b in range(QB):
        px[b][0].wait()
        for d in FAR:
            px[b][d].wait_recv()
            px[b][d].wait_send()
            py[b][d].wait_send()


def gather(p, extra):
    return pl.pallas_call(
        gather_kernel,
        out_shape=jax.ShapeDtypeStruct((QB, ROWS, NX * SLICE), BF16),
        in_specs=[VMEM, VMEM],
        out_specs=VMEM,
        scratch_shapes=[
            pltpu.VMEM((NY, QB, PART, SLICE), BF16),
            pltpu.VMEM((NY, PART, 128), BF16),
            pltpu.VMEM((QB, NX, ROWS, SLICE), BF16),
        ]
        + [DMA((NY,))] * 2
        + [DMA((QB, NY))] * 2
        + [DMA((QB, NX))] * 2
        + [DMA((QB,))],
        compiler_params=pltpu.CompilerParams(
            collective_id=1, has_side_effects=True, vmem_limit_bytes=16 << 20
        ),
        name="gather",
    )(p, extra)


def hbm(array):
    return pltpu.with_memory_space_constraint(array, pltpu.HBM)


def per_device(queries, key_cache, value_cache, key_scale, value_scale, pattern, target):
    q_all, keys, values, factors, lists = spread(
        hbm(target),
        hbm(queries),
        hbm(key_cache),
        hbm(value_cache),
        hbm(key_scale.T),
        hbm(value_scale.T),
        hbm(jnp.swapaxes(pattern, 1, 2)),
    )
    part, extra = attend(lists, q_all, keys, values, factors)
    return gather(part, extra)


def solution(mesh):
    return jax.shard_map(
        per_device,
        mesh=mesh,
        in_specs=(
            P("replica", "ctx", None),
            P("ctx", None),
            P("ctx", None),
            P("ctx", None),
            P("ctx", None),
            P(),
            P(),
        ),
        out_specs=P("replica", "ctx", None),
        check_vma=False,
    )
```

```python
import functools
import math

import jax
import jax.numpy as jnp
from jax import lax
from jax.experimental import pallas as pl
from jax.experimental.pallas import tpu as pltpu
from jax.sharding import PartitionSpec as P

MESH = pl.DeviceIdType.MESH
BF16 = jnp.bfloat16
F32 = jnp.float32
I32 = jnp.int32

NX = 4
NY = 4
NZ = 8
HEADS = 7
D = 128
B = 128
QB = 4
KB = 32
SHARD = 8
SLICE = HEADS * D
ROWS = B // (NX * NY)
PART = NX * ROWS
KEYS = SHARD * B
PAIRS = 32
SUM_LANE = 64
NEG = -(2.0**100)
STEP = 24
TOGETHER = 2
LANES = 8 * TOGETHER
FIRST = 64
FAR = (1, 3, 2)
ORDER = (8, 9, 6, 7, 10, 11, 4, 5, 12, 13, 2, 3, 14, 15, 1, 0)
TO_LOG2 = math.log2(math.e) / math.sqrt(D)

DMA = pltpu.SemaphoreType.DMA
HBM = pl.BlockSpec(memory_space=pltpu.HBM)
VMEM = pl.BlockSpec(memory_space=pltpu.VMEM)
SMEM = pl.BlockSpec(memory_space=pltpu.SMEM)


def place():
    rep = lax.axis_index("replica")
    ctx = lax.axis_index("ctx")
    return rep, rep // 2, rep % 2, ctx // NY, ctx % NY


def greet(partners):
    barrier = pltpu.get_barrier_semaphore()
    for who in partners:
        pl.semaphore_signal(barrier, inc=1, device_id=who, device_id_type=MESH)
    pl.semaphore_wait(barrier, len(partners))


def remote(src, dst, send, recv, who):
    return pltpu.make_async_remote_copy(
        src_ref=src, dst_ref=dst, send_sem=send, recv_sem=recv, device_id=who, device_id_type=MESH
    )


def iota(shape, dim):
    return lax.broadcasted_iota(I32, shape, dim)


def block_lists(listed, blocks, y):
    shape = (PAIRS, 128)
    lane, row = iota(shape, 1), iota(shape, 0)
    block = (lane >> 3) * (SHARD * NY) + y * SHARD + (lane & 7)
    hits = jnp.zeros(shape, I32)
    own = jnp.zeros(shape, I32)
    column = iota(listed.shape[1:], 1)
    for s in range(QB):
        own = jnp.where(row >> 3 == s, blocks[s], own)
        for h in range(HEADS):
            entry = jnp.max(jnp.where(column == blocks[s], listed[h], -1), axis=1, keepdims=True)
            found = (jnp.broadcast_to(entry, shape) == block).astype(I32)
            found = jnp.max(found, axis=0, keepdims=True)
            hits = jnp.where(row == s * 8 + h, found, hits)
    below = FIRST + own - block
    hits = jnp.where(below == 0, 1, hits)
    hits = jnp.where((below >= 0) & (lane < KB) & ((row & 7) < HEADS), hits, 0)
    upto = hits
    for s in (1, 2, 4, 8, 16):
        upto = upto + jnp.where(lane >= s, pltpu.roll(upto, s, 1), 0)
    slot = jnp.where(hits > 0, upto - 1, -1)
    code = lane + KB * below
    packed = jnp.full(shape, -KB * 1024, I32)
    for b in range(KB):
        at = jnp.broadcast_to(slot[:, b : b + 1], shape) == lane
        packed = jnp.where(at, jnp.broadcast_to(code[:, b : b + 1], shape), packed)
    number = jnp.broadcast_to(upto[:, KB - 1 : KB], shape)
    return jnp.where(lane == KB, number, packed)


def spread_kernel(
    target, q, k, v, ks, vs, pattern,
    q_all, keys, values, factors, lists,
    held0, held1, held2, held3, packed, came0, came1, came2, came3,
    v_land, scales, k_loc, v_loc, listed, goes,
    z_send, z_recv, q_send, q_recv, y_send, y_recv, k_send, k_recv, v_send, v_recv, s_send, s_recv,
    kc_send, kc_recv, vc_send, vc_recv, own,
):
    rep, z, c, x, y = place()
    sib = (rep + 1 - 2 * c, x * NY + y)
    xs = [(x + d) % NX for d in range(NX)]
    back = [(x + NX - d) % NX for d in range(NX)]
    at_x = [(rep, xs[d] * NY + y) for d in range(NX)]
    at_y = [(rep, x * NY + (y + d) % NY) for d in range(NY)]
    half = pl.ds(pl.multiple_of(c * (KEYS // 2), KEYS // 2), KEYS // 2)
    groups = [((z + d) % NZ) * 2 + (c + e) % 2 for d in range(NZ) for e in range(2)]
    at_group = [(g, x * NY + y) for g in groups]
    held = (held0, held1, held2, held3)
    came = (came0, came1, came2, came3)

    def cols(d, n):
        return pl.ds(pl.multiple_of(xs[d] * n, n), n)

    partners = at_group[1:] + at_x[1:] + at_y[1:]
    barrier = pltpu.get_barrier_semaphore()
    for who in partners:
        pl.semaphore_signal(barrier, inc=1, device_id=who, device_id_type=MESH)
    stay = [
        pltpu.make_async_copy(target, goes, own.at[0]),
        pltpu.make_async_copy(q.at[:, :, cols(0, SLICE)], held[0], own.at[1]),
        pltpu.make_async_copy(ks, k_loc, own.at[2]),
        pltpu.make_async_copy(vs, v_loc, own.at[3]),
        pltpu.make_async_copy(pattern.at[pl.ds(x * HEADS, HEADS)], listed, own.at[4]),
        pltpu.make_async_copy(k.at[:, cols(0, D)], keys.at[x], own.at[5]),
        pltpu.make_async_copy(v.at[:, cols(0, D)], v_land.at[0], own.at[6]),
    ]
    for copy in stay:
        copy.start()

    qx, kx, vx, sx, kc, vc = ([None] * NX for _ in range(6))
    qy = [[None] * NY for _ in range(NX)]
    qz = [[None] * len(groups) for _ in range(NX)]

    stay[0].wait()
    goes_to = [goes[rep * QB + b] for b in range(QB)]
    leaving = []
    for group in groups:
        b = jnp.int32(0)
        for other in range(1, QB):
            b = jnp.where(goes_to[other] == group, other, b)
        leaving.append(b)

    def pack(d):
        for n in ORDER:
            block = held[d][leaving[n]]
            if n == 0:
                came[d][n] = block
            else:
                packed[d, n] = block

    def over_z(d):
        for n in ORDER[:-1]:
            qz[d][n] = remote(packed.at[d, n], came[d].at[n], z_send.at[d, n], z_recv.at[d, n], at_group[n])
            qz[d][n].start()

    stay[1].wait()
    pack(0)
    scales[0] = jnp.zeros((2 * NX, 128), F32)
    stay[2].wait()
    stay[3].wait()
    scales[0, 0:NX, 0:SHARD] = k_loc[...]
    scales[0, NX : 2 * NX, 0:SHARD] = v_loc[...]

    pl.semaphore_wait(barrier, len(partners))
    for d in FAR:
        qx[d] = remote(q.at[:, :, cols(d, SLICE)], held[d], q_send.at[d], q_recv.at[d], at_x[d])
        qx[d].start()
    over_z(0)
    for d in FAR:
        sx[d] = remote(scales.at[0], scales.at[d], s_send.at[d], s_recv.at[d], at_x[d])
        sx[d].start()
    for d in FAR:
        kx[d] = remote(k.at[half, cols(d, D)], keys.at[x, half], k_send.at[d], k_recv.at[d], at_x[d])
        vx[d] = remote(v.at[half, cols(d, D)], v_land.at[d, half], v_send.at[d], v_recv.at[d], at_x[d])
        kx[d].start()
        vx[d].start()

    def look(j, state):
        found, *at = state
        hit = goes[j] == rep
        at = [jnp.where(hit & (found == s), j, a) for s, a in enumerate(at)]
        return (found + hit.astype(I32), *at)

    _, *blocks = lax.fori_loop(0, 2 * NZ * QB, look, (jnp.int32(0),) * (1 + QB))

    for d in FAR:
        qx[d].wait_recv()
        pack(d)
        over_z(d)

    stay[4].wait()
    lists[...] = block_lists(listed, blocks, y)

    scale_row = iota((2 * NX, 128), 0)

    def pick_row(tile, n):
        return jnp.sum(jnp.where(scale_row == n, tile, 0.0), axis=0, keepdims=True)

    def finish(d):
        tile = scales[d]
        for_keys = pick_row(tile, x) * TO_LOG2
        for_values = pick_row(tile, NX + x)
        for b in range(SHARD):
            at = back[d] * SHARD + b
            factors[at] = jnp.broadcast_to(for_keys[:, b : b + 1], (8, 128))
            rows = slice(b * B, (b + 1) * B)
            scaled = v_land[d, rows].astype(F32) * jnp.broadcast_to(for_values[:, b : b + 1], (B, D))
            values[at] = scaled.astype(BF16).T

    def hand_over(d):
        kx[d].wait_recv()
        piece = keys.at[back[d], half]
        kc[d] = remote(piece, piece, kc_send.at[d], kc_recv.at[d], sib)
        kc[d].start()
        vx[d].wait_recv()
        vc[d] = remote(v_land.at[d, half], v_land.at[d, half], vc_send.at[d], vc_recv.at[d], sib)
        vc[d].start()
        sx[d].wait_recv()

    def whole(d):
        kc[d].wait_recv()
        vc[d].wait_recv()
        finish(d)

    def over_y(d):
        for n in range(1, len(groups)):
            qz[d][n].wait_recv()
        for s in range(QB):
            source = blocks[s] >> 2
            n = (((z + NZ - (source >> 1)) & (NZ - 1)) << 1) + ((source & 1) ^ c)
            q_all[y, back[d], s] = came[d][n]
        for e in FAR:
            piece = q_all.at[y, back[d]]
            qy[d][e] = remote(piece, piece, y_send.at[d, e], y_recv.at[d, e], at_y[e])
            qy[d][e].start()

    for copy in stay[5:]:
        copy.wait()
    finish(0)
    hand_over(1)
    hand_over(3)
    over_y(0)
    whole(1)
    whole(3)
    over_y(1)
    hand_over(2)
    whole(2)
    over_y(3)
    over_y(2)
    for d in range(NX):
        for e in FAR:
            qy[d][e].wait_recv()
            qy[d][e].wait_send()
    for d in FAR:
        for copy in (qx[d], kx[d], vx[d], sx[d], kc[d], vc[d]):
            copy.wait_send()
    for copies in qz:
        for copy in copies[1:]:
            copy.wait_send()


def spread(target, q, k, v, ks, vs, pattern):
    slots = pltpu.VMEM((2 * NZ, ROWS, SLICE), BF16)
    return pl.pallas_call(
        spread_kernel,
        out_shape=[
            jax.ShapeDtypeStruct((NY, NX, QB, ROWS, SLICE), BF16),
            jax.ShapeDtypeStruct((NX, KEYS, D), BF16),
            jax.ShapeDtypeStruct((KB, D, B), BF16),
            jax.ShapeDtypeStruct((KB, 8, 128), F32),
            jax.ShapeDtypeStruct((PAIRS, 128), I32),
        ],
        in_specs=[HBM] * 7,
        out_specs=[VMEM] * 5,
        scratch_shapes=[pltpu.VMEM((QB, ROWS, SLICE), BF16)] * NX
        + [pltpu.VMEM((NX, 2 * NZ, ROWS, SLICE), BF16)]
        + [slots] * NX
        + [
            pltpu.VMEM((NX, KEYS, D), BF16),
            pltpu.VMEM((NX, 2 * NX, 128), F32),
            pltpu.VMEM((NX, SHARD), F32),
            pltpu.VMEM((NX, SHARD), F32),
            pltpu.VMEM((HEADS, *pattern.shape[1:]), I32),
            pltpu.SMEM(target.shape, I32),
        ]
        + [DMA((NX, 2 * NZ))] * 2
        + [DMA((NX,))] * 2
        + [DMA((NX, NY))] * 2
        + [DMA((NX,))] * 10
        + [DMA((7,))],
        compiler_params=pltpu.CompilerParams(
            collective_id=0, has_side_effects=True, vmem_limit_bytes=24 << 20
        ),
        name="spread",
    )(target, q, k, v, ks, vs, pattern)


def attend_kernel(ints, q_ref, keys, values, factors, out, extra_out, qs, sc, mx, acc, su, extra, items):
    row = iota((B, B), 1)
    row = ((row >> 3) & 3) * PART + (row >> 5) * ROWS + (row & 7)
    ahead = iota((B, B), 0) - row
    extra[...] = jnp.zeros((B, B), F32)
    qs[HEADS] = jnp.zeros((D, B), BF16)

    def tall(tile):
        return jnp.broadcast_to(tile[None], (B // 8, 8, B)).reshape(B, B)

    @pl.loop(0, QB // TOGETHER)
    def _(part_of):
        def add_pair(r, n):
            def add(t, n):
                items[n] = r * 16 + t
                return n + 1

            return lax.fori_loop(0, (ints[part_of * LANES + r, KB] + 1) // 2, add, n)

        n = lax.fori_loop(0, LANES, add_pair, jnp.int32(0))
        for g in range(STEP):
            items[n + g] = HEADS * 16
        count = (n + STEP - 1) // STEP
        for j in range(TOGETHER):
            rows = q_ref[:, :, part_of * TOGETHER + j].astype(F32).reshape(B, SLICE).astype(BF16)
            for h in range(HEADS):
                qs[j * 8 + h] = rows[:, h * D : (h + 1) * D].T
        mx[...] = jnp.full(mx.shape, NEG, F32)
        acc[...] = jnp.zeros(acc.shape, F32)
        su[...] = jnp.zeros(su.shape, F32)

        def item_at(i, g):
            item = items[i * STEP + g]
            r, t = item >> 4, item & 15
            codes = [ints[part_of * LANES + r, t * 2 + u] for u in range(2)]
            return r, codes, [code & (KB - 1) for code in codes]

        @pl.loop(0, count)
        def _(i):
            for g in range(STEP):
                r, codes, kbs = item_at(i, g)
                both = jnp.dot(
                    jnp.concatenate([keys[kb] for kb in kbs], axis=0), qs[r], preferred_element_type=F32
                )
                top = mx[r]
                for u in range(2):
                    score = both[u * B : (u + 1) * B] * tall(factors[kbs[u]])
                    score = jnp.where(ahead <= (codes[u] >> 5) * B, score, NEG)
                    sc[(i * STEP + g) * 2 + u] = score
                    top = jnp.maximum(top, jnp.max(score.reshape(B // 8, 8, B), axis=0))
                mx[r] = top

        for j in range(TOGETHER):
            for h in range(HEADS):
                top = jnp.max(mx[j * 8 + h], axis=0, keepdims=True)
                mx[j * 8 + h] = jnp.broadcast_to(top, (8, B)).astype(BF16).astype(F32)

        @pl.loop(0, count)
        def _(i):
            for g in range(STEP):
                r, codes, kbs = item_at(i, g)
                top = tall(mx[r])
                weights = [jnp.exp2(sc[(i * STEP + g) * 2 + u] - top) for u in range(2)]
                su[r] += jnp.sum((weights[0] + weights[1]).reshape(B // 8, 8, B), axis=0)
                acc[r] += jnp.dot(
                    jnp.concatenate([values[kb] for kb in kbs], axis=1),
                    jnp.concatenate([w.astype(BF16) for w in weights], axis=0),
                    preferred_element_type=F32,
                )

        for j in range(TOGETHER):
            for h in range(HEADS):
                r = j * 8 + h
                at = part_of * LANES + r
                extra[pl.ds(at, 1), :] = mx[r][0:1]
                extra[pl.ds(SUM_LANE + at, 1), :] = jnp.sum(su[r], axis=0, keepdims=True)
                part = acc[r].astype(BF16).T
                for d in range(NY):
                    out[d, part_of * TOGETHER + j, :, h * D : (h + 1) * D] = part[d * PART : (d + 1) * PART]

    turned = extra[...].T
    for d in range(NY):
        extra_out[d] = turned[d * PART : (d + 1) * PART].astype(BF16)


def attend(lists, q_all, keys, values, factors):
    most = TOGETHER * HEADS * KB // 2 + STEP
    return pl.pallas_call(
        attend_kernel,
        out_shape=[
            jax.ShapeDtypeStruct((NY, QB, PART, SLICE), BF16),
            jax.ShapeDtypeStruct((NY, PART, 128), BF16),
        ],
        in_specs=[SMEM] + [VMEM] * 4,
        out_specs=[VMEM] * 2,
        scratch_shapes=[
            pltpu.VMEM((LANES, D, B), BF16),
            pltpu.VMEM((2 * most, B, B), F32),
            pltpu.VMEM((LANES, 8, B), F32),
            pltpu.VMEM((LANES, D, B), F32),
            pltpu.VMEM((LANES, 8, B), F32),
            pltpu.VMEM((B, B), F32),
            pltpu.SMEM((most,), I32),
        ],
        compiler_params=pltpu.CompilerParams(vmem_limit_bytes=46 << 20),
        name="attend",
    )(lists, q_all, keys.reshape(KB, B, D), values, factors)


def gather_kernel(
    p, extra_in, out, parts, extra, att, e_send, e_recv, y_send, y_recv, x_send, x_recv, own
):
    rep, z, c, x, y = place()
    xs = [(x + d) % NX for d in range(NX)]
    ys = [(y + d) % NY for d in range(NY)]
    at_x = [(rep, xs[d] * NY + y) for d in range(NX)]
    at_y = [(rep, x * NY + ys[d]) for d in range(NY)]
    greet(at_x[1:] + at_y[1:])

    ex = [None] * NY
    py = [[None] * NY for _ in range(QB)]
    px = [[None] * NX for _ in range(QB)]
    for d in FAR:
        ex[d] = remote(extra_in.at[ys[d]], extra.at[d], e_send.at[d], e_recv.at[d], at_y[d])
        ex[d].start()
    for b in range(QB):
        for d in FAR:
            py[b][d] = remote(p.at[ys[d], b], parts.at[d, b], y_send.at[b, d], y_recv.at[b, d], at_y[d])
            py[b][d].start()
    for d in FAR:
        ex[d].wait_recv()
    marks = [extra_in[y].astype(F32)] + [extra[d].astype(F32) for d in range(1, NY)]
    top = functools.reduce(jnp.maximum, marks)
    shift = [jnp.exp2(e - top) for e in marks]
    total = sum(w * pltpu.roll(e, SUM_LANE, 1) for w, e in zip(shift, marks))
    lane = iota((PART, 128), 1)
    total = jnp.where((lane < QB * 8) & ((lane & 7) < HEADS), total, 1.0)
    ratio = [w / total for w in shift]
    mine = pl.ds(pl.multiple_of(x * SLICE, SLICE), SLICE)

    for b in range(QB):
        for d in FAR:
            py[b][d].wait_recv()
        for h in range(HEADS):
            cols = slice(h * D, (h + 1) * D)
            at = b * 8 + h
            value = sum(
                jnp.broadcast_to(ratio[d][:, at : at + 1], (PART, D))
                * (parts[d, b, :, cols] if d else p[y, b, :, cols]).astype(F32)
                for d in range(NY)
            )
            value = value.reshape(NX, ROWS, D).astype(BF16)
            for d in range(NX):
                att[b, d, :, cols] = value[d]
        for d in FAR:
            px[b][d] = remote(
                att.at[b, xs[d]], out.at[b, :, mine], x_send.at[b, d], x_recv.at[b, d], at_x[d]
            )
            px[b][d].start()
        px[b][0] = pltpu.make_async_copy(att.at[b, x], out.at[b, :, mine], own.at[b])
        px[b][0].start()

    for d in FAR:
        ex[d].wait_send()
    for b in range(QB):
        px[b][0].wait()
        for d in FAR:
            px[b][d].wait_recv()
            px[b][d].wait_send()
            py[b][d].wait_send()


def gather(p, extra):
    return pl.pallas_call(
        gather_kernel,
        out_shape=jax.ShapeDtypeStruct((QB, ROWS, NX * SLICE), BF16),
        in_specs=[VMEM, VMEM],
        out_specs=VMEM,
        scratch_shapes=[
            pltpu.VMEM((NY, QB, PART, SLICE), BF16),
            pltpu.VMEM((NY, PART, 128), BF16),
            pltpu.VMEM((QB, NX, ROWS, SLICE), BF16),
        ]
        + [DMA((NY,))] * 2
        + [DMA((QB, NY))] * 2
        + [DMA((QB, NX))] * 2
        + [DMA((QB,))],
        compiler_params=pltpu.CompilerParams(
            collective_id=1, has_side_effects=True, vmem_limit_bytes=16 << 20
        ),
        name="gather",
    )(p, extra)


def hbm(array):
    return pltpu.with_memory_space_constraint(array, pltpu.HBM)


def per_device(queries, key_cache, value_cache, key_scale, value_scale, pattern, target):
    q_all, keys, values, factors, lists = spread(
        hbm(target),
        hbm(queries),
        hbm(key_cache),
        hbm(value_cache),
        hbm(key_scale.T),
        hbm(value_scale.T),
        hbm(jnp.swapaxes(pattern, 1, 2)),
    )
    part, extra = attend(lists, q_all, keys, values, factors)
    return gather(part, extra)


def solution(mesh):
    return jax.shard_map(
        per_device,
        mesh=mesh,
        in_specs=(
            P("replica", "ctx", None),
            P("ctx", None),
            P("ctx", None),
            P("ctx", None),
            P("ctx", None),
            P(),
            P(),
        ),
        out_specs=P("replica", "ctx", None),
        check_vma=False,
    )
```

```python
import functools
import math

import jax
import jax.numpy as jnp
from jax import lax
from jax.experimental import pallas as pl
from jax.experimental.pallas import tpu as pltpu
from jax.sharding import PartitionSpec as P

MESH = pl.DeviceIdType.MESH
BF16 = jnp.bfloat16
F32 = jnp.float32
I32 = jnp.int32

NX = 4
NY = 4
NZ = 8
HEADS = 7
D = 128
B = 128
QB = 4
KB = 32
SHARD = 8
SLICE = HEADS * D
EARLY = 5
FORE = EARLY * D
REST = SLICE - FORE
ROWS = B // (NX * NY)
PART = NX * ROWS
KEYS = SHARD * B
PAIRS = 32
SUM_LANE = 64
NEG = -(2.0**100)
STEP = 24
TOGETHER = 2
LANES = 8 * TOGETHER
FIRST = 64
FAR = (1, 3, 2)
ORDER = (8, 9, 6, 7, 10, 11, 4, 5, 12, 13, 2, 3, 14, 15, 1, 0)
TO_LOG2 = math.log2(math.e) / math.sqrt(D)

DMA = pltpu.SemaphoreType.DMA
HBM = pl.BlockSpec(memory_space=pltpu.HBM)
VMEM = pl.BlockSpec(memory_space=pltpu.VMEM)
SMEM = pl.BlockSpec(memory_space=pltpu.SMEM)


def place():
    rep = lax.axis_index("replica")
    ctx = lax.axis_index("ctx")
    return rep, rep // 2, rep % 2, ctx // NY, ctx % NY


def remote(src, dst, send, recv, who):
    return pltpu.make_async_remote_copy(
        src_ref=src, dst_ref=dst, send_sem=send, recv_sem=recv, device_id=who, device_id_type=MESH
    )


def iota(shape, dim):
    return lax.broadcasted_iota(I32, shape, dim)


def block_lists(listed, blocks, rep, y):
    shape = (PAIRS, 128)
    lane, row = iota(shape, 1), iota(shape, 0)
    block = (lane >> 3) * (SHARD * NY) + y * SHARD + (lane & 7)
    hits = jnp.zeros(shape, I32)
    own = jnp.zeros(shape, I32)
    column = iota(listed.shape[1:], 1)
    for s in range(QB):
        own = jnp.where(row >> 3 == s, jnp.where((row & 7) < EARLY, blocks[s], rep * QB + s), own)
        for h in range(HEADS):
            of = blocks[s] if h < EARLY else rep * QB + s
            entry = jnp.max(jnp.where(column == of, listed[h], -1), axis=1, keepdims=True)
            found = (jnp.broadcast_to(entry, shape) == block).astype(I32)
            found = jnp.max(found, axis=0, keepdims=True)
            hits = jnp.where(row == s * 8 + h, found, hits)
    below = FIRST + own - block
    hits = jnp.where(below == 0, 1, hits)
    hits = jnp.where((below >= 0) & (lane < KB) & ((row & 7) < HEADS), hits, 0)
    upto = hits
    for s in (1, 2, 4, 8, 16):
        upto = upto + jnp.where(lane >= s, pltpu.roll(upto, s, 1), 0)
    slot = jnp.where(hits > 0, upto - 1, -1)
    code = lane + KB * below
    packed = jnp.full(shape, -KB * 1024, I32)
    for b in range(KB):
        at = jnp.broadcast_to(slot[:, b : b + 1], shape) == lane
        packed = jnp.where(at, jnp.broadcast_to(code[:, b : b + 1], shape), packed)
    number = jnp.broadcast_to(upto[:, KB - 1 : KB], shape)
    return jnp.where(lane == KB, number, packed)


def near_groups(z, c):
    return [((z + d) % NZ) * 2 + (c + e) % 2 for d in range(NZ) for e in range(2)]


def slot_of(block, z, c):
    source = block >> 2
    return (((z + NZ - (source >> 1)) & (NZ - 1)) << 1) + ((source & 1) ^ c)


def routes(goes, rep, groups):
    goes_to = [goes[rep * QB + b] for b in range(QB)]
    leaving = []
    for group in groups:
        b = jnp.int32(0)
        for other in range(1, QB):
            b = jnp.where(goes_to[other] == group, other, b)
        leaving.append(b)

    def look(j, state):
        found, *at = state
        hit = goes[j] == rep
        at = [jnp.where(hit & (found == s), j, a) for s, a in enumerate(at)]
        return (found + hit.astype(I32), *at)

    _, *blocks = lax.fori_loop(0, 2 * NZ * QB, look, (jnp.int32(0),) * (1 + QB))
    return leaving, blocks


def spread_kernel(
    target, q, k, v, ks, vs, pattern,
    q_fore, q_rest, keys, values, factors, lists,
    held0, held1, held2, held3, packed, came0, came1, came2, came3,
    v_land, scales, k_loc, v_loc, listed, goes,
    z_send, z_recv, q_send, q_recv, r_send, r_recv, y_send, y_recv, t_send, t_recv, k_send, k_recv, v_send, v_recv, s_send, s_recv,
    kc_send, kc_recv, vc_send, vc_recv, own,
):
    rep, z, c, x, y = place()
    sib = (rep + 1 - 2 * c, x * NY + y)
    xs = [(x + d) % NX for d in range(NX)]
    back = [(x + NX - d) % NX for d in range(NX)]
    at_x = [(rep, xs[d] * NY + y) for d in range(NX)]
    at_y = [(rep, x * NY + (y + d) % NY) for d in range(NY)]
    half = pl.ds(pl.multiple_of(c * (KEYS // 2), KEYS // 2), KEYS // 2)
    groups = near_groups(z, c)
    at_group = [(g, x * NY + y) for g in groups]
    held = (held0, held1, held2, held3)
    came = (came0, came1, came2, came3)

    def cols(d, n):
        return pl.ds(pl.multiple_of(xs[d] * n, n), n)

    def fore(d):
        return q.at[:, :, pl.ds(pl.multiple_of(xs[d] * SLICE, D), FORE)]

    def rest(d):
        return q.at[:, :, pl.ds(pl.multiple_of(xs[d] * SLICE + FORE, D), REST)]

    partners = at_group[1:] + at_x[1:] + at_y[1:]
    barrier = pltpu.get_barrier_semaphore()
    for who in partners:
        pl.semaphore_signal(barrier, inc=1, device_id=who, device_id_type=MESH)
    stay = [
        pltpu.make_async_copy(target, goes, own.at[0]),
        pltpu.make_async_copy(fore(0), held[0], own.at[1]),
        pltpu.make_async_copy(ks, k_loc, own.at[2]),
        pltpu.make_async_copy(vs, v_loc, own.at[3]),
        pltpu.make_async_copy(pattern.at[pl.ds(x * HEADS, HEADS)], listed, own.at[4]),
        pltpu.make_async_copy(k.at[:, cols(0, D)], keys.at[x], own.at[5]),
        pltpu.make_async_copy(v.at[:, cols(0, D)], v_land.at[0], own.at[6]),
        pltpu.make_async_copy(rest(0), q_rest.at[y, x], own.at[7]),
    ]
    for copy in stay:
        copy.start()

    qx, rx, kx, vx, sx, kc, vc = ([None] * NX for _ in range(7))
    qy, ry = ([[None] * NY for _ in range(NX)] for _ in range(2))
    qz = [[None] * len(groups) for _ in range(NX)]

    stay[0].wait()
    leaving, blocks = routes(goes, rep, groups)

    def pack(d):
        for n in ORDER:
            block = held[d][leaving[n]]
            if n == 0:
                came[d][n] = block
            else:
                packed[d, n] = block

    def over_z(d):
        for n in ORDER[:-1]:
            qz[d][n] = remote(packed.at[d, n], came[d].at[n], z_send.at[d, n], z_recv.at[d, n], at_group[n])
            qz[d][n].start()

    stay[1].wait()
    pack(0)
    scales[0] = jnp.zeros((2 * NX, 128), F32)
    stay[2].wait()
    stay[3].wait()
    scales[0, 0:NX, 0:SHARD] = k_loc[...]
    scales[0, NX : 2 * NX, 0:SHARD] = v_loc[...]

    pl.semaphore_wait(barrier, len(partners))
    for d in FAR:
        qx[d] = remote(fore(d), held[d], q_send.at[d], q_recv.at[d], at_x[d])
        qx[d].start()
    over_z(0)
    for d in FAR:
        rx[d] = remote(rest(d), q_rest.at[y, x], r_send.at[d], r_recv.at[d], at_x[d])
        rx[d].start()
    for d in FAR:
        sx[d] = remote(scales.at[0], scales.at[d], s_send.at[d], s_recv.at[d], at_x[d])
        sx[d].start()
    for d in FAR:
        kx[d] = remote(k.at[half, cols(d, D)], keys.at[x, half], k_send.at[d], k_recv.at[d], at_x[d])
        vx[d] = remote(v.at[half, cols(d, D)], v_land.at[d, half], v_send.at[d], v_recv.at[d], at_x[d])
        kx[d].start()
        vx[d].start()

    for d in FAR:
        qx[d].wait_recv()
        pack(d)
        over_z(d)

    stay[4].wait()
    lists[...] = block_lists(listed, blocks, rep, y)

    scale_row = iota((2 * NX, 128), 0)

    def pick_row(tile, n):
        return jnp.sum(jnp.where(scale_row == n, tile, 0.0), axis=0, keepdims=True)

    def finish(d):
        tile = scales[d]
        for_keys = pick_row(tile, x) * TO_LOG2
        for_values = pick_row(tile, NX + x)
        for b in range(SHARD):
            at = back[d] * SHARD + b
            factors[at] = jnp.broadcast_to(for_keys[:, b : b + 1], (8, 128))
            rows = slice(b * B, (b + 1) * B)
            scaled = v_land[d, rows].astype(F32) * jnp.broadcast_to(for_values[:, b : b + 1], (B, D))
            values[at] = scaled.astype(BF16).T

    def hand_over(d):
        kx[d].wait_recv()
        piece = keys.at[back[d], half]
        kc[d] = remote(piece, piece, kc_send.at[d], kc_recv.at[d], sib)
        kc[d].start()
        vx[d].wait_recv()
        vc[d] = remote(v_land.at[d, half], v_land.at[d, half], vc_send.at[d], vc_recv.at[d], sib)
        vc[d].start()
        sx[d].wait_recv()

    def whole(d):
        kc[d].wait_recv()
        vc[d].wait_recv()
        finish(d)

    def over_y(d):
        for n in range(1, len(groups)):
            qz[d][n].wait_recv()
        for s in range(QB):
            q_fore[y, back[d], s] = came[d][slot_of(blocks[s], z, c)]
        for e in FAR:
            piece = q_fore.at[y, back[d]]
            qy[d][e] = remote(piece, piece, y_send.at[d, e], y_recv.at[d, e], at_y[e])
            qy[d][e].start()

    stay[7].wait()
    for d in (0, *FAR):
        if d:
            rx[d].wait_recv()
        for e in FAR:
            piece = q_rest.at[y, back[d]]
            ry[d][e] = remote(piece, piece, t_send.at[d, e], t_recv.at[d, e], at_y[e])
            ry[d][e].start()
    for copy in stay[5:7]:
        copy.wait()
    finish(0)
    hand_over(1)
    hand_over(3)
    over_y(0)
    whole(1)
    whole(3)
    over_y(1)
    hand_over(2)
    whole(2)
    over_y(3)
    over_y(2)
    for d in range(NX):
        for e in FAR:
            for copy in (qy[d][e], ry[d][e]):
                copy.wait_recv()
                copy.wait_send()
    for d in FAR:
        for copy in (qx[d], rx[d], kx[d], vx[d], sx[d], kc[d], vc[d]):
            copy.wait_send()
    for copies in qz:
        for copy in copies[1:]:
            copy.wait_send()


def spread(target, q, k, v, ks, vs, pattern):
    slots = pltpu.VMEM((2 * NZ, ROWS, FORE), BF16)
    return pl.pallas_call(
        spread_kernel,
        out_shape=[
            jax.ShapeDtypeStruct((NY, NX, QB, ROWS, FORE), BF16),
            jax.ShapeDtypeStruct((NY, NX, QB, ROWS, REST), BF16),
            jax.ShapeDtypeStruct((NX, KEYS, D), BF16),
            jax.ShapeDtypeStruct((KB, D, B), BF16),
            jax.ShapeDtypeStruct((KB, 8, 128), F32),
            jax.ShapeDtypeStruct((PAIRS, 128), I32),
        ],
        in_specs=[HBM] * 7,
        out_specs=[VMEM] * 6,
        scratch_shapes=[pltpu.VMEM((QB, ROWS, FORE), BF16)] * NX
        + [pltpu.VMEM((NX, 2 * NZ, ROWS, FORE), BF16)]
        + [slots] * NX
        + [
            pltpu.VMEM((NX, KEYS, D), BF16),
            pltpu.VMEM((NX, 2 * NX, 128), F32),
            pltpu.VMEM((NX, SHARD), F32),
            pltpu.VMEM((NX, SHARD), F32),
            pltpu.VMEM((HEADS, *pattern.shape[1:]), I32),
            pltpu.SMEM(target.shape, I32),
        ]
        + [DMA((NX, 2 * NZ))] * 2
        + [DMA((NX,))] * 4
        + [DMA((NX, NY))] * 4
        + [DMA((NX,))] * 10
        + [DMA((8,))],
        compiler_params=pltpu.CompilerParams(
            collective_id=0, has_side_effects=True, vmem_limit_bytes=24 << 20
        ),
        name="spread",
    )(target, q, k, v, ks, vs, pattern)


def attend_kernel(
    ints, q_fore, q_rest, keys, values, factors, out_fore, out_rest, extra_out,
    qs, sc, mx, acc, su, extra, items,
):
    row = iota((B, B), 1)
    row = ((row >> 3) & 3) * PART + (row >> 5) * ROWS + (row & 7)
    ahead = iota((B, B), 0) - row
    extra[...] = jnp.zeros((B, B), F32)
    qs[HEADS] = jnp.zeros((D, B), BF16)

    def tall(tile):
        return jnp.broadcast_to(tile[None], (B // 8, 8, B)).reshape(B, B)

    @pl.loop(0, QB // TOGETHER)
    def _(part_of):
        def add_pair(r, n):
            def add(t, n):
                items[n] = r * 16 + t
                return n + 1

            return lax.fori_loop(0, (ints[part_of * LANES + r, KB] + 1) // 2, add, n)

        n = lax.fori_loop(0, LANES, add_pair, jnp.int32(0))
        for g in range(STEP):
            items[n + g] = HEADS * 16
        count = (n + STEP - 1) // STEP
        for j in range(TOGETHER):
            for q_ref, low, high in ((q_fore, 0, EARLY), (q_rest, EARLY, HEADS)):
                rows = q_ref[:, :, part_of * TOGETHER + j].astype(F32).reshape(B, (high - low) * D)
                rows = rows.astype(BF16)
                for h in range(low, high):
                    qs[j * 8 + h] = rows[:, (h - low) * D : (h - low + 1) * D].T
        mx[...] = jnp.full(mx.shape, NEG, F32)
        acc[...] = jnp.zeros(acc.shape, F32)
        su[...] = jnp.zeros(su.shape, F32)

        def item_at(i, g):
            item = items[i * STEP + g]
            r, t = item >> 4, item & 15
            codes = [ints[part_of * LANES + r, t * 2 + u] for u in range(2)]
            return r, codes, [code & (KB - 1) for code in codes]

        @pl.loop(0, count)
        def _(i):
            for g in range(STEP):
                r, codes, kbs = item_at(i, g)
                both = jnp.dot(
                    jnp.concatenate([keys[kb] for kb in kbs], axis=0), qs[r], preferred_element_type=F32
                )
                top = mx[r]
                for u in range(2):
                    score = both[u * B : (u + 1) * B] * tall(factors[kbs[u]])
                    score = jnp.where(ahead <= (codes[u] >> 5) * B, score, NEG)
                    sc[(i * STEP + g) * 2 + u] = score
                    top = jnp.maximum(top, jnp.max(score.reshape(B // 8, 8, B), axis=0))
                mx[r] = top

        for j in range(TOGETHER):
            for h in range(HEADS):
                top = jnp.max(mx[j * 8 + h], axis=0, keepdims=True)
                mx[j * 8 + h] = jnp.broadcast_to(top, (8, B)).astype(BF16).astype(F32)

        @pl.loop(0, count)
        def _(i):
            for g in range(STEP):
                r, codes, kbs = item_at(i, g)
                top = tall(mx[r])
                weights = [jnp.exp2(sc[(i * STEP + g) * 2 + u] - top) for u in range(2)]
                su[r] += jnp.sum((weights[0] + weights[1]).reshape(B // 8, 8, B), axis=0)
                acc[r] += jnp.dot(
                    jnp.concatenate([values[kb] for kb in kbs], axis=1),
                    jnp.concatenate([w.astype(BF16) for w in weights], axis=0),
                    preferred_element_type=F32,
                )

        for j in range(TOGETHER):
            for h in range(HEADS):
                r = j * 8 + h
                at = part_of * LANES + r
                extra[pl.ds(at, 1), :] = mx[r][0:1]
                extra[pl.ds(SUM_LANE + at, 1), :] = jnp.sum(su[r], axis=0, keepdims=True)
                part = acc[r].astype(BF16).T
                out, i = (out_fore, h) if h < EARLY else (out_rest, h - EARLY)
                for d in range(NY):
                    out[d, part_of * TOGETHER + j, :, i * D : (i + 1) * D] = part[d * PART : (d + 1) * PART]

    turned = extra[...].T
    for d in range(NY):
        extra_out[d] = turned[d * PART : (d + 1) * PART].astype(BF16)


def attend(lists, q_fore, q_rest, keys, values, factors):
    most = TOGETHER * HEADS * KB // 2 + STEP
    return pl.pallas_call(
        attend_kernel,
        out_shape=[
            jax.ShapeDtypeStruct((NY, QB, PART, FORE), BF16),
            jax.ShapeDtypeStruct((NY, QB, PART, REST), BF16),
            jax.ShapeDtypeStruct((NY, PART, 128), BF16),
        ],
        in_specs=[SMEM] + [VMEM] * 5,
        out_specs=[VMEM] * 3,
        scratch_shapes=[
            pltpu.VMEM((LANES, D, B), BF16),
            pltpu.VMEM((2 * most, B, B), F32),
            pltpu.VMEM((LANES, 8, B), F32),
            pltpu.VMEM((LANES, D, B), F32),
            pltpu.VMEM((LANES, 8, B), F32),
            pltpu.VMEM((B, B), F32),
            pltpu.SMEM((most,), I32),
        ],
        compiler_params=pltpu.CompilerParams(vmem_limit_bytes=46 << 20),
        name="attend",
    )(lists, q_fore, q_rest, keys.reshape(KB, B, D), values, factors)


def gather_kernel(
    target, p, p_rest, extra_in, out,
    parts, parts_rest, extra, att, att_rest, held, packed, came, goes,
    e_send, e_recv, y_send, y_recv, t_send, t_recv, x_send, x_recv, r_send, r_recv, z_send, z_recv, own,
):
    rep, z, c, x, y = place()
    xs = [(x + d) % NX for d in range(NX)]
    back = [(x + NX - d) % NX for d in range(NX)]
    ys = [(y + d) % NY for d in range(NY)]
    at_x = [(rep, xs[d] * NY + y) for d in range(NX)]
    at_y = [(rep, x * NY + ys[d]) for d in range(NY)]
    groups = near_groups(z, c)
    at_group = [(g, x * NY + y) for g in groups]
    partners = at_group[1:] + at_x[1:] + at_y[1:]
    barrier = pltpu.get_barrier_semaphore()
    for who in partners:
        pl.semaphore_signal(barrier, inc=1, device_id=who, device_id_type=MESH)
    told = pltpu.make_async_copy(target, goes, own.at[QB])
    told.start()
    told.wait()
    leaving, blocks = routes(goes, rep, groups)
    pl.semaphore_wait(barrier, len(partners))

    ex, ty, rx = ([None] * NY for _ in range(3))
    py = [[None] * NY for _ in range(QB)]
    px = [[None] * NX for _ in range(QB)]
    pz = [None] * len(groups)
    for d in FAR:
        ex[d] = remote(extra_in.at[ys[d]], extra.at[d], e_send.at[d], e_recv.at[d], at_y[d])
        ex[d].start()
        ty[d] = remote(p_rest.at[ys[d]], parts_rest.at[d], t_send.at[d], t_recv.at[d], at_y[d])
        ty[d].start()
    for b in range(QB):
        for d in FAR:
            py[b][d] = remote(p.at[ys[d], b], parts.at[d, b], y_send.at[b, d], y_recv.at[b, d], at_y[d])
            py[b][d].start()
    for d in FAR:
        ex[d].wait_recv()
    marks = [extra_in[y].astype(F32)] + [extra[d].astype(F32) for d in range(1, NY)]
    top = functools.reduce(jnp.maximum, marks)
    shift = [jnp.exp2(e - top) for e in marks]
    total = sum(w * pltpu.roll(e, SUM_LANE, 1) for w, e in zip(shift, marks))
    lane = iota((PART, 128), 1)
    total = jnp.where((lane < QB * 8) & ((lane & 7) < HEADS), total, 1.0)
    ratio = [w / total for w in shift]

    def quotient(b, h, mine, theirs, cols):
        at = b * 8 + h
        value = sum(
            jnp.broadcast_to(ratio[d][:, at : at + 1], (PART, D))
            * (theirs[d, b, :, cols] if d else mine[y, b, :, cols]).astype(F32)
            for d in range(NY)
        )
        return value.reshape(NX, ROWS, D).astype(BF16)

    for d in FAR:
        ty[d].wait_recv()
    for b in range(QB):
        for h in range(EARLY, HEADS):
            cols = slice((h - EARLY) * D, (h - EARLY + 1) * D)
            value = quotient(b, h, p_rest, parts_rest, cols)
            for d in range(NX):
                att_rest[d, b, :, cols] = value[d]
    for d in FAR:
        rx[d] = remote(att_rest.at[xs[d]], held.at[d], r_send.at[d], r_recv.at[d], at_x[d])
        rx[d].start()
    held[0] = att_rest[x]
    for d in FAR:
        rx[d].wait_recv()
    for n in ORDER:
        for d in range(NX):
            block = held[d, leaving[n]]
            if n == 0:
                came[n, d] = block
            else:
                packed[n, d] = block
        if n > 0:
            pz[n] = remote(packed.at[n], came.at[n], z_send.at[n], z_recv.at[n], at_group[n])
            pz[n].start()

    mine = pl.ds(pl.multiple_of(x * SLICE, D), FORE)
    for b in range(QB):
        for d in FAR:
            py[b][d].wait_recv()
        for h in range(EARLY):
            cols = slice(h * D, (h + 1) * D)
            value = quotient(b, h, p, parts, cols)
            for d in range(NX):
                att[b, d, :, cols] = value[d]
        for d in FAR:
            px[b][d] = remote(
                att.at[b, xs[d]], out.at[b, :, mine], x_send.at[b, d], x_recv.at[b, d], at_x[d]
            )
            px[b][d].start()
        px[b][0] = pltpu.make_async_copy(att.at[b, x], out.at[b, :, mine], own.at[b])
        px[b][0].start()

    for n in range(1, len(groups)):
        pz[n].wait_recv()
    for b in range(QB):
        px[b][0].wait()
        for d in FAR:
            px[b][d].wait_recv()
    for s in range(QB):
        n = slot_of(blocks[s], z, c)
        for d in range(NX):
            out[s, :, pl.ds(pl.multiple_of(back[d] * SLICE + FORE, D), REST)] = came[n, d]

    for n in range(1, len(groups)):
        pz[n].wait_send()
    for d in FAR:
        for copy in (ex[d], ty[d], rx[d]):
            copy.wait_send()
        for b in range(QB):
            px[b][d].wait_send()
            py[b][d].wait_send()


def gather(target, p, p_rest, extra):
    slots = pltpu.VMEM((2 * NZ, NX, ROWS, REST), BF16)
    return pl.pallas_call(
        gather_kernel,
        out_shape=jax.ShapeDtypeStruct((QB, ROWS, NX * SLICE), BF16),
        in_specs=[HBM, VMEM, VMEM, VMEM],
        out_specs=VMEM,
        scratch_shapes=[
            pltpu.VMEM((NY, QB, PART, FORE), BF16),
            pltpu.VMEM((NY, QB, PART, REST), BF16),
            pltpu.VMEM((NY, PART, 128), BF16),
            pltpu.VMEM((QB, NX, ROWS, FORE), BF16),
            pltpu.VMEM((NX, QB, ROWS, REST), BF16),
            pltpu.VMEM((NX, QB, ROWS, REST), BF16),
            slots,
            slots,
            pltpu.SMEM(target.shape, I32),
        ]
        + [DMA((NY,))] * 2
        + [DMA((QB, NY))] * 2
        + [DMA((NY,))] * 2
        + [DMA((QB, NX))] * 2
        + [DMA((NX,))] * 2
        + [DMA((2 * NZ,))] * 2
        + [DMA((QB + 1,))],
        compiler_params=pltpu.CompilerParams(
            collective_id=1, has_side_effects=True, vmem_limit_bytes=16 << 20
        ),
        name="gather",
    )(target, p, p_rest, extra)


def hbm(array):
    return pltpu.with_memory_space_constraint(array, pltpu.HBM)


def per_device(queries, key_cache, value_cache, key_scale, value_scale, pattern, target):
    target = hbm(target)
    q_fore, q_rest, keys, values, factors, lists = spread(
        target,
        hbm(queries),
        hbm(key_cache),
        hbm(value_cache),
        hbm(key_scale.T),
        hbm(value_scale.T),
        hbm(jnp.swapaxes(pattern, 1, 2)),
    )
    part, rest, extra = attend(lists, q_fore, q_rest, keys, values, factors)
    return gather(target, part, rest, extra)


def solution(mesh):
    return jax.shard_map(
        per_device,
        mesh=mesh,
        in_specs=(
            P("replica", "ctx", None),
            P("ctx", None),
            P("ctx", None),
            P("ctx", None),
            P("ctx", None),
            P(),
            P(),
        ),
        out_specs=P("replica", "ctx", None),
        check_vma=False,
    )
```

```python
import functools
import math

import jax
import jax.numpy as jnp
from jax import lax
from jax.experimental import pallas as pl
from jax.experimental.pallas import tpu as pltpu
from jax.sharding import PartitionSpec as P

MESH = pl.DeviceIdType.MESH
BF16 = jnp.bfloat16
F32 = jnp.float32
I32 = jnp.int32

NX = 4
NY = 4
NZ = 8
HEADS = 7
D = 128
B = 128
QB = 4
KB = 32
SHARD = 8
SLICE = HEADS * D
EARLY = 6
FORE = EARLY * D
REST = SLICE - FORE
ROWS = B // (NX * NY)
PART = NX * ROWS
KEYS = SHARD * B
PAIRS = 32
SUM_LANE = 64
NEG = -(2.0**100)
STEP = 24
TOGETHER = 2
LANES = 8 * TOGETHER
FIRST = 64
FAR = (1, 3, 2)
ORDER = (8, 9, 6, 7, 10, 11, 4, 5, 12, 13, 2, 3, 14, 15, 1, 0)
TO_LOG2 = math.log2(math.e) / math.sqrt(D)

DMA = pltpu.SemaphoreType.DMA
HBM = pl.BlockSpec(memory_space=pltpu.HBM)
VMEM = pl.BlockSpec(memory_space=pltpu.VMEM)
SMEM = pl.BlockSpec(memory_space=pltpu.SMEM)


def place():
    rep = lax.axis_index("replica")
    ctx = lax.axis_index("ctx")
    return rep, rep // 2, rep % 2, ctx // NY, ctx % NY


def remote(src, dst, send, recv, who):
    return pltpu.make_async_remote_copy(
        src_ref=src, dst_ref=dst, send_sem=send, recv_sem=recv, device_id=who, device_id_type=MESH
    )


def iota(shape, dim):
    return lax.broadcasted_iota(I32, shape, dim)


def block_lists(listed, blocks, rep, y):
    shape = (PAIRS, 128)
    lane, row = iota(shape, 1), iota(shape, 0)
    block = (lane >> 3) * (SHARD * NY) + y * SHARD + (lane & 7)
    hits = jnp.zeros(shape, I32)
    own = jnp.zeros(shape, I32)
    column = iota(listed.shape[1:], 1)
    for s in range(QB):
        own = jnp.where(row >> 3 == s, jnp.where((row & 7) < EARLY, blocks[s], rep * QB + s), own)
        for h in range(HEADS):
            of = blocks[s] if h < EARLY else rep * QB + s
            entry = jnp.max(jnp.where(column == of, listed[h], -1), axis=1, keepdims=True)
            found = (jnp.broadcast_to(entry, shape) == block).astype(I32)
            found = jnp.max(found, axis=0, keepdims=True)
            hits = jnp.where(row == s * 8 + h, found, hits)
    below = FIRST + own - block
    hits = jnp.where(below == 0, 1, hits)
    hits = jnp.where((below >= 0) & (lane < KB) & ((row & 7) < HEADS), hits, 0)
    upto = hits
    for s in (1, 2, 4, 8, 16):
        upto = upto + jnp.where(lane >= s, pltpu.roll(upto, s, 1), 0)
    slot = jnp.where(hits > 0, upto - 1, -1)
    code = lane + KB * below
    packed = jnp.full(shape, -KB * 1024, I32)
    for b in range(KB):
        at = jnp.broadcast_to(slot[:, b : b + 1], shape) == lane
        packed = jnp.where(at, jnp.broadcast_to(code[:, b : b + 1], shape), packed)
    number = jnp.broadcast_to(upto[:, KB - 1 : KB], shape)
    return jnp.where(lane == KB, number, packed)


def near_groups(z, c):
    return [((z + d) % NZ) * 2 + (c + e) % 2 for d in range(NZ) for e in range(2)]


def slot_of(block, z, c):
    source = block >> 2
    return (((z + NZ - (source >> 1)) & (NZ - 1)) << 1) + ((source & 1) ^ c)


def routes(goes, rep, groups):
    goes_to = [goes[rep * QB + b] for b in range(QB)]
    leaving = []
    for group in groups:
        b = jnp.int32(0)
        for other in range(1, QB):
            b = jnp.where(goes_to[other] == group, other, b)
        leaving.append(b)

    def look(j, state):
        found, *at = state
        hit = goes[j] == rep
        at = [jnp.where(hit & (found == s), j, a) for s, a in enumerate(at)]
        return (found + hit.astype(I32), *at)

    _, *blocks = lax.fori_loop(0, 2 * NZ * QB, look, (jnp.int32(0),) * (1 + QB))
    return leaving, blocks


def spread_kernel(
    target, q, k, v, ks, vs, pattern,
    q_fore, q_rest, keys, values, factors, lists,
    held0, held1, held2, held3, packed, came0, came1, came2, came3,
    v_land, scales, k_loc, v_loc, listed, goes,
    z_send, z_recv, q_send, q_recv, r_send, r_recv, y_send, y_recv, t_send, t_recv, k_send, k_recv, v_send, v_recv, s_send, s_recv,
    kc_send, kc_recv, vc_send, vc_recv, own,
):
    rep, z, c, x, y = place()
    sib = (rep + 1 - 2 * c, x * NY + y)
    xs = [(x + d) % NX for d in range(NX)]
    back = [(x + NX - d) % NX for d in range(NX)]
    at_x = [(rep, xs[d] * NY + y) for d in range(NX)]
    at_y = [(rep, x * NY + (y + d) % NY) for d in range(NY)]
    half = pl.ds(pl.multiple_of(c * (KEYS // 2), KEYS // 2), KEYS // 2)
    groups = near_groups(z, c)
    at_group = [(g, x * NY + y) for g in groups]
    held = (held0, held1, held2, held3)
    came = (came0, came1, came2, came3)

    def cols(d, n):
        return pl.ds(pl.multiple_of(xs[d] * n, n), n)

    def fore(d):
        return q.at[:, :, pl.ds(pl.multiple_of(xs[d] * SLICE, D), FORE)]

    def rest(d):
        return q.at[:, :, pl.ds(pl.multiple_of(xs[d] * SLICE + FORE, D), REST)]

    partners = at_group[1:] + at_x[1:] + at_y[1:]
    barrier = pltpu.get_barrier_semaphore()
    for who in partners:
        pl.semaphore_signal(barrier, inc=1, device_id=who, device_id_type=MESH)
    stay = [
        pltpu.make_async_copy(target, goes, own.at[0]),
        pltpu.make_async_copy(fore(0), held[0], own.at[1]),
        pltpu.make_async_copy(ks, k_loc, own.at[2]),
        pltpu.make_async_copy(vs, v_loc, own.at[3]),
        pltpu.make_async_copy(pattern.at[pl.ds(x * HEADS, HEADS)], listed, own.at[4]),
        pltpu.make_async_copy(k.at[:, cols(0, D)], keys.at[x], own.at[5]),
        pltpu.make_async_copy(v.at[:, cols(0, D)], v_land.at[0], own.at[6]),
        pltpu.make_async_copy(rest(0), q_rest.at[y, x], own.at[7]),
    ]
    for copy in stay:
        copy.start()

    qx, rx, kx, vx, sx, kc, vc = ([None] * NX for _ in range(7))
    qy, ry = ([[None] * NY for _ in range(NX)] for _ in range(2))
    qz = [[None] * len(groups) for _ in range(NX)]

    stay[0].wait()
    leaving, blocks = routes(goes, rep, groups)

    def pack(d):
        for n in ORDER:
            block = held[d][leaving[n]]
            if n == 0:
                came[d][n] = block
            else:
                packed[d, n] = block

    def over_z(d):
        for n in ORDER[:-1]:
            qz[d][n] = remote(packed.at[d, n], came[d].at[n], z_send.at[d, n], z_recv.at[d, n], at_group[n])
            qz[d][n].start()

    stay[1].wait()
    pack(0)
    scales[0] = jnp.zeros((2 * NX, 128), F32)
    stay[2].wait()
    stay[3].wait()
    scales[0, 0:NX, 0:SHARD] = k_loc[...]
    scales[0, NX : 2 * NX, 0:SHARD] = v_loc[...]

    pl.semaphore_wait(barrier, len(partners))
    for d in FAR:
        qx[d] = remote(fore(d), held[d], q_send.at[d], q_recv.at[d], at_x[d])
        qx[d].start()
    over_z(0)
    for d in FAR:
        rx[d] = remote(rest(d), q_rest.at[y, x], r_send.at[d], r_recv.at[d], at_x[d])
        rx[d].start()
    for d in FAR:
        sx[d] = remote(scales.at[0], scales.at[d], s_send.at[d], s_recv.at[d], at_x[d])
        sx[d].start()
    for d in FAR:
        kx[d] = remote(k.at[half, cols(d, D)], keys.at[x, half], k_send.at[d], k_recv.at[d], at_x[d])
        vx[d] = remote(v.at[half, cols(d, D)], v_land.at[d, half], v_send.at[d], v_recv.at[d], at_x[d])
        kx[d].start()
        vx[d].start()

    for d in FAR:
        qx[d].wait_recv()
        pack(d)
        over_z(d)

    stay[4].wait()
    lists[...] = block_lists(listed, blocks, rep, y)

    scale_row = iota((2 * NX, 128), 0)

    def pick_row(tile, n):
        return jnp.sum(jnp.where(scale_row == n, tile, 0.0), axis=0, keepdims=True)

    def finish(d):
        tile = scales[d]
        for_keys = pick_row(tile, x) * TO_LOG2
        for_values = pick_row(tile, NX + x)
        for b in range(SHARD):
            at = back[d] * SHARD + b
            factors[at] = jnp.broadcast_to(for_keys[:, b : b + 1], (8, 128))
            rows = slice(b * B, (b + 1) * B)
            scaled = v_land[d, rows].astype(F32) * jnp.broadcast_to(for_values[:, b : b + 1], (B, D))
            values[at] = scaled.astype(BF16).T

    def hand_over(d):
        kx[d].wait_recv()
        piece = keys.at[back[d], half]
        kc[d] = remote(piece, piece, kc_send.at[d], kc_recv.at[d], sib)
        kc[d].start()
        vx[d].wait_recv()
        vc[d] = remote(v_land.at[d, half], v_land.at[d, half], vc_send.at[d], vc_recv.at[d], sib)
        vc[d].start()
        sx[d].wait_recv()

    def whole(d):
        kc[d].wait_recv()
        vc[d].wait_recv()
        finish(d)

    def over_y(d):
        for n in range(1, len(groups)):
            qz[d][n].wait_recv()
        for s in range(QB):
            q_fore[y, back[d], s] = came[d][slot_of(blocks[s], z, c)]
        for e in FAR:
            piece = q_fore.at[y, back[d]]
            qy[d][e] = remote(piece, piece, y_send.at[d, e], y_recv.at[d, e], at_y[e])
            qy[d][e].start()

    stay[7].wait()
    for d in (0, *FAR):
        if d:
            rx[d].wait_recv()
        for e in FAR:
            piece = q_rest.at[y, back[d]]
            ry[d][e] = remote(piece, piece, t_send.at[d, e], t_recv.at[d, e], at_y[e])
            ry[d][e].start()
    for copy in stay[5:7]:
        copy.wait()
    finish(0)
    hand_over(1)
    hand_over(3)
    over_y(0)
    whole(1)
    whole(3)
    over_y(1)
    hand_over(2)
    whole(2)
    over_y(3)
    over_y(2)
    for d in range(NX):
        for e in FAR:
            for copy in (qy[d][e], ry[d][e]):
                copy.wait_recv()
                copy.wait_send()
    for d in FAR:
        for copy in (qx[d], rx[d], kx[d], vx[d], sx[d], kc[d], vc[d]):
            copy.wait_send()
    for copies in qz:
        for copy in copies[1:]:
            copy.wait_send()


def spread(target, q, k, v, ks, vs, pattern):
    slots = pltpu.VMEM((2 * NZ, ROWS, FORE), BF16)
    return pl.pallas_call(
        spread_kernel,
        out_shape=[
            jax.ShapeDtypeStruct((NY, NX, QB, ROWS, FORE), BF16),
            jax.ShapeDtypeStruct((NY, NX, QB, ROWS, REST), BF16),
            jax.ShapeDtypeStruct((NX, KEYS, D), BF16),
            jax.ShapeDtypeStruct((KB, D, B), BF16),
            jax.ShapeDtypeStruct((KB, 8, 128), F32),
            jax.ShapeDtypeStruct((PAIRS, 128), I32),
        ],
        in_specs=[HBM] * 7,
        out_specs=[VMEM] * 6,
        scratch_shapes=[pltpu.VMEM((QB, ROWS, FORE), BF16)] * NX
        + [pltpu.VMEM((NX, 2 * NZ, ROWS, FORE), BF16)]
        + [slots] * NX
        + [
            pltpu.VMEM((NX, KEYS, D), BF16),
            pltpu.VMEM((NX, 2 * NX, 128), F32),
            pltpu.VMEM((NX, SHARD), F32),
            pltpu.VMEM((NX, SHARD), F32),
            pltpu.VMEM((HEADS, *pattern.shape[1:]), I32),
            pltpu.SMEM(target.shape, I32),
        ]
        + [DMA((NX, 2 * NZ))] * 2
        + [DMA((NX,))] * 4
        + [DMA((NX, NY))] * 4
        + [DMA((NX,))] * 10
        + [DMA((8,))],
        compiler_params=pltpu.CompilerParams(
            collective_id=0, has_side_effects=True, vmem_limit_bytes=24 << 20
        ),
        name="spread",
    )(target, q, k, v, ks, vs, pattern)


def attend_kernel(
    ints, q_fore, q_rest, keys, values, factors, out_fore, out_rest, extra_out,
    qs, sc, mx, acc, su, extra, items,
):
    row = iota((B, B), 1)
    row = ((row >> 3) & 3) * PART + (row >> 5) * ROWS + (row & 7)
    ahead = iota((B, B), 0) - row
    extra[...] = jnp.zeros((B, B), F32)
    qs[HEADS] = jnp.zeros((D, B), BF16)

    def tall(tile):
        return jnp.broadcast_to(tile[None], (B // 8, 8, B)).reshape(B, B)

    @pl.loop(0, QB // TOGETHER)
    def _(part_of):
        def add_pair(r, n):
            def add(t, n):
                items[n] = r * 16 + t
                return n + 1

            return lax.fori_loop(0, (ints[part_of * LANES + r, KB] + 1) // 2, add, n)

        n = lax.fori_loop(0, LANES, add_pair, jnp.int32(0))
        for g in range(STEP):
            items[n + g] = HEADS * 16
        count = (n + STEP - 1) // STEP
        for j in range(TOGETHER):
            for q_ref, low, high in ((q_fore, 0, EARLY), (q_rest, EARLY, HEADS)):
                rows = q_ref[:, :, part_of * TOGETHER + j].astype(F32).reshape(B, (high - low) * D)
                rows = rows.astype(BF16)
                for h in range(low, high):
                    qs[j * 8 + h] = rows[:, (h - low) * D : (h - low + 1) * D].T
        mx[...] = jnp.full(mx.shape, NEG, F32)
        acc[...] = jnp.zeros(acc.shape, F32)
        su[...] = jnp.zeros(su.shape, F32)

        def item_at(i, g):
            item = items[i * STEP + g]
            r, t = item >> 4, item & 15
            codes = [ints[part_of * LANES + r, t * 2 + u] for u in range(2)]
            return r, codes, [code & (KB - 1) for code in codes]

        @pl.loop(0, count)
        def _(i):
            for g in range(STEP):
                r, codes, kbs = item_at(i, g)
                both = jnp.dot(
                    jnp.concatenate([keys[kb] for kb in kbs], axis=0), qs[r], preferred_element_type=F32
                )
                top = mx[r]
                for u in range(2):
                    score = both[u * B : (u + 1) * B] * tall(factors[kbs[u]])
                    score = jnp.where(ahead <= (codes[u] >> 5) * B, score, NEG)
                    sc[(i * STEP + g) * 2 + u] = score
                    top = jnp.maximum(top, jnp.max(score.reshape(B // 8, 8, B), axis=0))
                mx[r] = top

        for j in range(TOGETHER):
            for h in range(HEADS):
                top = jnp.max(mx[j * 8 + h], axis=0, keepdims=True)
                mx[j * 8 + h] = jnp.broadcast_to(top, (8, B)).astype(BF16).astype(F32)

        @pl.loop(0, count)
        def _(i):
            for g in range(STEP):
                r, codes, kbs = item_at(i, g)
                top = tall(mx[r])
                weights = [jnp.exp2(sc[(i * STEP + g) * 2 + u] - top) for u in range(2)]
                su[r] += jnp.sum((weights[0] + weights[1]).reshape(B // 8, 8, B), axis=0)
                acc[r] += jnp.dot(
                    jnp.concatenate([values[kb] for kb in kbs], axis=1),
                    jnp.concatenate([w.astype(BF16) for w in weights], axis=0),
                    preferred_element_type=F32,
                )

        for j in range(TOGETHER):
            for h in range(HEADS):
                r = j * 8 + h
                at = part_of * LANES + r
                extra[pl.ds(at, 1), :] = mx[r][0:1]
                extra[pl.ds(SUM_LANE + at, 1), :] = jnp.sum(su[r], axis=0, keepdims=True)
                part = acc[r].astype(BF16).T
                out, i = (out_fore, h) if h < EARLY else (out_rest, h - EARLY)
                for d in range(NY):
                    out[d, part_of * TOGETHER + j, :, i * D : (i + 1) * D] = part[d * PART : (d + 1) * PART]

    turned = extra[...].T
    for d in range(NY):
        extra_out[d] = turned[d * PART : (d + 1) * PART].astype(BF16)


def attend(lists, q_fore, q_rest, keys, values, factors):
    most = TOGETHER * HEADS * KB // 2 + STEP
    return pl.pallas_call(
        attend_kernel,
        out_shape=[
            jax.ShapeDtypeStruct((NY, QB, PART, FORE), BF16),
            jax.ShapeDtypeStruct((NY, QB, PART, REST), BF16),
            jax.ShapeDtypeStruct((NY, PART, 128), BF16),
        ],
        in_specs=[SMEM] + [VMEM] * 5,
        out_specs=[VMEM] * 3,
        scratch_shapes=[
            pltpu.VMEM((LANES, D, B), BF16),
            pltpu.VMEM((2 * most, B, B), F32),
            pltpu.VMEM((LANES, 8, B), F32),
            pltpu.VMEM((LANES, D, B), F32),
            pltpu.VMEM((LANES, 8, B), F32),
            pltpu.VMEM((B, B), F32),
            pltpu.SMEM((most,), I32),
        ],
        compiler_params=pltpu.CompilerParams(vmem_limit_bytes=46 << 20),
        name="attend",
    )(lists, q_fore, q_rest, keys.reshape(KB, B, D), values, factors)


def gather_kernel(
    target, p, p_rest, extra_in, out,
    parts, parts_rest, extra, att, att_rest, held, packed, came, goes,
    e_send, e_recv, y_send, y_recv, t_send, t_recv, x_send, x_recv, r_send, r_recv, z_send, z_recv, own,
):
    rep, z, c, x, y = place()
    xs = [(x + d) % NX for d in range(NX)]
    back = [(x + NX - d) % NX for d in range(NX)]
    ys = [(y + d) % NY for d in range(NY)]
    at_x = [(rep, xs[d] * NY + y) for d in range(NX)]
    at_y = [(rep, x * NY + ys[d]) for d in range(NY)]
    groups = near_groups(z, c)
    at_group = [(g, x * NY + y) for g in groups]
    partners = at_group[1:] + at_x[1:] + at_y[1:]
    barrier = pltpu.get_barrier_semaphore()
    for who in partners:
        pl.semaphore_signal(barrier, inc=1, device_id=who, device_id_type=MESH)
    told = pltpu.make_async_copy(target, goes, own.at[QB])
    told.start()
    told.wait()
    leaving, blocks = routes(goes, rep, groups)
    pl.semaphore_wait(barrier, len(partners))

    ex, ty, rx = ([None] * NY for _ in range(3))
    py = [[None] * NY for _ in range(QB)]
    px = [[None] * NX for _ in range(QB)]
    pz = [None] * len(groups)
    for d in FAR:
        ex[d] = remote(extra_in.at[ys[d]], extra.at[d], e_send.at[d], e_recv.at[d], at_y[d])
        ex[d].start()
        ty[d] = remote(p_rest.at[ys[d]], parts_rest.at[d], t_send.at[d], t_recv.at[d], at_y[d])
        ty[d].start()
    for b in range(QB):
        for d in FAR:
            py[b][d] = remote(p.at[ys[d], b], parts.at[d, b], y_send.at[b, d], y_recv.at[b, d], at_y[d])
            py[b][d].start()
    for d in FAR:
        ex[d].wait_recv()
    marks = [extra_in[y].astype(F32)] + [extra[d].astype(F32) for d in range(1, NY)]
    top = functools.reduce(jnp.maximum, marks)
    shift = [jnp.exp2(e - top) for e in marks]
    total = sum(w * pltpu.roll(e, SUM_LANE, 1) for w, e in zip(shift, marks))
    lane = iota((PART, 128), 1)
    total = jnp.where((lane < QB * 8) & ((lane & 7) < HEADS), total, 1.0)
    ratio = [w / total for w in shift]

    def quotient(b, h, mine, theirs, cols):
        at = b * 8 + h
        value = sum(
            jnp.broadcast_to(ratio[d][:, at : at + 1], (PART, D))
            * (theirs[d, b, :, cols] if d else mine[y, b, :, cols]).astype(F32)
            for d in range(NY)
        )
        return value.reshape(NX, ROWS, D).astype(BF16)

    for d in FAR:
        ty[d].wait_recv()
    for b in range(QB):
        for h in range(EARLY, HEADS):
            cols = slice((h - EARLY) * D, (h - EARLY + 1) * D)
            value = quotient(b, h, p_rest, parts_rest, cols)
            for d in range(NX):
                att_rest[d, b, :, cols] = value[d]
    for d in FAR:
        rx[d] = remote(att_rest.at[xs[d]], held.at[d], r_send.at[d], r_recv.at[d], at_x[d])
        rx[d].start()
    held[0] = att_rest[x]
    for d in FAR:
        rx[d].wait_recv()
    for n in ORDER:
        for d in range(NX):
            block = held[d, leaving[n]]
            if n == 0:
                came[n, d] = block
            else:
                packed[n, d] = block
        if n > 0:
            pz[n] = remote(packed.at[n], came.at[n], z_send.at[n], z_recv.at[n], at_group[n])
            pz[n].start()

    mine = pl.ds(pl.multiple_of(x * SLICE, D), FORE)
    for b in range(QB):
        for d in FAR:
            py[b][d].wait_recv()
        for h in range(EARLY):
            cols = slice(h * D, (h + 1) * D)
            value = quotient(b, h, p, parts, cols)
            for d in range(NX):
                att[b, d, :, cols] = value[d]
        for d in FAR:
            px[b][d] = remote(
                att.at[b, xs[d]], out.at[b, :, mine], x_send.at[b, d], x_recv.at[b, d], at_x[d]
            )
            px[b][d].start()
        px[b][0] = pltpu.make_async_copy(att.at[b, x], out.at[b, :, mine], own.at[b])
        px[b][0].start()

    for n in range(1, len(groups)):
        pz[n].wait_recv()
    for b in range(QB):
        px[b][0].wait()
        for d in FAR:
            px[b][d].wait_recv()
    for s in range(QB):
        n = slot_of(blocks[s], z, c)
        for d in range(NX):
            out[s, :, pl.ds(pl.multiple_of(back[d] * SLICE + FORE, D), REST)] = came[n, d]

    for n in range(1, len(groups)):
        pz[n].wait_send()
    for d in FAR:
        for copy in (ex[d], ty[d], rx[d]):
            copy.wait_send()
        for b in range(QB):
            px[b][d].wait_send()
            py[b][d].wait_send()


def gather(target, p, p_rest, extra):
    slots = pltpu.VMEM((2 * NZ, NX, ROWS, REST), BF16)
    return pl.pallas_call(
        gather_kernel,
        out_shape=jax.ShapeDtypeStruct((QB, ROWS, NX * SLICE), BF16),
        in_specs=[HBM, VMEM, VMEM, VMEM],
        out_specs=VMEM,
        scratch_shapes=[
            pltpu.VMEM((NY, QB, PART, FORE), BF16),
            pltpu.VMEM((NY, QB, PART, REST), BF16),
            pltpu.VMEM((NY, PART, 128), BF16),
            pltpu.VMEM((QB, NX, ROWS, FORE), BF16),
            pltpu.VMEM((NX, QB, ROWS, REST), BF16),
            pltpu.VMEM((NX, QB, ROWS, REST), BF16),
            slots,
            slots,
            pltpu.SMEM(target.shape, I32),
        ]
        + [DMA((NY,))] * 2
        + [DMA((QB, NY))] * 2
        + [DMA((NY,))] * 2
        + [DMA((QB, NX))] * 2
        + [DMA((NX,))] * 2
        + [DMA((2 * NZ,))] * 2
        + [DMA((QB + 1,))],
        compiler_params=pltpu.CompilerParams(
            collective_id=1, has_side_effects=True, vmem_limit_bytes=16 << 20
        ),
        name="gather",
    )(target, p, p_rest, extra)


def hbm(array):
    return pltpu.with_memory_space_constraint(array, pltpu.HBM)


def per_device(queries, key_cache, value_cache, key_scale, value_scale, pattern, target):
    target = hbm(target)
    q_fore, q_rest, keys, values, factors, lists = spread(
        target,
        hbm(queries),
        hbm(key_cache),
        hbm(value_cache),
        hbm(key_scale.T),
        hbm(value_scale.T),
        hbm(jnp.swapaxes(pattern, 1, 2)),
    )
    part, rest, extra = attend(lists, q_fore, q_rest, keys, values, factors)
    return gather(target, part, rest, extra)


def solution(mesh):
    return jax.shard_map(
        per_device,
        mesh=mesh,
        in_specs=(
            P("replica", "ctx", None),
            P("ctx", None),
            P("ctx", None),
            P("ctx", None),
            P("ctx", None),
            P(),
            P(),
        ),
        out_specs=P("replica", "ctx", None),
        check_vma=False,
    )
```

```python
import functools
import math

import jax
import jax.numpy as jnp
from jax import lax
from jax.experimental import pallas as pl
from jax.experimental.pallas import tpu as pltpu
from jax.sharding import PartitionSpec as P

MESH = pl.DeviceIdType.MESH
BF16 = jnp.bfloat16
F32 = jnp.float32
I32 = jnp.int32

NX = 4
NY = 4
NZ = 8
HEADS = 7
D = 128
B = 128
QB = 4
KB = 32
SHARD = 8
SLICE = HEADS * D
EARLY = 5
FORE = EARLY * D
REST = SLICE - FORE
ROWS = B // (NX * NY)
PART = NX * ROWS
KEYS = SHARD * B
PAIRS = 32
SUM_LANE = 64
NEG = -(2.0**100)
STEP = 24
TOGETHER = 2
LANES = 8 * TOGETHER
FIRST = 64
FAR = (1, 3, 2)
ORDER = (8, 9, 6, 7, 10, 11, 4, 5, 12, 13, 2, 3, 14, 15, 1, 0)
TO_LOG2 = math.log2(math.e) / math.sqrt(D)

DMA = pltpu.SemaphoreType.DMA
HBM = pl.BlockSpec(memory_space=pltpu.HBM)
VMEM = pl.BlockSpec(memory_space=pltpu.VMEM)
SMEM = pl.BlockSpec(memory_space=pltpu.SMEM)


def place():
    rep = lax.axis_index("replica")
    ctx = lax.axis_index("ctx")
    return rep, rep // 2, rep % 2, ctx // NY, ctx % NY


def remote(src, dst, send, recv, who):
    return pltpu.make_async_remote_copy(
        src_ref=src, dst_ref=dst, send_sem=send, recv_sem=recv, device_id=who, device_id_type=MESH
    )


def iota(shape, dim):
    return lax.broadcasted_iota(I32, shape, dim)


def block_lists(listed, blocks, rep, y):
    shape = (PAIRS, 128)
    lane, row = iota(shape, 1), iota(shape, 0)
    block = (lane >> 3) * (SHARD * NY) + y * SHARD + (lane & 7)
    hits = jnp.zeros(shape, I32)
    own = jnp.zeros(shape, I32)
    column = iota(listed.shape[1:], 1)
    for s in range(QB):
        own = jnp.where(row >> 3 == s, jnp.where((row & 7) < EARLY, blocks[s], rep * QB + s), own)
        for h in range(HEADS):
            of = blocks[s] if h < EARLY else rep * QB + s
            entry = jnp.max(jnp.where(column == of, listed[h], -1), axis=1, keepdims=True)
            found = (jnp.broadcast_to(entry, shape) == block).astype(I32)
            found = jnp.max(found, axis=0, keepdims=True)
            hits = jnp.where(row == s * 8 + h, found, hits)
    below = FIRST + own - block
    hits = jnp.where(below == 0, 1, hits)
    hits = jnp.where((below >= 0) & (lane < KB) & ((row & 7) < HEADS), hits, 0)
    upto = hits
    for s in (1, 2, 4, 8, 16):
        upto = upto + jnp.where(lane >= s, pltpu.roll(upto, s, 1), 0)
    slot = jnp.where(hits > 0, upto - 1, -1)
    code = lane + KB * below
    packed = jnp.full(shape, -KB * 1024, I32)
    for b in range(KB):
        at = jnp.broadcast_to(slot[:, b : b + 1], shape) == lane
        packed = jnp.where(at, jnp.broadcast_to(code[:, b : b + 1], shape), packed)
    number = jnp.broadcast_to(upto[:, KB - 1 : KB], shape)
    return jnp.where(lane == KB, number, packed)


def near_groups(z, c):
    return [((z + d) % NZ) * 2 + (c + e) % 2 for d in range(NZ) for e in range(2)]


def slot_of(block, z, c):
    source = block >> 2
    return (((z + NZ - (source >> 1)) & (NZ - 1)) << 1) + ((source & 1) ^ c)


def blocks_out(goes, rep, groups):
    goes_to = [goes[rep * QB + b] for b in range(QB)]
    leaving = []
    for group in groups:
        b = jnp.int32(0)
        for other in range(1, QB):
            b = jnp.where(goes_to[other] == group, other, b)
        leaving.append(b)
    return leaving


def blocks_in(goes, rep):
    def look(j, state):
        found, *at = state
        hit = goes[j] == rep
        at = [jnp.where(hit & (found == s), j, a) for s, a in enumerate(at)]
        return (found + hit.astype(I32), *at)

    _, *blocks = lax.fori_loop(0, 2 * NZ * QB, look, (jnp.int32(0),) * (1 + QB))
    return blocks


def spread_kernel(
    target, q, k, v, ks, vs, pattern,
    q_fore, q_rest, keys, values, factors, lists,
    held0, held1, held2, held3, packed, came0, came1, came2, came3,
    v_land, scales, k_loc, v_loc, listed, goes,
    z_send, z_recv, q_send, q_recv, r_send, r_recv, y_send, y_recv, t_send, t_recv, k_send, k_recv, v_send, v_recv, s_send, s_recv,
    kc_send, kc_recv, vc_send, vc_recv, own,
):
    rep, z, c, x, y = place()
    sib = (rep + 1 - 2 * c, x * NY + y)
    xs = [(x + d) % NX for d in range(NX)]
    back = [(x + NX - d) % NX for d in range(NX)]
    at_x = [(rep, xs[d] * NY + y) for d in range(NX)]
    at_y = [(rep, x * NY + (y + d) % NY) for d in range(NY)]
    half = pl.ds(pl.multiple_of(c * (KEYS // 2), KEYS // 2), KEYS // 2)
    groups = near_groups(z, c)
    at_group = [(g, x * NY + y) for g in groups]
    held = (held0, held1, held2, held3)
    came = (came0, came1, came2, came3)

    def cols(d, n):
        return pl.ds(pl.multiple_of(xs[d] * n, n), n)

    def fore(d):
        return q.at[:, :, pl.ds(pl.multiple_of(xs[d] * SLICE, D), FORE)]

    def rest(d):
        return q.at[:, :, pl.ds(pl.multiple_of(xs[d] * SLICE + FORE, D), REST)]

    partners = at_group[1:] + at_x[1:] + at_y[1:]
    barrier = pltpu.get_barrier_semaphore()
    for who in partners:
        pl.semaphore_signal(barrier, inc=1, device_id=who, device_id_type=MESH)
    stay = [
        pltpu.make_async_copy(target, goes, own.at[0]),
        pltpu.make_async_copy(fore(0), held[0], own.at[1]),
        pltpu.make_async_copy(ks, k_loc, own.at[2]),
        pltpu.make_async_copy(vs, v_loc, own.at[3]),
        pltpu.make_async_copy(pattern.at[pl.ds(x * HEADS, HEADS)], listed, own.at[4]),
        pltpu.make_async_copy(k.at[:, cols(0, D)], keys.at[x], own.at[5]),
        pltpu.make_async_copy(v.at[:, cols(0, D)], v_land.at[0], own.at[6]),
        pltpu.make_async_copy(rest(0), q_rest.at[y, x], own.at[7]),
    ]
    for copy in stay:
        copy.start()

    qx, rx, kx, vx, sx, kc, vc = ([None] * NX for _ in range(7))
    qy, ry = ([[None] * NY for _ in range(NX)] for _ in range(2))
    qz = [[None] * len(groups) for _ in range(NX)]

    pl.semaphore_wait(barrier, len(partners))
    for d in FAR:
        qx[d] = remote(fore(d), held[d], q_send.at[d], q_recv.at[d], at_x[d])
        qx[d].start()
    stay[0].wait()
    leaving = blocks_out(goes, rep, groups)

    def pack(d):
        for n in ORDER:
            block = held[d][leaving[n]]
            if n == 0:
                came[d][n] = block
            else:
                packed[d, n] = block

    def over_z(d):
        for n in ORDER[:-1]:
            qz[d][n] = remote(packed.at[d, n], came[d].at[n], z_send.at[d, n], z_recv.at[d, n], at_group[n])
            qz[d][n].start()

    stay[1].wait()
    pack(0)
    over_z(0)
    for d in FAR:
        kx[d] = remote(k.at[half, cols(d, D)], keys.at[x, half], k_send.at[d], k_recv.at[d], at_x[d])
        vx[d] = remote(v.at[half, cols(d, D)], v_land.at[d, half], v_send.at[d], v_recv.at[d], at_x[d])
        rx[d] = remote(rest(d), q_rest.at[y, x], r_send.at[d], r_recv.at[d], at_x[d])
        rx[d].start()
        kx[d].start()
        vx[d].start()
    for d in FAR:
        qx[d].wait_recv()
        pack(d)
        over_z(d)
    scales[0] = jnp.zeros((2 * NX, 128), F32)
    stay[2].wait()
    stay[3].wait()
    scales[0, 0:NX, 0:SHARD] = k_loc[...]
    scales[0, NX : 2 * NX, 0:SHARD] = v_loc[...]
    for d in FAR:
        sx[d] = remote(scales.at[0], scales.at[d], s_send.at[d], s_recv.at[d], at_x[d])
        sx[d].start()
    blocks = blocks_in(goes, rep)

    stay[4].wait()
    lists[...] = block_lists(listed, blocks, rep, y)

    scale_row = iota((2 * NX, 128), 0)

    def pick_row(tile, n):
        return jnp.sum(jnp.where(scale_row == n, tile, 0.0), axis=0, keepdims=True)

    def finish(d):
        tile = scales[d]
        for_keys = pick_row(tile, x) * TO_LOG2
        for_values = pick_row(tile, NX + x)
        for b in range(SHARD):
            at = back[d] * SHARD + b
            factors[at] = jnp.broadcast_to(for_keys[:, b : b + 1], (8, 128))
            rows = slice(b * B, (b + 1) * B)
            scaled = v_land[d, rows].astype(F32) * jnp.broadcast_to(for_values[:, b : b + 1], (B, D))
            values[at] = scaled.astype(BF16).T

    def hand_over(d):
        kx[d].wait_recv()
        piece = keys.at[back[d], half]
        kc[d] = remote(piece, piece, kc_send.at[d], kc_recv.at[d], sib)
        kc[d].start()
        vx[d].wait_recv()
        vc[d] = remote(v_land.at[d, half], v_land.at[d, half], vc_send.at[d], vc_recv.at[d], sib)
        vc[d].start()
        sx[d].wait_recv()

    def whole(d):
        kc[d].wait_recv()
        vc[d].wait_recv()
        finish(d)

    def over_y(d):
        for n in range(1, len(groups)):
            qz[d][n].wait_recv()
        for s in range(QB):
            q_fore[y, back[d], s] = came[d][slot_of(blocks[s], z, c)]
        for e in FAR:
            piece = q_fore.at[y, back[d]]
            qy[d][e] = remote(piece, piece, y_send.at[d, e], y_recv.at[d, e], at_y[e])
            qy[d][e].start()

    stay[7].wait()
    for d in (0, *FAR):
        if d:
            rx[d].wait_recv()
        for e in FAR:
            piece = q_rest.at[y, back[d]]
            ry[d][e] = remote(piece, piece, t_send.at[d, e], t_recv.at[d, e], at_y[e])
            ry[d][e].start()
    for copy in stay[5:7]:
        copy.wait()
    finish(0)
    hand_over(1)
    hand_over(3)
    over_y(0)
    whole(1)
    whole(3)
    over_y(1)
    hand_over(2)
    whole(2)
    over_y(3)
    over_y(2)
    for d in range(NX):
        for e in FAR:
            for copy in (qy[d][e], ry[d][e]):
                copy.wait_recv()
                copy.wait_send()
    for d in FAR:
        for copy in (qx[d], rx[d], kx[d], vx[d], sx[d], kc[d], vc[d]):
            copy.wait_send()
    for copies in qz:
        for copy in copies[1:]:
            copy.wait_send()


def spread(target, q, k, v, ks, vs, pattern):
    slots = pltpu.VMEM((2 * NZ, ROWS, FORE), BF16)
    return pl.pallas_call(
        spread_kernel,
        out_shape=[
            jax.ShapeDtypeStruct((NY, NX, QB, ROWS, FORE), BF16),
            jax.ShapeDtypeStruct((NY, NX, QB, ROWS, REST), BF16),
            jax.ShapeDtypeStruct((NX, KEYS, D), BF16),
            jax.ShapeDtypeStruct((KB, D, B), BF16),
            jax.ShapeDtypeStruct((KB, 8, 128), F32),
            jax.ShapeDtypeStruct((PAIRS, 128), I32),
        ],
        in_specs=[HBM] * 7,
        out_specs=[VMEM] * 6,
        scratch_shapes=[pltpu.VMEM((QB, ROWS, FORE), BF16)] * NX
        + [pltpu.VMEM((NX, 2 * NZ, ROWS, FORE), BF16)]
        + [slots] * NX
        + [
            pltpu.VMEM((NX, KEYS, D), BF16),
            pltpu.VMEM((NX, 2 * NX, 128), F32),
            pltpu.VMEM((NX, SHARD), F32),
            pltpu.VMEM((NX, SHARD), F32),
            pltpu.VMEM((HEADS, *pattern.shape[1:]), I32),
            pltpu.SMEM(target.shape, I32),
        ]
        + [DMA((NX, 2 * NZ))] * 2
        + [DMA((NX,))] * 4
        + [DMA((NX, NY))] * 4
        + [DMA((NX,))] * 10
        + [DMA((8,))],
        compiler_params=pltpu.CompilerParams(
            collective_id=0, has_side_effects=True, vmem_limit_bytes=24 << 20
        ),
        name="spread",
    )(target, q, k, v, ks, vs, pattern)


def attend_kernel(
    ints, q_fore, q_rest, keys, values, factors, out_fore, out_rest, extra_out,
    qs, sc, mx, acc, su, extra, items,
):
    row = iota((B, B), 1)
    row = ((row >> 3) & 3) * PART + (row >> 5) * ROWS + (row & 7)
    ahead = iota((B, B), 0) - row
    extra[...] = jnp.zeros((B, B), F32)
    qs[HEADS] = jnp.zeros((D, B), BF16)

    def tall(tile):
        return jnp.broadcast_to(tile[None], (B // 8, 8, B)).reshape(B, B)

    @pl.loop(0, QB // TOGETHER)
    def _(part_of):
        def add_pair(r, n):
            def add(t, n):
                items[n] = r * 16 + t
                return n + 1

            return lax.fori_loop(0, (ints[part_of * LANES + r, KB] + 1) // 2, add, n)

        n = lax.fori_loop(0, LANES, add_pair, jnp.int32(0))
        for g in range(STEP):
            items[n + g] = HEADS * 16
        count = (n + STEP - 1) // STEP
        for j in range(TOGETHER):
            for q_ref, low, high in ((q_fore, 0, EARLY), (q_rest, EARLY, HEADS)):
                rows = q_ref[:, :, part_of * TOGETHER + j].astype(F32).reshape(B, (high - low) * D)
                rows = rows.astype(BF16)
                for h in range(low, high):
                    qs[j * 8 + h] = rows[:, (h - low) * D : (h - low + 1) * D].T
        mx[...] = jnp.full(mx.shape, NEG, F32)
        acc[...] = jnp.zeros(acc.shape, F32)
        su[...] = jnp.zeros(su.shape, F32)

        def item_at(i, g):
            item = items[i * STEP + g]
            r, t = item >> 4, item & 15
            codes = [ints[part_of * LANES + r, t * 2 + u] for u in range(2)]
            return r, codes, [code & (KB - 1) for code in codes]

        @pl.loop(0, count)
        def _(i):
            for g in range(STEP):
                r, codes, kbs = item_at(i, g)
                both = jnp.dot(
                    jnp.concatenate([keys[kb] for kb in kbs], axis=0), qs[r], preferred_element_type=F32
                )
                top = mx[r]
                for u in range(2):
                    score = both[u * B : (u + 1) * B] * tall(factors[kbs[u]])
                    score = jnp.where(ahead <= (codes[u] >> 5) * B, score, NEG)
                    sc[(i * STEP + g) * 2 + u] = score
                    top = jnp.maximum(top, jnp.max(score.reshape(B // 8, 8, B), axis=0))
                mx[r] = top

        for j in range(TOGETHER):
            for h in range(HEADS):
                top = jnp.max(mx[j * 8 + h], axis=0, keepdims=True)
                mx[j * 8 + h] = jnp.broadcast_to(top, (8, B)).astype(BF16).astype(F32)

        @pl.loop(0, count)
        def _(i):
            for g in range(STEP):
                r, codes, kbs = item_at(i, g)
                top = tall(mx[r])
                weights = [jnp.exp2(sc[(i * STEP + g) * 2 + u] - top) for u in range(2)]
                su[r] += jnp.sum((weights[0] + weights[1]).reshape(B // 8, 8, B), axis=0)
                acc[r] += jnp.dot(
                    jnp.concatenate([values[kb] for kb in kbs], axis=1),
                    jnp.concatenate([w.astype(BF16) for w in weights], axis=0),
                    preferred_element_type=F32,
                )

        for j in range(TOGETHER):
            for h in range(HEADS):
                r = j * 8 + h
                at = part_of * LANES + r
                extra[pl.ds(at, 1), :] = mx[r][0:1]
                extra[pl.ds(SUM_LANE + at, 1), :] = jnp.sum(su[r], axis=0, keepdims=True)
                part = acc[r].astype(BF16).T
                out, i = (out_fore, h) if h < EARLY else (out_rest, h - EARLY)
                for d in range(NY):
                    out[d, part_of * TOGETHER + j, :, i * D : (i + 1) * D] = part[d * PART : (d + 1) * PART]

    turned = extra[...].T
    for d in range(NY):
        extra_out[d] = turned[d * PART : (d + 1) * PART].astype(BF16)


def attend(lists, q_fore, q_rest, keys, values, factors):
    most = TOGETHER * HEADS * KB // 2 + STEP
    return pl.pallas_call(
        attend_kernel,
        out_shape=[
            jax.ShapeDtypeStruct((NY, QB, PART, FORE), BF16),
            jax.ShapeDtypeStruct((NY, QB, PART, REST), BF16),
            jax.ShapeDtypeStruct((NY, PART, 128), BF16),
        ],
        in_specs=[SMEM] + [VMEM] * 5,
        out_specs=[VMEM] * 3,
        scratch_shapes=[
            pltpu.VMEM((LANES, D, B), BF16),
            pltpu.VMEM((2 * most, B, B), F32),
            pltpu.VMEM((LANES, 8, B), F32),
            pltpu.VMEM((LANES, D, B), F32),
            pltpu.VMEM((LANES, 8, B), F32),
            pltpu.VMEM((B, B), F32),
            pltpu.SMEM((most,), I32),
        ],
        compiler_params=pltpu.CompilerParams(vmem_limit_bytes=46 << 20),
        name="attend",
    )(lists, q_fore, q_rest, keys.reshape(KB, B, D), values, factors)


def gather_kernel(
    target, p, p_rest, extra_in, out,
    parts, parts_rest, extra, att, att_rest, held, packed, came, goes,
    e_send, e_recv, y_send, y_recv, t_send, t_recv, x_send, x_recv, r_send, r_recv, z_send, z_recv, own,
):
    rep, z, c, x, y = place()
    xs = [(x + d) % NX for d in range(NX)]
    back = [(x + NX - d) % NX for d in range(NX)]
    ys = [(y + d) % NY for d in range(NY)]
    at_x = [(rep, xs[d] * NY + y) for d in range(NX)]
    at_y = [(rep, x * NY + ys[d]) for d in range(NY)]
    groups = near_groups(z, c)
    at_group = [(g, x * NY + y) for g in groups]
    partners = at_group[1:] + at_x[1:] + at_y[1:]
    barrier = pltpu.get_barrier_semaphore()
    for who in partners:
        pl.semaphore_signal(barrier, inc=1, device_id=who, device_id_type=MESH)
    told = pltpu.make_async_copy(target, goes, own.at[QB])
    told.start()
    pl.semaphore_wait(barrier, len(partners))

    ex, ty, rx = ([None] * NY for _ in range(3))
    py = [[None] * NY for _ in range(QB)]
    px = [[None] * NX for _ in range(QB)]
    pz = [None] * len(groups)
    for d in FAR:
        ex[d] = remote(extra_in.at[ys[d]], extra.at[d], e_send.at[d], e_recv.at[d], at_y[d])
        ex[d].start()
        ty[d] = remote(p_rest.at[ys[d]], parts_rest.at[d], t_send.at[d], t_recv.at[d], at_y[d])
        ty[d].start()
    for b in range(QB):
        for d in FAR:
            py[b][d] = remote(p.at[ys[d], b], parts.at[d, b], y_send.at[b, d], y_recv.at[b, d], at_y[d])
            py[b][d].start()
    told.wait()
    leaving = blocks_out(goes, rep, groups)
    blocks = blocks_in(goes, rep)
    for d in FAR:
        ex[d].wait_recv()
    marks = [extra_in[y].astype(F32)] + [extra[d].astype(F32) for d in range(1, NY)]
    top = functools.reduce(jnp.maximum, marks)
    shift = [jnp.exp2(e - top) for e in marks]
    total = sum(w * pltpu.roll(e, SUM_LANE, 1) for w, e in zip(shift, marks))
    lane = iota((PART, 128), 1)
    total = jnp.where((lane < QB * 8) & ((lane & 7) < HEADS), total, 1.0)
    ratio = [w / total for w in shift]

    def quotient(b, h, mine, theirs, cols):
        at = b * 8 + h
        value = sum(
            jnp.broadcast_to(ratio[d][:, at : at + 1], (PART, D))
            * (theirs[d, b, :, cols] if d else mine[y, b, :, cols]).astype(F32)
            for d in range(NY)
        )
        return value.reshape(NX, ROWS, D).astype(BF16)

    for d in FAR:
        ty[d].wait_recv()
    for b in range(QB):
        for h in range(EARLY, HEADS):
            cols = slice((h - EARLY) * D, (h - EARLY + 1) * D)
            value = quotient(b, h, p_rest, parts_rest, cols)
            for d in range(NX):
                att_rest[d, b, :, cols] = value[d]
    for d in FAR:
        rx[d] = remote(att_rest.at[xs[d]], held.at[d], r_send.at[d], r_recv.at[d], at_x[d])
        rx[d].start()
    held[0] = att_rest[x]
    for d in FAR:
        rx[d].wait_recv()
    for n in ORDER:
        for d in range(NX):
            block = held[d, leaving[n]]
            if n == 0:
                came[n, d] = block
            else:
                packed[n, d] = block
        if n > 0:
            pz[n] = remote(packed.at[n], came.at[n], z_send.at[n], z_recv.at[n], at_group[n])
            pz[n].start()

    mine = pl.ds(pl.multiple_of(x * SLICE, D), FORE)
    for b in range(QB):
        for d in FAR:
            py[b][d].wait_recv()
        for h in range(EARLY):
            cols = slice(h * D, (h + 1) * D)
            value = quotient(b, h, p, parts, cols)
            for d in range(NX):
                att[b, d, :, cols] = value[d]
        for d in FAR:
            px[b][d] = remote(
                att.at[b, xs[d]], out.at[b, :, mine], x_send.at[b, d], x_recv.at[b, d], at_x[d]
            )
            px[b][d].start()
        px[b][0] = pltpu.make_async_copy(att.at[b, x], out.at[b, :, mine], own.at[b])
        px[b][0].start()

    for n in range(1, len(groups)):
        pz[n].wait_recv()
    for b in range(QB):
        px[b][0].wait()
        for d in FAR:
            px[b][d].wait_recv()
    for s in range(QB):
        n = slot_of(blocks[s], z, c)
        for d in range(NX):
            out[s, :, pl.ds(pl.multiple_of(back[d] * SLICE + FORE, D), REST)] = came[n, d]

    for n in range(1, len(groups)):
        pz[n].wait_send()
    for d in FAR:
        for copy in (ex[d], ty[d], rx[d]):
            copy.wait_send()
        for b in range(QB):
            px[b][d].wait_send()
            py[b][d].wait_send()


def gather(target, p, p_rest, extra):
    slots = pltpu.VMEM((2 * NZ, NX, ROWS, REST), BF16)
    return pl.pallas_call(
        gather_kernel,
        out_shape=jax.ShapeDtypeStruct((QB, ROWS, NX * SLICE), BF16),
        in_specs=[HBM, VMEM, VMEM, VMEM],
        out_specs=VMEM,
        scratch_shapes=[
            pltpu.VMEM((NY, QB, PART, FORE), BF16),
            pltpu.VMEM((NY, QB, PART, REST), BF16),
            pltpu.VMEM((NY, PART, 128), BF16),
            pltpu.VMEM((QB, NX, ROWS, FORE), BF16),
            pltpu.VMEM((NX, QB, ROWS, REST), BF16),
            pltpu.VMEM((NX, QB, ROWS, REST), BF16),
            slots,
            slots,
            pltpu.SMEM(target.shape, I32),
        ]
        + [DMA((NY,))] * 2
        + [DMA((QB, NY))] * 2
        + [DMA((NY,))] * 2
        + [DMA((QB, NX))] * 2
        + [DMA((NX,))] * 2
        + [DMA((2 * NZ,))] * 2
        + [DMA((QB + 1,))],
        compiler_params=pltpu.CompilerParams(
            collective_id=1, has_side_effects=True, vmem_limit_bytes=16 << 20
        ),
        name="gather",
    )(target, p, p_rest, extra)


def hbm(array):
    return pltpu.with_memory_space_constraint(array, pltpu.HBM)


def per_device(queries, key_cache, value_cache, key_scale, value_scale, pattern, target):
    target = hbm(target)
    q_fore, q_rest, keys, values, factors, lists = spread(
        target,
        hbm(queries),
        hbm(key_cache),
        hbm(value_cache),
        hbm(key_scale.T),
        hbm(value_scale.T),
        hbm(jnp.swapaxes(pattern, 1, 2)),
    )
    part, rest, extra = attend(lists, q_fore, q_rest, keys, values, factors)
    return gather(target, part, rest, extra)


def solution(mesh):
    return jax.shard_map(
        per_device,
        mesh=mesh,
        in_specs=(
            P("replica", "ctx", None),
            P("ctx", None),
            P("ctx", None),
            P("ctx", None),
            P("ctx", None),
            P(),
            P(),
        ),
        out_specs=P("replica", "ctx", None),
        check_vma=False,
    )
```

```python
import functools
import math

import jax
import jax.numpy as jnp
from jax import lax
from jax.experimental import pallas as pl
from jax.experimental.pallas import tpu as pltpu
from jax.sharding import PartitionSpec as P

MESH = pl.DeviceIdType.MESH
BF16 = jnp.bfloat16
F32 = jnp.float32
I32 = jnp.int32

NX = 4
NY = 4
NZ = 8
HEADS = 7
D = 128
B = 128
QB = 4
KB = 32
SHARD = 8
SLICE = HEADS * D
EARLY = 5
FORE = EARLY * D
REST = SLICE - FORE
ROWS = B // (NX * NY)
PART = NX * ROWS
KEYS = SHARD * B
PAIRS = 32
SUM_LANE = 64
NEG = -(2.0**100)
STEP = 24
TOGETHER = 2
LANES = 8 * TOGETHER
FIRST = 64
FAR = (1, 3, 2)
ORDER = (8, 9, 6, 7, 10, 11, 4, 5, 12, 13, 2, 3, 14, 15, 1, 0)
TO_LOG2 = math.log2(math.e) / math.sqrt(D)

DMA = pltpu.SemaphoreType.DMA
HBM = pl.BlockSpec(memory_space=pltpu.HBM)
VMEM = pl.BlockSpec(memory_space=pltpu.VMEM)
SMEM = pl.BlockSpec(memory_space=pltpu.SMEM)


def place():
    rep = lax.axis_index("replica")
    ctx = lax.axis_index("ctx")
    return rep, rep // 2, rep % 2, ctx // NY, ctx % NY


def remote(src, dst, send, recv, who):
    return pltpu.make_async_remote_copy(
        src_ref=src, dst_ref=dst, send_sem=send, recv_sem=recv, device_id=who, device_id_type=MESH
    )


def iota(shape, dim):
    return lax.broadcasted_iota(I32, shape, dim)


def block_lists(listed, blocks, rep, y):
    shape = (PAIRS, 128)
    lane, row = iota(shape, 1), iota(shape, 0)
    block = (lane >> 3) * (SHARD * NY) + y * SHARD + (lane & 7)
    hits = jnp.zeros(shape, I32)
    own = jnp.zeros(shape, I32)
    column = iota(listed.shape[1:], 1)
    for s in range(QB):
        own = jnp.where(row >> 3 == s, jnp.where((row & 7) < EARLY, blocks[s], rep * QB + s), own)
        for h in range(HEADS):
            of = blocks[s] if h < EARLY else rep * QB + s
            entry = jnp.max(jnp.where(column == of, listed[h], -1), axis=1, keepdims=True)
            found = (jnp.broadcast_to(entry, shape) == block).astype(I32)
            found = jnp.max(found, axis=0, keepdims=True)
            hits = jnp.where(row == s * 8 + h, found, hits)
    below = FIRST + own - block
    hits = jnp.where(below == 0, 1, hits)
    hits = jnp.where((below >= 0) & (lane < KB) & ((row & 7) < HEADS), hits, 0)
    upto = hits
    for s in (1, 2, 4, 8, 16):
        upto = upto + jnp.where(lane >= s, pltpu.roll(upto, s, 1), 0)
    slot = jnp.where(hits > 0, upto - 1, -1)
    code = lane + KB * below
    packed = jnp.full(shape, -KB * 1024, I32)
    for b in range(KB):
        at = jnp.broadcast_to(slot[:, b : b + 1], shape) == lane
        packed = jnp.where(at, jnp.broadcast_to(code[:, b : b + 1], shape), packed)
    number = jnp.broadcast_to(upto[:, KB - 1 : KB], shape)
    return jnp.where(lane == KB, number, packed)


def near_groups(z, c):
    return [((z + d) % NZ) * 2 + (c + e) % 2 for d in range(NZ) for e in range(2)]


def slot_of(block, z, c):
    source = block >> 2
    return (((z + NZ - (source >> 1)) & (NZ - 1)) << 1) + ((source & 1) ^ c)


def blocks_out(goes, rep, groups):
    goes_to = [goes[rep * QB + b] for b in range(QB)]
    leaving = []
    for group in groups:
        b = jnp.int32(0)
        for other in range(1, QB):
            b = jnp.where(goes_to[other] == group, other, b)
        leaving.append(b)
    return leaving


def blocks_in(goes, rep):
    def look(j, state):
        found, *at = state
        hit = goes[j] == rep
        at = [jnp.where(hit & (found == s), j, a) for s, a in enumerate(at)]
        return (found + hit.astype(I32), *at)

    _, *blocks = lax.fori_loop(0, 2 * NZ * QB, look, (jnp.int32(0),) * (1 + QB))
    return blocks


def spread_kernel(
    target, q, k, v, ks, vs, pattern,
    q_fore, q_rest, keys, values, factors, lists,
    held0, held1, held2, held3, packed, came0, came1, came2, came3,
    v_land, scales, k_loc, v_loc, listed, goes,
    z_send, z_recv, q_send, q_recv, r_send, r_recv, y_send, y_recv, t_send, t_recv, k_send, k_recv, v_send, v_recv, s_send, s_recv,
    kc_send, kc_recv, vc_send, vc_recv, own,
):
    rep, z, c, x, y = place()
    sib = (rep + 1 - 2 * c, x * NY + y)
    xs = [(x + d) % NX for d in range(NX)]
    back = [(x + NX - d) % NX for d in range(NX)]
    at_x = [(rep, xs[d] * NY + y) for d in range(NX)]
    at_y = [(rep, x * NY + (y + d) % NY) for d in range(NY)]
    half = pl.ds(pl.multiple_of(c * (KEYS // 2), KEYS // 2), KEYS // 2)
    groups = near_groups(z, c)
    at_group = [(g, x * NY + y) for g in groups]
    held = (held0, held1, held2, held3)
    came = (came0, came1, came2, came3)

    def cols(d, n):
        return pl.ds(pl.multiple_of(xs[d] * n, n), n)

    def fore(d):
        return q.at[:, :, pl.ds(pl.multiple_of(xs[d] * SLICE, D), FORE)]

    def rest(d):
        return q.at[:, :, pl.ds(pl.multiple_of(xs[d] * SLICE + FORE, D), REST)]

    partners = at_group[1:] + at_x[1:] + at_y[1:]
    barrier = pltpu.get_barrier_semaphore()
    for who in partners:
        pl.semaphore_signal(barrier, inc=1, device_id=who, device_id_type=MESH)
    stay = [
        pltpu.make_async_copy(target, goes, own.at[0]),
        pltpu.make_async_copy(fore(0), held[0], own.at[1]),
        pltpu.make_async_copy(ks, k_loc, own.at[2]),
        pltpu.make_async_copy(vs, v_loc, own.at[3]),
        pltpu.make_async_copy(pattern.at[pl.ds(x * HEADS, HEADS)], listed, own.at[4]),
        pltpu.make_async_copy(k.at[:, cols(0, D)], keys.at[x], own.at[5]),
        pltpu.make_async_copy(v.at[:, cols(0, D)], v_land.at[0], own.at[6]),
        pltpu.make_async_copy(rest(0), q_rest.at[y, x], own.at[7]),
    ]
    for copy in stay:
        copy.start()

    qx, rx, kx, vx, sx, kc, vc = ([None] * NX for _ in range(7))
    qy, ry = ([[None] * NY for _ in range(NX)] for _ in range(2))
    qz = [[None] * len(groups) for _ in range(NX)]

    stay[0].wait()
    leaving = blocks_out(goes, rep, groups)
    blocks = blocks_in(goes, rep)

    def pack(d):
        for n in ORDER:
            block = held[d][leaving[n]]
            if n == 0:
                came[d][n] = block
            else:
                packed[d, n] = block

    def over_z(d):
        for n in ORDER[:-1]:
            qz[d][n] = remote(packed.at[d, n], came[d].at[n], z_send.at[d, n], z_recv.at[d, n], at_group[n])
            qz[d][n].start()

    stay[1].wait()
    pack(0)
    scales[0] = jnp.zeros((2 * NX, 128), F32)
    stay[2].wait()
    stay[3].wait()
    scales[0, 0:NX, 0:SHARD] = k_loc[...]
    scales[0, NX : 2 * NX, 0:SHARD] = v_loc[...]

    pl.semaphore_wait(barrier, len(partners))
    for d in FAR:
        qx[d] = remote(fore(d), held[d], q_send.at[d], q_recv.at[d], at_x[d])
        qx[d].start()
    over_z(0)
    for d in FAR:
        rx[d] = remote(rest(d), q_rest.at[y, x], r_send.at[d], r_recv.at[d], at_x[d])
        rx[d].start()
    for d in FAR:
        sx[d] = remote(scales.at[0], scales.at[d], s_send.at[d], s_recv.at[d], at_x[d])
        sx[d].start()
    for d in FAR:
        kx[d] = remote(k.at[half, cols(d, D)], keys.at[x, half], k_send.at[d], k_recv.at[d], at_x[d])
        vx[d] = remote(v.at[half, cols(d, D)], v_land.at[d, half], v_send.at[d], v_recv.at[d], at_x[d])
        kx[d].start()
        vx[d].start()

    for d in FAR:
        qx[d].wait_recv()
        pack(d)
        over_z(d)

    stay[4].wait()
    lists[...] = block_lists(listed, blocks, rep, y)

    scale_row = iota((2 * NX, 128), 0)

    def pick_row(tile, n):
        return jnp.sum(jnp.where(scale_row == n, tile, 0.0), axis=0, keepdims=True)

    def finish(d):
        tile = scales[d]
        for_keys = pick_row(tile, x) * TO_LOG2
        for_values = pick_row(tile, NX + x)
        for b in range(SHARD):
            at = back[d] * SHARD + b
            factors[at] = jnp.broadcast_to(for_keys[:, b : b + 1], (8, 128))
            rows = slice(b * B, (b + 1) * B)
            scaled = v_land[d, rows].astype(F32) * jnp.broadcast_to(for_values[:, b : b + 1], (B, D))
            values[at] = scaled.astype(BF16).T

    def hand_over(d):
        kx[d].wait_recv()
        piece = keys.at[back[d], half]
        kc[d] = remote(piece, piece, kc_send.at[d], kc_recv.at[d], sib)
        kc[d].start()
        vx[d].wait_recv()
        vc[d] = remote(v_land.at[d, half], v_land.at[d, half], vc_send.at[d], vc_recv.at[d], sib)
        vc[d].start()
        sx[d].wait_recv()

    def whole(d):
        kc[d].wait_recv()
        vc[d].wait_recv()
        finish(d)

    def over_y(d):
        for n in range(1, len(groups)):
            qz[d][n].wait_recv()
        for s in range(QB):
            q_fore[y, back[d], s] = came[d][slot_of(blocks[s], z, c)]
        for e in FAR:
            piece = q_fore.at[y, back[d]]
            qy[d][e] = remote(piece, piece, y_send.at[d, e], y_recv.at[d, e], at_y[e])
            qy[d][e].start()

    stay[7].wait()
    for d in (0, *FAR):
        if d:
            rx[d].wait_recv()
        for e in FAR:
            piece = q_rest.at[y, back[d]]
            ry[d][e] = remote(piece, piece, t_send.at[d, e], t_recv.at[d, e], at_y[e])
            ry[d][e].start()
    for copy in stay[5:7]:
        copy.wait()
    finish(0)
    hand_over(1)
    hand_over(3)
    over_y(0)
    whole(1)
    over_y(1)
    whole(3)
    over_y(3)
    over_y(2)
    hand_over(2)
    whole(2)
    for d in range(NX):
        for e in FAR:
            for copy in (qy[d][e], ry[d][e]):
                copy.wait_recv()
                copy.wait_send()
    for d in FAR:
        for copy in (qx[d], rx[d], kx[d], vx[d], sx[d], kc[d], vc[d]):
            copy.wait_send()
    for copies in qz:
        for copy in copies[1:]:
            copy.wait_send()


def spread(target, q, k, v, ks, vs, pattern):
    slots = pltpu.VMEM((2 * NZ, ROWS, FORE), BF16)
    return pl.pallas_call(
        spread_kernel,
        out_shape=[
            jax.ShapeDtypeStruct((NY, NX, QB, ROWS, FORE), BF16),
            jax.ShapeDtypeStruct((NY, NX, QB, ROWS, REST), BF16),
            jax.ShapeDtypeStruct((NX, KEYS, D), BF16),
            jax.ShapeDtypeStruct((KB, D, B), BF16),
            jax.ShapeDtypeStruct((KB, 8, 128), F32),
            jax.ShapeDtypeStruct((PAIRS, 128), I32),
        ],
        in_specs=[HBM] * 7,
        out_specs=[VMEM] * 6,
        scratch_shapes=[pltpu.VMEM((QB, ROWS, FORE), BF16)] * NX
        + [pltpu.VMEM((NX, 2 * NZ, ROWS, FORE), BF16)]
        + [slots] * NX
        + [
            pltpu.VMEM((NX, KEYS, D), BF16),
            pltpu.VMEM((NX, 2 * NX, 128), F32),
            pltpu.VMEM((NX, SHARD), F32),
            pltpu.VMEM((NX, SHARD), F32),
            pltpu.VMEM((HEADS, *pattern.shape[1:]), I32),
            pltpu.SMEM(target.shape, I32),
        ]
        + [DMA((NX, 2 * NZ))] * 2
        + [DMA((NX,))] * 4
        + [DMA((NX, NY))] * 4
        + [DMA((NX,))] * 10
        + [DMA((8,))],
        compiler_params=pltpu.CompilerParams(
            collective_id=0, has_side_effects=True, vmem_limit_bytes=24 << 20
        ),
        name="spread",
    )(target, q, k, v, ks, vs, pattern)


def attend_kernel(
    ints, q_fore, q_rest, keys, values, factors, out_fore, out_rest, extra_out,
    qs, sc, mx, acc, su, extra, items,
):
    row = iota((B, B), 1)
    row = ((row >> 3) & 3) * PART + (row >> 5) * ROWS + (row & 7)
    ahead = iota((B, B), 0) - row
    extra[...] = jnp.zeros((B, B), F32)
    qs[HEADS] = jnp.zeros((D, B), BF16)

    def tall(tile):
        return jnp.broadcast_to(tile[None], (B // 8, 8, B)).reshape(B, B)

    @pl.loop(0, QB // TOGETHER)
    def _(part_of):
        def add_pair(r, n):
            def add(t, n):
                items[n] = r * 16 + t
                return n + 1

            return lax.fori_loop(0, (ints[part_of * LANES + r, KB] + 1) // 2, add, n)

        n = lax.fori_loop(0, LANES, add_pair, jnp.int32(0))
        for g in range(STEP):
            items[n + g] = HEADS * 16
        count = (n + STEP - 1) // STEP
        for j in range(TOGETHER):
            for q_ref, low, high in ((q_fore, 0, EARLY), (q_rest, EARLY, HEADS)):
                rows = q_ref[:, :, part_of * TOGETHER + j].astype(F32).reshape(B, (high - low) * D)
                rows = rows.astype(BF16)
                for h in range(low, high):
                    qs[j * 8 + h] = rows[:, (h - low) * D : (h - low + 1) * D].T
        mx[...] = jnp.full(mx.shape, NEG, F32)
        acc[...] = jnp.zeros(acc.shape, F32)
        su[...] = jnp.zeros(su.shape, F32)

        def item_at(i, g):
            item = items[i * STEP + g]
            r, t = item >> 4, item & 15
            codes = [ints[part_of * LANES + r, t * 2 + u] for u in range(2)]
            return r, codes, [code & (KB - 1) for code in codes]

        @pl.loop(0, count)
        def _(i):
            for g in range(STEP):
                r, codes, kbs = item_at(i, g)
                both = jnp.dot(
                    jnp.concatenate([keys[kb] for kb in kbs], axis=0), qs[r], preferred_element_type=F32
                )
                top = mx[r]
                for u in range(2):
                    score = both[u * B : (u + 1) * B] * tall(factors[kbs[u]])
                    score = jnp.where(ahead <= (codes[u] >> 5) * B, score, NEG)
                    sc[(i * STEP + g) * 2 + u] = score
                    top = jnp.maximum(top, jnp.max(score.reshape(B // 8, 8, B), axis=0))
                mx[r] = top

        for j in range(TOGETHER):
            for h in range(HEADS):
                top = jnp.max(mx[j * 8 + h], axis=0, keepdims=True)
                mx[j * 8 + h] = jnp.broadcast_to(top, (8, B)).astype(BF16).astype(F32)

        @pl.loop(0, count)
        def _(i):
            for g in range(STEP):
                r, codes, kbs = item_at(i, g)
                top = tall(mx[r])
                weights = [jnp.exp2(sc[(i * STEP + g) * 2 + u] - top) for u in range(2)]
                su[r] += jnp.sum((weights[0] + weights[1]).reshape(B // 8, 8, B), axis=0)
                acc[r] += jnp.dot(
                    jnp.concatenate([values[kb] for kb in kbs], axis=1),
                    jnp.concatenate([w.astype(BF16) for w in weights], axis=0),
                    preferred_element_type=F32,
                )

        for j in range(TOGETHER):
            for h in range(HEADS):
                r = j * 8 + h
                at = part_of * LANES + r
                extra[pl.ds(at, 1), :] = mx[r][0:1]
                extra[pl.ds(SUM_LANE + at, 1), :] = jnp.sum(su[r], axis=0, keepdims=True)
                part = acc[r].astype(BF16).T
                out, i = (out_fore, h) if h < EARLY else (out_rest, h - EARLY)
                for d in range(NY):
                    out[d, part_of * TOGETHER + j, :, i * D : (i + 1) * D] = part[d * PART : (d + 1) * PART]

    turned = extra[...].T
    for d in range(NY):
        extra_out[d] = turned[d * PART : (d + 1) * PART].astype(BF16)


def attend(lists, q_fore, q_rest, keys, values, factors):
    most = TOGETHER * HEADS * KB // 2 + STEP
    return pl.pallas_call(
        attend_kernel,
        out_shape=[
            jax.ShapeDtypeStruct((NY, QB, PART, FORE), BF16),
            jax.ShapeDtypeStruct((NY, QB, PART, REST), BF16),
            jax.ShapeDtypeStruct((NY, PART, 128), BF16),
        ],
        in_specs=[SMEM] + [VMEM] * 5,
        out_specs=[VMEM] * 3,
        scratch_shapes=[
            pltpu.VMEM((LANES, D, B), BF16),
            pltpu.VMEM((2 * most, B, B), F32),
            pltpu.VMEM((LANES, 8, B), F32),
            pltpu.VMEM((LANES, D, B), F32),
            pltpu.VMEM((LANES, 8, B), F32),
            pltpu.VMEM((B, B), F32),
            pltpu.SMEM((most,), I32),
        ],
        compiler_params=pltpu.CompilerParams(vmem_limit_bytes=46 << 20),
        name="attend",
    )(lists, q_fore, q_rest, keys.reshape(KB, B, D), values, factors)


def gather_kernel(
    target, p, p_rest, extra_in, out,
    parts, parts_rest, extra, att, att_rest, held, packed, came, goes,
    e_send, e_recv, y_send, y_recv, t_send, t_recv, x_send, x_recv, r_send, r_recv, z_send, z_recv, own,
):
    rep, z, c, x, y = place()
    xs = [(x + d) % NX for d in range(NX)]
    back = [(x + NX - d) % NX for d in range(NX)]
    ys = [(y + d) % NY for d in range(NY)]
    at_x = [(rep, xs[d] * NY + y) for d in range(NX)]
    at_y = [(rep, x * NY + ys[d]) for d in range(NY)]
    groups = near_groups(z, c)
    at_group = [(g, x * NY + y) for g in groups]
    partners = at_group[1:] + at_x[1:] + at_y[1:]
    barrier = pltpu.get_barrier_semaphore()
    for who in partners:
        pl.semaphore_signal(barrier, inc=1, device_id=who, device_id_type=MESH)
    told = pltpu.make_async_copy(target, goes, own.at[QB])
    told.start()
    pl.semaphore_wait(barrier, len(partners))

    ex, ty, rx = ([None] * NY for _ in range(3))
    py = [[None] * NY for _ in range(QB)]
    px = [[None] * NX for _ in range(QB)]
    pz = [None] * len(groups)
    for d in FAR:
        ex[d] = remote(extra_in.at[ys[d]], extra.at[d], e_send.at[d], e_recv.at[d], at_y[d])
        ex[d].start()
        ty[d] = remote(p_rest.at[ys[d]], parts_rest.at[d], t_send.at[d], t_recv.at[d], at_y[d])
        ty[d].start()
    for b in range(QB):
        for d in FAR:
            py[b][d] = remote(p.at[ys[d], b], parts.at[d, b], y_send.at[b, d], y_recv.at[b, d], at_y[d])
            py[b][d].start()
    told.wait()
    leaving = blocks_out(goes, rep, groups)
    blocks = blocks_in(goes, rep)
    for d in FAR:
        ex[d].wait_recv()
    marks = [extra_in[y].astype(F32)] + [extra[d].astype(F32) for d in range(1, NY)]
    top = functools.reduce(jnp.maximum, marks)
    shift = [jnp.exp2(e - top) for e in marks]
    total = sum(w * pltpu.roll(e, SUM_LANE, 1) for w, e in zip(shift, marks))
    lane = iota((PART, 128), 1)
    total = jnp.where((lane < QB * 8) & ((lane & 7) < HEADS), total, 1.0)
    ratio = [w / total for w in shift]

    def quotient(b, h, mine, theirs, cols):
        at = b * 8 + h
        value = sum(
            jnp.broadcast_to(ratio[d][:, at : at + 1], (PART, D))
            * (theirs[d, b, :, cols] if d else mine[y, b, :, cols]).astype(F32)
            for d in range(NY)
        )
        return value.reshape(NX, ROWS, D).astype(BF16)

    for d in FAR:
        ty[d].wait_recv()
    for b in range(QB):
        for h in range(EARLY, HEADS):
            cols = slice((h - EARLY) * D, (h - EARLY + 1) * D)
            value = quotient(b, h, p_rest, parts_rest, cols)
            for d in range(NX):
                att_rest[d, b, :, cols] = value[d]
    for d in FAR:
        rx[d] = remote(att_rest.at[xs[d]], held.at[d], r_send.at[d], r_recv.at[d], at_x[d])
        rx[d].start()
    held[0] = att_rest[x]
    mine = pl.ds(pl.multiple_of(x * SLICE, D), FORE)
    for b in range(QB):
        if b == 1:
            for d in FAR:
                rx[d].wait_recv()
            for n in ORDER:
                for d in range(NX):
                    block = held[d, leaving[n]]
                    if n == 0:
                        came[n, d] = block
                    else:
                        packed[n, d] = block
                if n > 0:
                    pz[n] = remote(packed.at[n], came.at[n], z_send.at[n], z_recv.at[n], at_group[n])
                    pz[n].start()
        for d in FAR:
            py[b][d].wait_recv()
        for h in range(EARLY):
            cols = slice(h * D, (h + 1) * D)
            value = quotient(b, h, p, parts, cols)
            for d in range(NX):
                att[b, d, :, cols] = value[d]
        for d in FAR:
            px[b][d] = remote(
                att.at[b, xs[d]], out.at[b, :, mine], x_send.at[b, d], x_recv.at[b, d], at_x[d]
            )
            px[b][d].start()
        px[b][0] = pltpu.make_async_copy(att.at[b, x], out.at[b, :, mine], own.at[b])
        px[b][0].start()

    for n in range(1, len(groups)):
        pz[n].wait_recv()
    for b in range(QB):
        px[b][0].wait()
        for d in FAR:
            px[b][d].wait_recv()
    for s in range(QB):
        n = slot_of(blocks[s], z, c)
        for d in range(NX):
            out[s, :, pl.ds(pl.multiple_of(back[d] * SLICE + FORE, D), REST)] = came[n, d]

    for n in range(1, len(groups)):
        pz[n].wait_send()
    for d in FAR:
        for copy in (ex[d], ty[d], rx[d]):
            copy.wait_send()
        for b in range(QB):
            px[b][d].wait_send()
            py[b][d].wait_send()


def gather(target, p, p_rest, extra):
    slots = pltpu.VMEM((2 * NZ, NX, ROWS, REST), BF16)
    return pl.pallas_call(
        gather_kernel,
        out_shape=jax.ShapeDtypeStruct((QB, ROWS, NX * SLICE), BF16),
        in_specs=[HBM, VMEM, VMEM, VMEM],
        out_specs=VMEM,
        scratch_shapes=[
            pltpu.VMEM((NY, QB, PART, FORE), BF16),
            pltpu.VMEM((NY, QB, PART, REST), BF16),
            pltpu.VMEM((NY, PART, 128), BF16),
            pltpu.VMEM((QB, NX, ROWS, FORE), BF16),
            pltpu.VMEM((NX, QB, ROWS, REST), BF16),
            pltpu.VMEM((NX, QB, ROWS, REST), BF16),
            slots,
            slots,
            pltpu.SMEM(target.shape, I32),
        ]
        + [DMA((NY,))] * 2
        + [DMA((QB, NY))] * 2
        + [DMA((NY,))] * 2
        + [DMA((QB, NX))] * 2
        + [DMA((NX,))] * 2
        + [DMA((2 * NZ,))] * 2
        + [DMA((QB + 1,))],
        compiler_params=pltpu.CompilerParams(
            collective_id=1, has_side_effects=True, vmem_limit_bytes=16 << 20
        ),
        name="gather",
    )(target, p, p_rest, extra)


def hbm(array):
    return pltpu.with_memory_space_constraint(array, pltpu.HBM)


def per_device(queries, key_cache, value_cache, key_scale, value_scale, pattern, target):
    target = hbm(target)
    q_fore, q_rest, keys, values, factors, lists = spread(
        target,
        hbm(queries),
        hbm(key_cache),
        hbm(value_cache),
        hbm(key_scale.T),
        hbm(value_scale.T),
        hbm(jnp.swapaxes(pattern, 1, 2)),
    )
    part, rest, extra = attend(lists, q_fore, q_rest, keys, values, factors)
    return gather(target, part, rest, extra)


def solution(mesh):
    return jax.shard_map(
        per_device,
        mesh=mesh,
        in_specs=(
            P("replica", "ctx", None),
            P("ctx", None),
            P("ctx", None),
            P("ctx", None),
            P("ctx", None),
            P(),
            P(),
        ),
        out_specs=P("replica", "ctx", None),
        check_vma=False,
    )
```

```python
import functools
import math

import jax
import jax.numpy as jnp
from jax import lax
from jax.experimental import pallas as pl
from jax.experimental.pallas import tpu as pltpu
from jax.sharding import PartitionSpec as P

MESH = pl.DeviceIdType.MESH
BF16 = jnp.bfloat16
F32 = jnp.float32
I32 = jnp.int32

NX = 4
NY = 4
NZ = 8
HEADS = 7
D = 128
B = 128
QB = 4
KB = 32
SHARD = 8
SLICE = HEADS * D
EARLY = 5
FORE = EARLY * D
REST = SLICE - FORE
ROWS = B // (NX * NY)
PART = NX * ROWS
KEYS = SHARD * B
PAIRS = 32
SUM_LANE = 64
NEG = -(2.0**100)
STEP = 24
TOGETHER = 2
LANES = 8 * TOGETHER
FIRST = 64
FAR = (1, 3, 2)
ORDER = (8, 9, 6, 7, 10, 11, 4, 5, 12, 13, 2, 3, 14, 15, 1, 0)
TO_LOG2 = math.log2(math.e) / math.sqrt(D)

DMA = pltpu.SemaphoreType.DMA
HBM = pl.BlockSpec(memory_space=pltpu.HBM)
VMEM = pl.BlockSpec(memory_space=pltpu.VMEM)
SMEM = pl.BlockSpec(memory_space=pltpu.SMEM)


def place():
    rep = lax.axis_index("replica")
    ctx = lax.axis_index("ctx")
    return rep, rep // 2, rep % 2, ctx // NY, ctx % NY


def remote(src, dst, send, recv, who):
    return pltpu.make_async_remote_copy(
        src_ref=src, dst_ref=dst, send_sem=send, recv_sem=recv, device_id=who, device_id_type=MESH
    )


def iota(shape, dim):
    return lax.broadcasted_iota(I32, shape, dim)


def block_lists(listed, blocks, rep, y):
    shape = (PAIRS, 128)
    lane, row = iota(shape, 1), iota(shape, 0)
    block = (lane >> 3) * (SHARD * NY) + y * SHARD + (lane & 7)
    hits = jnp.zeros(shape, I32)
    own = jnp.zeros(shape, I32)
    column = iota(listed.shape[1:], 1)
    for s in range(QB):
        own = jnp.where(row >> 3 == s, jnp.where((row & 7) < EARLY, blocks[s], rep * QB + s), own)
        for h in range(HEADS):
            of = blocks[s] if h < EARLY else rep * QB + s
            entry = jnp.max(jnp.where(column == of, listed[h], -1), axis=1, keepdims=True)
            found = (jnp.broadcast_to(entry, shape) == block).astype(I32)
            found = jnp.max(found, axis=0, keepdims=True)
            hits = jnp.where(row == s * 8 + h, found, hits)
    below = FIRST + own - block
    hits = jnp.where(below == 0, 1, hits)
    hits = jnp.where((below >= 0) & (lane < KB) & ((row & 7) < HEADS), hits, 0)
    upto = hits
    for s in (1, 2, 4, 8, 16):
        upto = upto + jnp.where(lane >= s, pltpu.roll(upto, s, 1), 0)
    slot = jnp.where(hits > 0, upto - 1, -1)
    code = lane + KB * below
    packed = jnp.full(shape, -KB * 1024, I32)
    for b in range(KB):
        at = jnp.broadcast_to(slot[:, b : b + 1], shape) == lane
        packed = jnp.where(at, jnp.broadcast_to(code[:, b : b + 1], shape), packed)
    number = jnp.broadcast_to(upto[:, KB - 1 : KB], shape)
    return jnp.where(lane == KB, number, packed)


def near_groups(z, c):
    return [((z + d) % NZ) * 2 + (c + e) % 2 for d in range(NZ) for e in range(2)]


def slot_of(block, z, c):
    source = block >> 2
    return (((z + NZ - (source >> 1)) & (NZ - 1)) << 1) + ((source & 1) ^ c)


def blocks_out(goes, rep, groups):
    goes_to = [goes[rep * QB + b] for b in range(QB)]
    leaving = []
    for group in groups:
        b = jnp.int32(0)
        for other in range(1, QB):
            b = jnp.where(goes_to[other] == group, other, b)
        leaving.append(b)
    return leaving


def blocks_in(goes, rep):
    def look(j, state):
        found, *at = state
        hit = goes[j] == rep
        at = [jnp.where(hit & (found == s), j, a) for s, a in enumerate(at)]
        return (found + hit.astype(I32), *at)

    _, *blocks = lax.fori_loop(0, 2 * NZ * QB, look, (jnp.int32(0),) * (1 + QB))
    return blocks


def spread_kernel(
    target, q, k, v, ks, vs, pattern,
    q_fore, q_rest, keys, values, factors, lists,
    held0, held1, held2, held3, packed, came0, came1, came2, came3,
    v_land, scales, k_loc, v_loc, listed, goes,
    z_send, z_recv, q_send, q_recv, r_send, r_recv, y_send, y_recv, t_send, t_recv, k_send, k_recv, v_send, v_recv, s_send, s_recv,
    kc_send, kc_recv, vc_send, vc_recv, own,
):
    rep, z, c, x, y = place()
    sib = (rep + 1 - 2 * c, x * NY + y)
    xs = [(x + d) % NX for d in range(NX)]
    back = [(x + NX - d) % NX for d in range(NX)]
    at_x = [(rep, xs[d] * NY + y) for d in range(NX)]
    at_y = [(rep, x * NY + (y + d) % NY) for d in range(NY)]
    half = pl.ds(pl.multiple_of(c * (KEYS // 2), KEYS // 2), KEYS // 2)
    groups = near_groups(z, c)
    at_group = [(g, x * NY + y) for g in groups]
    held = (held0, held1, held2, held3)
    came = (came0, came1, came2, came3)

    def cols(d, n):
        return pl.ds(pl.multiple_of(xs[d] * n, n), n)

    def fore(d):
        return q.at[:, :, pl.ds(pl.multiple_of(xs[d] * SLICE, D), FORE)]

    def rest(d):
        return q.at[:, :, pl.ds(pl.multiple_of(xs[d] * SLICE + FORE, D), REST)]

    partners = at_group[1:] + at_x[1:] + at_y[1:]
    barrier = pltpu.get_barrier_semaphore()
    for who in partners:
        pl.semaphore_signal(barrier, inc=1, device_id=who, device_id_type=MESH)
    stay = [
        pltpu.make_async_copy(target, goes, own.at[0]),
        pltpu.make_async_copy(fore(0), held[0], own.at[1]),
        pltpu.make_async_copy(ks, k_loc, own.at[2]),
        pltpu.make_async_copy(vs, v_loc, own.at[3]),
        pltpu.make_async_copy(pattern.at[pl.ds(x * HEADS, HEADS)], listed, own.at[4]),
        pltpu.make_async_copy(k.at[:, cols(0, D)], keys.at[x], own.at[5]),
        pltpu.make_async_copy(v.at[:, cols(0, D)], v_land.at[0], own.at[6]),
        pltpu.make_async_copy(rest(0), q_rest.at[y, x], own.at[7]),
    ]
    for copy in stay:
        copy.start()

    qx, rx, kx, vx, sx, kc, vc = ([None] * NX for _ in range(7))
    qy, ry = ([[None] * NY for _ in range(NX)] for _ in range(2))
    qz = [[None] * len(groups) for _ in range(NX)]

    stay[0].wait()
    leaving = blocks_out(goes, rep, groups)

    def pack(d):
        for n in ORDER:
            block = held[d][leaving[n]]
            if n == 0:
                came[d][n] = block
            else:
                packed[d, n] = block

    def over_z(d):
        for n in ORDER[:-1]:
            qz[d][n] = remote(packed.at[d, n], came[d].at[n], z_send.at[d, n], z_recv.at[d, n], at_group[n])
            qz[d][n].start()

    stay[1].wait()
    pack(0)
    scales[0] = jnp.zeros((2 * NX, 128), F32)
    stay[2].wait()
    stay[3].wait()
    scales[0, 0:NX, 0:SHARD] = k_loc[...]
    scales[0, NX : 2 * NX, 0:SHARD] = v_loc[...]

    pl.semaphore_wait(barrier, len(partners))
    for d in FAR:
        qx[d] = remote(fore(d), held[d], q_send.at[d], q_recv.at[d], at_x[d])
        qx[d].start()
    over_z(0)
    for d in FAR:
        rx[d] = remote(rest(d), q_rest.at[y, x], r_send.at[d], r_recv.at[d], at_x[d])
        rx[d].start()
    for d in FAR:
        sx[d] = remote(scales.at[0], scales.at[d], s_send.at[d], s_recv.at[d], at_x[d])
        sx[d].start()
    for d in FAR:
        kx[d] = remote(k.at[half, cols(d, D)], keys.at[x, half], k_send.at[d], k_recv.at[d], at_x[d])
        vx[d] = remote(v.at[half, cols(d, D)], v_land.at[d, half], v_send.at[d], v_recv.at[d], at_x[d])
        kx[d].start()
        vx[d].start()

    for d in FAR:
        qx[d].wait_recv()
        pack(d)
        over_z(d)
    blocks = blocks_in(goes, rep)

    stay[4].wait()
    lists[...] = block_lists(listed, blocks, rep, y)

    scale_row = iota((2 * NX, 128), 0)

    def pick_row(tile, n):
        return jnp.sum(jnp.where(scale_row == n, tile, 0.0), axis=0, keepdims=True)

    def finish(d):
        tile = scales[d]
        for_keys = pick_row(tile, x) * TO_LOG2
        for_values = pick_row(tile, NX + x)
        for b in range(SHARD):
            at = back[d] * SHARD + b
            factors[at] = jnp.broadcast_to(for_keys[:, b : b + 1], (8, 128))
            rows = slice(b * B, (b + 1) * B)
            scaled = v_land[d, rows].astype(F32) * jnp.broadcast_to(for_values[:, b : b + 1], (B, D))
            values[at] = scaled.astype(BF16).T

    def hand_over(d):
        kx[d].wait_recv()
        piece = keys.at[back[d], half]
        kc[d] = remote(piece, piece, kc_send.at[d], kc_recv.at[d], sib)
        kc[d].start()
        vx[d].wait_recv()
        vc[d] = remote(v_land.at[d, half], v_land.at[d, half], vc_send.at[d], vc_recv.at[d], sib)
        vc[d].start()
        sx[d].wait_recv()

    def whole(d):
        kc[d].wait_recv()
        vc[d].wait_recv()
        finish(d)

    def over_y(d):
        for n in range(1, len(groups)):
            qz[d][n].wait_recv()
        for s in range(QB):
            q_fore[y, back[d], s] = came[d][slot_of(blocks[s], z, c)]
        for e in FAR:
            piece = q_fore.at[y, back[d]]
            qy[d][e] = remote(piece, piece, y_send.at[d, e], y_recv.at[d, e], at_y[e])
            qy[d][e].start()

    stay[7].wait()
    for d in (0, *FAR):
        if d:
            rx[d].wait_recv()
        for e in FAR:
            piece = q_rest.at[y, back[d]]
            ry[d][e] = remote(piece, piece, t_send.at[d, e], t_recv.at[d, e], at_y[e])
            ry[d][e].start()
    for copy in stay[5:7]:
        copy.wait()
    finish(0)
    hand_over(1)
    hand_over(3)
    over_y(0)
    whole(1)
    over_y(1)
    whole(3)
    over_y(3)
    over_y(2)
    hand_over(2)
    whole(2)
    for d in range(NX):
        for e in FAR:
            for copy in (qy[d][e], ry[d][e]):
                copy.wait_recv()
                copy.wait_send()
    for d in FAR:
        for copy in (qx[d], rx[d], kx[d], vx[d], sx[d], kc[d], vc[d]):
            copy.wait_send()
    for copies in qz:
        for copy in copies[1:]:
            copy.wait_send()


def spread(target, q, k, v, ks, vs, pattern):
    slots = pltpu.VMEM((2 * NZ, ROWS, FORE), BF16)
    return pl.pallas_call(
        spread_kernel,
        out_shape=[
            jax.ShapeDtypeStruct((NY, NX, QB, ROWS, FORE), BF16),
            jax.ShapeDtypeStruct((NY, NX, QB, ROWS, REST), BF16),
            jax.ShapeDtypeStruct((NX, KEYS, D), BF16),
            jax.ShapeDtypeStruct((KB, D, B), BF16),
            jax.ShapeDtypeStruct((KB, 8, 128), F32),
            jax.ShapeDtypeStruct((PAIRS, 128), I32),
        ],
        in_specs=[HBM] * 7,
        out_specs=[VMEM] * 6,
        scratch_shapes=[pltpu.VMEM((QB, ROWS, FORE), BF16)] * NX
        + [pltpu.VMEM((NX, 2 * NZ, ROWS, FORE), BF16)]
        + [slots] * NX
        + [
            pltpu.VMEM((NX, KEYS, D), BF16),
            pltpu.VMEM((NX, 2 * NX, 128), F32),
            pltpu.VMEM((NX, SHARD), F32),
            pltpu.VMEM((NX, SHARD), F32),
            pltpu.VMEM((HEADS, *pattern.shape[1:]), I32),
            pltpu.SMEM(target.shape, I32),
        ]
        + [DMA((NX, 2 * NZ))] * 2
        + [DMA((NX,))] * 4
        + [DMA((NX, NY))] * 4
        + [DMA((NX,))] * 10
        + [DMA((8,))],
        compiler_params=pltpu.CompilerParams(
            collective_id=0, has_side_effects=True, vmem_limit_bytes=24 << 20
        ),
        name="spread",
    )(target, q, k, v, ks, vs, pattern)


def attend_kernel(
    ints, q_fore, q_rest, keys, values, factors, out_fore, out_rest, extra_out,
    qs, sc, mx, acc, su, extra, items,
):
    row = iota((B, B), 1)
    row = ((row >> 3) & 3) * PART + (row >> 5) * ROWS + (row & 7)
    ahead = iota((B, B), 0) - row
    extra[...] = jnp.zeros((B, B), F32)
    qs[HEADS] = jnp.zeros((D, B), BF16)

    def tall(tile):
        return jnp.broadcast_to(tile[None], (B // 8, 8, B)).reshape(B, B)

    @pl.loop(0, QB // TOGETHER)
    def _(part_of):
        def add_pair(r, n):
            def add(t, n):
                items[n] = r * 16 + t
                return n + 1

            return lax.fori_loop(0, (ints[part_of * LANES + r, KB] + 1) // 2, add, n)

        n = lax.fori_loop(0, LANES, add_pair, jnp.int32(0))
        for g in range(STEP):
            items[n + g] = HEADS * 16
        count = (n + STEP - 1) // STEP
        for j in range(TOGETHER):
            for q_ref, low, high in ((q_fore, 0, EARLY), (q_rest, EARLY, HEADS)):
                rows = q_ref[:, :, part_of * TOGETHER + j].astype(F32).reshape(B, (high - low) * D)
                rows = rows.astype(BF16)
                for h in range(low, high):
                    qs[j * 8 + h] = rows[:, (h - low) * D : (h - low + 1) * D].T
        mx[...] = jnp.full(mx.shape, NEG, F32)
        acc[...] = jnp.zeros(acc.shape, F32)
        su[...] = jnp.zeros(su.shape, F32)

        def item_at(i, g):
            item = items[i * STEP + g]
            r, t = item >> 4, item & 15
            codes = [ints[part_of * LANES + r, t * 2 + u] for u in range(2)]
            return r, codes, [code & (KB - 1) for code in codes]

        @pl.loop(0, count)
        def _(i):
            for g in range(STEP):
                r, codes, kbs = item_at(i, g)
                both = jnp.dot(
                    jnp.concatenate([keys[kb] for kb in kbs], axis=0), qs[r], preferred_element_type=F32
                )
                top = mx[r]
                for u in range(2):
                    score = both[u * B : (u + 1) * B] * tall(factors[kbs[u]])
                    score = jnp.where(ahead <= (codes[u] >> 5) * B, score, NEG)
                    sc[(i * STEP + g) * 2 + u] = score
                    top = jnp.maximum(top, jnp.max(score.reshape(B // 8, 8, B), axis=0))
                mx[r] = top

        for j in range(TOGETHER):
            for h in range(HEADS):
                top = jnp.max(mx[j * 8 + h], axis=0, keepdims=True)
                mx[j * 8 + h] = jnp.broadcast_to(top, (8, B)).astype(BF16).astype(F32)

        @pl.loop(0, count)
        def _(i):
            for g in range(STEP):
                r, codes, kbs = item_at(i, g)
                top = tall(mx[r])
                weights = [jnp.exp2(sc[(i * STEP + g) * 2 + u] - top) for u in range(2)]
                su[r] += jnp.sum((weights[0] + weights[1]).reshape(B // 8, 8, B), axis=0)
                acc[r] += jnp.dot(
                    jnp.concatenate([values[kb] for kb in kbs], axis=1),
                    jnp.concatenate([w.astype(BF16) for w in weights], axis=0),
                    preferred_element_type=F32,
                )

        for j in range(TOGETHER):
            for h in range(HEADS):
                r = j * 8 + h
                at = part_of * LANES + r
                extra[pl.ds(at, 1), :] = mx[r][0:1]
                extra[pl.ds(SUM_LANE + at, 1), :] = jnp.sum(su[r], axis=0, keepdims=True)
                part = acc[r].astype(BF16).T
                out, i = (out_fore, h) if h < EARLY else (out_rest, h - EARLY)
                for d in range(NY):
                    out[d, part_of * TOGETHER + j, :, i * D : (i + 1) * D] = part[d * PART : (d + 1) * PART]

    turned = extra[...].T
    for d in range(NY):
        extra_out[d] = turned[d * PART : (d + 1) * PART].astype(BF16)


def attend(lists, q_fore, q_rest, keys, values, factors):
    most = TOGETHER * HEADS * KB // 2 + STEP
    return pl.pallas_call(
        attend_kernel,
        out_shape=[
            jax.ShapeDtypeStruct((NY, QB, PART, FORE), BF16),
            jax.ShapeDtypeStruct((NY, QB, PART, REST), BF16),
            jax.ShapeDtypeStruct((NY, PART, 128), BF16),
        ],
        in_specs=[SMEM] + [VMEM] * 5,
        out_specs=[VMEM] * 3,
        scratch_shapes=[
            pltpu.VMEM((LANES, D, B), BF16),
            pltpu.VMEM((2 * most, B, B), F32),
            pltpu.VMEM((LANES, 8, B), F32),
            pltpu.VMEM((LANES, D, B), F32),
            pltpu.VMEM((LANES, 8, B), F32),
            pltpu.VMEM((B, B), F32),
            pltpu.SMEM((most,), I32),
        ],
        compiler_params=pltpu.CompilerParams(vmem_limit_bytes=46 << 20),
        name="attend",
    )(lists, q_fore, q_rest, keys.reshape(KB, B, D), values, factors)


def gather_kernel(
    target, p, p_rest, extra_in, out,
    parts, parts_rest, extra, att, att_rest, held, packed, came, goes,
    e_send, e_recv, y_send, y_recv, t_send, t_recv, x_send, x_recv, r_send, r_recv, z_send, z_recv, own,
):
    rep, z, c, x, y = place()
    xs = [(x + d) % NX for d in range(NX)]
    back = [(x + NX - d) % NX for d in range(NX)]
    ys = [(y + d) % NY for d in range(NY)]
    at_x = [(rep, xs[d] * NY + y) for d in range(NX)]
    at_y = [(rep, x * NY + ys[d]) for d in range(NY)]
    groups = near_groups(z, c)
    at_group = [(g, x * NY + y) for g in groups]
    partners = at_group[1:] + at_x[1:] + at_y[1:]
    barrier = pltpu.get_barrier_semaphore()
    for who in partners:
        pl.semaphore_signal(barrier, inc=1, device_id=who, device_id_type=MESH)
    told = pltpu.make_async_copy(target, goes, own.at[QB])
    told.start()
    pl.semaphore_wait(barrier, len(partners))

    ex, ty, rx = ([None] * NY for _ in range(3))
    py = [[None] * NY for _ in range(QB)]
    px = [[None] * NX for _ in range(QB)]
    pz = [None] * len(groups)
    for d in FAR:
        ex[d] = remote(extra_in.at[ys[d]], extra.at[d], e_send.at[d], e_recv.at[d], at_y[d])
        ex[d].start()
        ty[d] = remote(p_rest.at[ys[d]], parts_rest.at[d], t_send.at[d], t_recv.at[d], at_y[d])
        ty[d].start()
    for b in range(QB):
        for d in FAR:
            py[b][d] = remote(p.at[ys[d], b], parts.at[d, b], y_send.at[b, d], y_recv.at[b, d], at_y[d])
            py[b][d].start()
    told.wait()
    leaving = blocks_out(goes, rep, groups)
    blocks = blocks_in(goes, rep)
    for d in FAR:
        ex[d].wait_recv()
    marks = [extra_in[y].astype(F32)] + [extra[d].astype(F32) for d in range(1, NY)]
    top = functools.reduce(jnp.maximum, marks)
    shift = [jnp.exp2(e - top) for e in marks]
    total = sum(w * pltpu.roll(e, SUM_LANE, 1) for w, e in zip(shift, marks))
    lane = iota((PART, 128), 1)
    total = jnp.where((lane < QB * 8) & ((lane & 7) < HEADS), total, 1.0)
    ratio = [w / total for w in shift]

    def quotient(b, h, mine, theirs, cols):
        at = b * 8 + h
        value = sum(
            jnp.broadcast_to(ratio[d][:, at : at + 1], (PART, D))
            * (theirs[d, b, :, cols] if d else mine[y, b, :, cols]).astype(F32)
            for d in range(NY)
        )
        return value.reshape(NX, ROWS, D).astype(BF16)

    for d in FAR:
        ty[d].wait_recv()
    for b in range(QB):
        for h in range(EARLY, HEADS):
            cols = slice((h - EARLY) * D, (h - EARLY + 1) * D)
            value = quotient(b, h, p_rest, parts_rest, cols)
            for d in range(NX):
                att_rest[d, b, :, cols] = value[d]
    for d in FAR:
        rx[d] = remote(att_rest.at[xs[d]], held.at[d], r_send.at[d], r_recv.at[d], at_x[d])
        rx[d].start()
    held[0] = att_rest[x]
    mine = pl.ds(pl.multiple_of(x * SLICE, D), FORE)
    for b in range(QB):
        if b == 1:
            for d in FAR:
                rx[d].wait_recv()
            for n in ORDER:
                for d in range(NX):
                    block = held[d, leaving[n]]
                    if n == 0:
                        came[n, d] = block
                    else:
                        packed[n, d] = block
                if n > 0:
                    pz[n] = remote(packed.at[n], came.at[n], z_send.at[n], z_recv.at[n], at_group[n])
                    pz[n].start()
        for d in FAR:
            py[b][d].wait_recv()
        for h in range(EARLY):
            cols = slice(h * D, (h + 1) * D)
            value = quotient(b, h, p, parts, cols)
            for d in range(NX):
                att[b, d, :, cols] = value[d]
        for d in FAR:
            px[b][d] = remote(
                att.at[b, xs[d]], out.at[b, :, mine], x_send.at[b, d], x_recv.at[b, d], at_x[d]
            )
            px[b][d].start()
        px[b][0] = pltpu.make_async_copy(att.at[b, x], out.at[b, :, mine], own.at[b])
        px[b][0].start()

    for n in range(1, len(groups)):
        pz[n].wait_recv()
    for b in range(QB):
        px[b][0].wait()
        for d in FAR:
            px[b][d].wait_recv()
    for s in range(QB):
        n = slot_of(blocks[s], z, c)
        for d in range(NX):
            out[s, :, pl.ds(pl.multiple_of(back[d] * SLICE + FORE, D), REST)] = came[n, d]

    for n in range(1, len(groups)):
        pz[n].wait_send()
    for d in FAR:
        for copy in (ex[d], ty[d], rx[d]):
            copy.wait_send()
        for b in range(QB):
            px[b][d].wait_send()
            py[b][d].wait_send()


def gather(target, p, p_rest, extra):
    slots = pltpu.VMEM((2 * NZ, NX, ROWS, REST), BF16)
    return pl.pallas_call(
        gather_kernel,
        out_shape=jax.ShapeDtypeStruct((QB, ROWS, NX * SLICE), BF16),
        in_specs=[HBM, VMEM, VMEM, VMEM],
        out_specs=VMEM,
        scratch_shapes=[
            pltpu.VMEM((NY, QB, PART, FORE), BF16),
            pltpu.VMEM((NY, QB, PART, REST), BF16),
            pltpu.VMEM((NY, PART, 128), BF16),
            pltpu.VMEM((QB, NX, ROWS, FORE), BF16),
            pltpu.VMEM((NX, QB, ROWS, REST), BF16),
            pltpu.VMEM((NX, QB, ROWS, REST), BF16),
            slots,
            slots,
            pltpu.SMEM(target.shape, I32),
        ]
        + [DMA((NY,))] * 2
        + [DMA((QB, NY))] * 2
        + [DMA((NY,))] * 2
        + [DMA((QB, NX))] * 2
        + [DMA((NX,))] * 2
        + [DMA((2 * NZ,))] * 2
        + [DMA((QB + 1,))],
        compiler_params=pltpu.CompilerParams(
            collective_id=1, has_side_effects=True, vmem_limit_bytes=16 << 20
        ),
        name="gather",
    )(target, p, p_rest, extra)


def hbm(array):
    return pltpu.with_memory_space_constraint(array, pltpu.HBM)


def per_device(queries, key_cache, value_cache, key_scale, value_scale, pattern, target):
    target = hbm(target)
    q_fore, q_rest, keys, values, factors, lists = spread(
        target,
        hbm(queries),
        hbm(key_cache),
        hbm(value_cache),
        hbm(key_scale.T),
        hbm(value_scale.T),
        hbm(jnp.swapaxes(pattern, 1, 2)),
    )
    part, rest, extra = attend(lists, q_fore, q_rest, keys, values, factors)
    return gather(target, part, rest, extra)


def solution(mesh):
    return jax.shard_map(
        per_device,
        mesh=mesh,
        in_specs=(
            P("replica", "ctx", None),
            P("ctx", None),
            P("ctx", None),
            P("ctx", None),
            P("ctx", None),
            P(),
            P(),
        ),
        out_specs=P("replica", "ctx", None),
        check_vma=False,
    )
```

```python
import functools
import math

import jax
import jax.numpy as jnp
from jax import lax
from jax.experimental import pallas as pl
from jax.experimental.pallas import tpu as pltpu
from jax.sharding import PartitionSpec as P

MESH = pl.DeviceIdType.MESH
BF16 = jnp.bfloat16
F32 = jnp.float32
I32 = jnp.int32

NX = 4
NY = 4
NZ = 8
HEADS = 7
D = 128
B = 128
QB = 4
KB = 32
SHARD = 8
SLICE = HEADS * D
EARLY = 5
FORE = EARLY * D
REST = SLICE - FORE
ROWS = B // (NX * NY)
PART = NX * ROWS
KEYS = SHARD * B
PAIRS = 32
SUM_LANE = 64
NEG = -(2.0**100)
STEP = 32
TOGETHER = 2
LANES = 8 * TOGETHER
FIRST = 64
FAR = (1, 3, 2)
ORDER = (8, 9, 6, 7, 10, 11, 4, 5, 12, 13, 2, 3, 14, 15, 1, 0)
TO_LOG2 = math.log2(math.e) / math.sqrt(D)

DMA = pltpu.SemaphoreType.DMA
HBM = pl.BlockSpec(memory_space=pltpu.HBM)
VMEM = pl.BlockSpec(memory_space=pltpu.VMEM)
SMEM = pl.BlockSpec(memory_space=pltpu.SMEM)


def place():
    rep = lax.axis_index("replica")
    ctx = lax.axis_index("ctx")
    return rep, rep // 2, rep % 2, ctx // NY, ctx % NY


def remote(src, dst, send, recv, who):
    return pltpu.make_async_remote_copy(
        src_ref=src, dst_ref=dst, send_sem=send, recv_sem=recv, device_id=who, device_id_type=MESH
    )


def iota(shape, dim):
    return lax.broadcasted_iota(I32, shape, dim)


def block_lists(listed, blocks, rep, y):
    shape = (PAIRS, 128)
    lane, row = iota(shape, 1), iota(shape, 0)
    block = (lane >> 3) * (SHARD * NY) + y * SHARD + (lane & 7)
    hits = jnp.zeros(shape, I32)
    own = jnp.zeros(shape, I32)
    column = iota(listed.shape[1:], 1)
    for s in range(QB):
        own = jnp.where(row >> 3 == s, jnp.where((row & 7) < EARLY, blocks[s], rep * QB + s), own)
        for h in range(HEADS):
            of = blocks[s] if h < EARLY else rep * QB + s
            entry = jnp.max(jnp.where(column == of, listed[h], -1), axis=1, keepdims=True)
            found = (jnp.broadcast_to(entry, shape) == block).astype(I32)
            found = jnp.max(found, axis=0, keepdims=True)
            hits = jnp.where(row == s * 8 + h, found, hits)
    below = FIRST + own - block
    hits = jnp.where(below == 0, 1, hits)
    hits = jnp.where((below >= 0) & (lane < KB) & ((row & 7) < HEADS), hits, 0)
    upto = hits
    for s in (1, 2, 4, 8, 16):
        upto = upto + jnp.where(lane >= s, pltpu.roll(upto, s, 1), 0)
    slot = jnp.where(hits > 0, upto - 1, -1)
    code = lane + KB * below
    packed = jnp.full(shape, -KB * 1024, I32)
    for b in range(KB):
        at = jnp.broadcast_to(slot[:, b : b + 1], shape) == lane
        packed = jnp.where(at, jnp.broadcast_to(code[:, b : b + 1], shape), packed)
    number = jnp.broadcast_to(upto[:, KB - 1 : KB], shape)
    return jnp.where(lane == KB, number, packed)


def near_groups(z, c):
    return [((z + d) % NZ) * 2 + (c + e) % 2 for d in range(NZ) for e in range(2)]


def slot_of(block, z, c):
    source = block >> 2
    return (((z + NZ - (source >> 1)) & (NZ - 1)) << 1) + ((source & 1) ^ c)


def blocks_out(goes, rep, groups):
    goes_to = [goes[rep * QB + b] for b in range(QB)]
    leaving = []
    for group in groups:
        b = jnp.int32(0)
        for other in range(1, QB):
            b = jnp.where(goes_to[other] == group, other, b)
        leaving.append(b)
    return leaving


def blocks_in(goes, rep):
    def look(j, state):
        found, *at = state
        hit = goes[j] == rep
        at = [jnp.where(hit & (found == s), j, a) for s, a in enumerate(at)]
        return (found + hit.astype(I32), *at)

    _, *blocks = lax.fori_loop(0, 2 * NZ * QB, look, (jnp.int32(0),) * (1 + QB))
    return blocks


def spread_kernel(
    target, q, k, v, ks, vs, pattern,
    q_fore, q_rest, keys, values, factors, lists,
    held0, held1, held2, held3, packed, came0, came1, came2, came3,
    v_land, scales, k_loc, v_loc, listed, goes,
    z_send, z_recv, q_send, q_recv, r_send, r_recv, y_send, y_recv, t_send, t_recv, k_send, k_recv, v_send, v_recv, s_send, s_recv,
    kc_send, kc_recv, vc_send, vc_recv, own,
):
    rep, z, c, x, y = place()
    sib = (rep + 1 - 2 * c, x * NY + y)
    xs = [(x + d) % NX for d in range(NX)]
    back = [(x + NX - d) % NX for d in range(NX)]
    at_x = [(rep, xs[d] * NY + y) for d in range(NX)]
    at_y = [(rep, x * NY + (y + d) % NY) for d in range(NY)]
    half = pl.ds(pl.multiple_of(c * (KEYS // 2), KEYS // 2), KEYS // 2)
    groups = near_groups(z, c)
    at_group = [(g, x * NY + y) for g in groups]
    held = (held0, held1, held2, held3)
    came = (came0, came1, came2, came3)

    def cols(d, n):
        return pl.ds(pl.multiple_of(xs[d] * n, n), n)

    def fore(d):
        return q.at[:, :, pl.ds(pl.multiple_of(xs[d] * SLICE, D), FORE)]

    def rest(d):
        return q.at[:, :, pl.ds(pl.multiple_of(xs[d] * SLICE + FORE, D), REST)]

    partners = at_group[1:] + at_x[1:] + at_y[1:]
    barrier = pltpu.get_barrier_semaphore()
    for who in partners:
        pl.semaphore_signal(barrier, inc=1, device_id=who, device_id_type=MESH)
    stay = [
        pltpu.make_async_copy(target, goes, own.at[0]),
        pltpu.make_async_copy(fore(0), held[0], own.at[1]),
        pltpu.make_async_copy(ks, k_loc, own.at[2]),
        pltpu.make_async_copy(vs, v_loc, own.at[3]),
        pltpu.make_async_copy(pattern.at[pl.ds(x * HEADS, HEADS)], listed, own.at[4]),
        pltpu.make_async_copy(k.at[:, cols(0, D)], keys.at[x], own.at[5]),
        pltpu.make_async_copy(v.at[:, cols(0, D)], v_land.at[0], own.at[6]),
        pltpu.make_async_copy(rest(0), q_rest.at[y, x], own.at[7]),
    ]
    for copy in stay:
        copy.start()

    qx, rx, kx, vx, sx, kc, vc = ([None] * NX for _ in range(7))
    qy, ry = ([[None] * NY for _ in range(NX)] for _ in range(2))
    qz = [[None] * len(groups) for _ in range(NX)]

    stay[0].wait()
    leaving = blocks_out(goes, rep, groups)

    def pack(d):
        for n in ORDER:
            block = held[d][leaving[n]]
            if n == 0:
                came[d][n] = block
            else:
                packed[d, n] = block

    def over_z(d):
        for n in ORDER[:-1]:
            qz[d][n] = remote(packed.at[d, n], came[d].at[n], z_send.at[d, n], z_recv.at[d, n], at_group[n])
            qz[d][n].start()

    stay[1].wait()
    pack(0)
    scales[0] = jnp.zeros((2 * NX, 128), F32)
    stay[2].wait()
    stay[3].wait()
    scales[0, 0:NX, 0:SHARD] = k_loc[...]
    scales[0, NX : 2 * NX, 0:SHARD] = v_loc[...]

    pl.semaphore_wait(barrier, len(partners))
    for d in FAR:
        qx[d] = remote(fore(d), held[d], q_send.at[d], q_recv.at[d], at_x[d])
        qx[d].start()
    over_z(0)
    for d in FAR:
        rx[d] = remote(rest(d), q_rest.at[y, x], r_send.at[d], r_recv.at[d], at_x[d])
        rx[d].start()
    for d in FAR:
        sx[d] = remote(scales.at[0], scales.at[d], s_send.at[d], s_recv.at[d], at_x[d])
        sx[d].start()
    for d in FAR:
        kx[d] = remote(k.at[half, cols(d, D)], keys.at[x, half], k_send.at[d], k_recv.at[d], at_x[d])
        vx[d] = remote(v.at[half, cols(d, D)], v_land.at[d, half], v_send.at[d], v_recv.at[d], at_x[d])
        kx[d].start()
        vx[d].start()

    for d in FAR:
        qx[d].wait_recv()
        pack(d)
        over_z(d)
    blocks = blocks_in(goes, rep)

    stay[4].wait()
    lists[...] = block_lists(listed, blocks, rep, y)

    scale_row = iota((2 * NX, 128), 0)

    def pick_row(tile, n):
        return jnp.sum(jnp.where(scale_row == n, tile, 0.0), axis=0, keepdims=True)

    def finish(d):
        tile = scales[d]
        for_keys = pick_row(tile, x) * TO_LOG2
        for_values = pick_row(tile, NX + x)
        for b in range(SHARD):
            at = back[d] * SHARD + b
            factors[at] = jnp.broadcast_to(for_keys[:, b : b + 1], (8, 128))
            rows = slice(b * B, (b + 1) * B)
            scaled = v_land[d, rows].astype(F32) * jnp.broadcast_to(for_values[:, b : b + 1], (B, D))
            values[at] = scaled.astype(BF16).T

    def hand_over(d):
        kx[d].wait_recv()
        piece = keys.at[back[d], half]
        kc[d] = remote(piece, piece, kc_send.at[d], kc_recv.at[d], sib)
        kc[d].start()
        vx[d].wait_recv()
        vc[d] = remote(v_land.at[d, half], v_land.at[d, half], vc_send.at[d], vc_recv.at[d], sib)
        vc[d].start()
        sx[d].wait_recv()

    def whole(d):
        kc[d].wait_recv()
        vc[d].wait_recv()
        finish(d)

    def over_y(d):
        for n in range(1, len(groups)):
            qz[d][n].wait_recv()
        for s in range(QB):
            q_fore[y, back[d], s] = came[d][slot_of(blocks[s], z, c)]
        for e in FAR:
            piece = q_fore.at[y, back[d]]
            qy[d][e] = remote(piece, piece, y_send.at[d, e], y_recv.at[d, e], at_y[e])
            qy[d][e].start()

    stay[7].wait()
    for d in (0, *FAR):
        if d:
            rx[d].wait_recv()
        for e in FAR:
            piece = q_rest.at[y, back[d]]
            ry[d][e] = remote(piece, piece, t_send.at[d, e], t_recv.at[d, e], at_y[e])
            ry[d][e].start()
    for copy in stay[5:7]:
        copy.wait()
    finish(0)
    hand_over(1)
    hand_over(3)
    over_y(0)
    whole(1)
    over_y(1)
    whole(3)
    over_y(3)
    over_y(2)
    hand_over(2)
    whole(2)
    for d in range(NX):
        for e in FAR:
            for copy in (qy[d][e], ry[d][e]):
                copy.wait_recv()
                copy.wait_send()
    for d in FAR:
        for copy in (qx[d], rx[d], kx[d], vx[d], sx[d], kc[d], vc[d]):
            copy.wait_send()
    for copies in qz:
        for copy in copies[1:]:
            copy.wait_send()


def spread(target, q, k, v, ks, vs, pattern):
    slots = pltpu.VMEM((2 * NZ, ROWS, FORE), BF16)
    return pl.pallas_call(
        spread_kernel,
        out_shape=[
            jax.ShapeDtypeStruct((NY, NX, QB, ROWS, FORE), BF16),
            jax.ShapeDtypeStruct((NY, NX, QB, ROWS, REST), BF16),
            jax.ShapeDtypeStruct((NX, KEYS, D), BF16),
            jax.ShapeDtypeStruct((KB, D, B), BF16),
            jax.ShapeDtypeStruct((KB, 8, 128), F32),
            jax.ShapeDtypeStruct((PAIRS, 128), I32),
        ],
        in_specs=[HBM] * 7,
        out_specs=[VMEM] * 6,
        scratch_shapes=[pltpu.VMEM((QB, ROWS, FORE), BF16)] * NX
        + [pltpu.VMEM((NX, 2 * NZ, ROWS, FORE), BF16)]
        + [slots] * NX
        + [
            pltpu.VMEM((NX, KEYS, D), BF16),
            pltpu.VMEM((NX, 2 * NX, 128), F32),
            pltpu.VMEM((NX, SHARD), F32),
            pltpu.VMEM((NX, SHARD), F32),
            pltpu.VMEM((HEADS, *pattern.shape[1:]), I32),
            pltpu.SMEM(target.shape, I32),
        ]
        + [DMA((NX, 2 * NZ))] * 2
        + [DMA((NX,))] * 4
        + [DMA((NX, NY))] * 4
        + [DMA((NX,))] * 10
        + [DMA((8,))],
        compiler_params=pltpu.CompilerParams(
            collective_id=0, has_side_effects=True, vmem_limit_bytes=24 << 20
        ),
        name="spread",
    )(target, q, k, v, ks, vs, pattern)


def attend_kernel(
    ints, q_fore, q_rest, keys, values, factors, out_fore, out_rest, extra_out,
    qs, sc, mx, acc, su, extra, items,
):
    row = iota((B, B), 1)
    row = ((row >> 3) & 3) * PART + (row >> 5) * ROWS + (row & 7)
    ahead = iota((B, B), 0) - row
    extra[...] = jnp.zeros((B, B), F32)
    qs[HEADS] = jnp.zeros((D, B), BF16)

    def tall(tile):
        return jnp.broadcast_to(tile[None], (B // 8, 8, B)).reshape(B, B)

    @pl.loop(0, QB // TOGETHER)
    def _(part_of):
        def add_pair(r, n):
            def add(t, n):
                items[n] = r * 16 + t
                return n + 1

            return lax.fori_loop(0, (ints[part_of * LANES + r, KB] + 1) // 2, add, n)

        n = lax.fori_loop(0, LANES, add_pair, jnp.int32(0))
        for g in range(STEP):
            items[n + g] = HEADS * 16
        count = (n + STEP - 1) // STEP
        for j in range(TOGETHER):
            for q_ref, low, high in ((q_fore, 0, EARLY), (q_rest, EARLY, HEADS)):
                rows = q_ref[:, :, part_of * TOGETHER + j].astype(F32).reshape(B, (high - low) * D)
                rows = rows.astype(BF16)
                for h in range(low, high):
                    qs[j * 8 + h] = rows[:, (h - low) * D : (h - low + 1) * D].T
        mx[...] = jnp.full(mx.shape, NEG, F32)
        acc[...] = jnp.zeros(acc.shape, F32)
        su[...] = jnp.zeros(su.shape, F32)

        def item_at(i, g):
            item = items[i * STEP + g]
            r, t = item >> 4, item & 15
            codes = [ints[part_of * LANES + r, t * 2 + u] for u in range(2)]
            return r, codes, [code & (KB - 1) for code in codes]

        @pl.loop(0, count)
        def _(i):
            for g in range(STEP):
                r, codes, kbs = item_at(i, g)
                both = jnp.dot(
                    jnp.concatenate([keys[kb] for kb in kbs], axis=0), qs[r], preferred_element_type=F32
                )
                top = mx[r]
                for u in range(2):
                    score = both[u * B : (u + 1) * B] * tall(factors[kbs[u]])
                    score = jnp.where(ahead <= (codes[u] >> 5) * B, score, NEG)
                    sc[(i * STEP + g) * 2 + u] = score
                    top = jnp.maximum(top, jnp.max(score.reshape(B // 8, 8, B), axis=0))
                mx[r] = top

        for j in range(TOGETHER):
            for h in range(HEADS):
                top = jnp.max(mx[j * 8 + h], axis=0, keepdims=True)
                mx[j * 8 + h] = jnp.broadcast_to(top, (8, B)).astype(BF16).astype(F32)

        @pl.loop(0, count)
        def _(i):
            for g in range(STEP):
                r, codes, kbs = item_at(i, g)
                top = tall(mx[r])
                weights = [jnp.exp2(sc[(i * STEP + g) * 2 + u] - top) for u in range(2)]
                su[r] += jnp.sum((weights[0] + weights[1]).reshape(B // 8, 8, B), axis=0)
                acc[r] += jnp.dot(
                    jnp.concatenate([values[kb] for kb in kbs], axis=1),
                    jnp.concatenate([w.astype(BF16) for w in weights], axis=0),
                    preferred_element_type=F32,
                )

        for j in range(TOGETHER):
            for h in range(HEADS):
                r = j * 8 + h
                at = part_of * LANES + r
                extra[pl.ds(at, 1), :] = mx[r][0:1]
                extra[pl.ds(SUM_LANE + at, 1), :] = jnp.sum(su[r], axis=0, keepdims=True)
                part = acc[r].astype(BF16).T
                out, i = (out_fore, h) if h < EARLY else (out_rest, h - EARLY)
                for d in range(NY):
                    out[d, part_of * TOGETHER + j, :, i * D : (i + 1) * D] = part[d * PART : (d + 1) * PART]

    turned = extra[...].T
    for d in range(NY):
        extra_out[d] = turned[d * PART : (d + 1) * PART].astype(BF16)


def attend(lists, q_fore, q_rest, keys, values, factors):
    most = TOGETHER * HEADS * KB // 2 + STEP
    return pl.pallas_call(
        attend_kernel,
        out_shape=[
            jax.ShapeDtypeStruct((NY, QB, PART, FORE), BF16),
            jax.ShapeDtypeStruct((NY, QB, PART, REST), BF16),
            jax.ShapeDtypeStruct((NY, PART, 128), BF16),
        ],
        in_specs=[SMEM] + [VMEM] * 5,
        out_specs=[VMEM] * 3,
        scratch_shapes=[
            pltpu.VMEM((LANES, D, B), BF16),
            pltpu.VMEM((2 * most, B, B), F32),
            pltpu.VMEM((LANES, 8, B), F32),
            pltpu.VMEM((LANES, D, B), F32),
            pltpu.VMEM((LANES, 8, B), F32),
            pltpu.VMEM((B, B), F32),
            pltpu.SMEM((most,), I32),
        ],
        compiler_params=pltpu.CompilerParams(vmem_limit_bytes=46 << 20),
        name="attend",
    )(lists, q_fore, q_rest, keys.reshape(KB, B, D), values, factors)


def gather_kernel(
    target, p, p_rest, extra_in, out,
    parts, parts_rest, extra, att, att_rest, held, packed, came, goes,
    e_send, e_recv, y_send, y_recv, t_send, t_recv, x_send, x_recv, r_send, r_recv, z_send, z_recv, own,
):
    rep, z, c, x, y = place()
    xs = [(x + d) % NX for d in range(NX)]
    back = [(x + NX - d) % NX for d in range(NX)]
    ys = [(y + d) % NY for d in range(NY)]
    at_x = [(rep, xs[d] * NY + y) for d in range(NX)]
    at_y = [(rep, x * NY + ys[d]) for d in range(NY)]
    groups = near_groups(z, c)
    at_group = [(g, x * NY + y) for g in groups]
    partners = at_group[1:] + at_x[1:] + at_y[1:]
    barrier = pltpu.get_barrier_semaphore()
    for who in partners:
        pl.semaphore_signal(barrier, inc=1, device_id=who, device_id_type=MESH)
    told = pltpu.make_async_copy(target, goes, own.at[QB])
    told.start()
    pl.semaphore_wait(barrier, len(partners))

    ex, ty, rx = ([None] * NY for _ in range(3))
    py = [[None] * NY for _ in range(QB)]
    px = [[None] * NX for _ in range(QB)]
    pz = [None] * len(groups)
    for d in FAR:
        ex[d] = remote(extra_in.at[ys[d]], extra.at[d], e_send.at[d], e_recv.at[d], at_y[d])
        ex[d].start()
        ty[d] = remote(p_rest.at[ys[d]], parts_rest.at[d], t_send.at[d], t_recv.at[d], at_y[d])
        ty[d].start()
    for b in range(QB):
        for d in FAR:
            py[b][d] = remote(p.at[ys[d], b], parts.at[d, b], y_send.at[b, d], y_recv.at[b, d], at_y[d])
            py[b][d].start()
    told.wait()
    leaving = blocks_out(goes, rep, groups)
    blocks = blocks_in(goes, rep)
    for d in FAR:
        ex[d].wait_recv()
    marks = [extra_in[y].astype(F32)] + [extra[d].astype(F32) for d in range(1, NY)]
    top = functools.reduce(jnp.maximum, marks)
    shift = [jnp.exp2(e - top) for e in marks]
    total = sum(w * pltpu.roll(e, SUM_LANE, 1) for w, e in zip(shift, marks))
    lane = iota((PART, 128), 1)
    total = jnp.where((lane < QB * 8) & ((lane & 7) < HEADS), total, 1.0)
    ratio = [w / total for w in shift]

    def quotient(b, h, mine, theirs, cols):
        at = b * 8 + h
        value = sum(
            jnp.broadcast_to(ratio[d][:, at : at + 1], (PART, D))
            * (theirs[d, b, :, cols] if d else mine[y, b, :, cols]).astype(F32)
            for d in range(NY)
        )
        return value.reshape(NX, ROWS, D).astype(BF16)

    for d in FAR:
        ty[d].wait_recv()
    for b in range(QB):
        for h in range(EARLY, HEADS):
            cols = slice((h - EARLY) * D, (h - EARLY + 1) * D)
            value = quotient(b, h, p_rest, parts_rest, cols)
            for d in range(NX):
                att_rest[d, b, :, cols] = value[d]
    for d in FAR:
        rx[d] = remote(att_rest.at[xs[d]], held.at[d], r_send.at[d], r_recv.at[d], at_x[d])
        rx[d].start()
    held[0] = att_rest[x]
    mine = pl.ds(pl.multiple_of(x * SLICE, D), FORE)
    for b in range(QB):
        if b == 1:
            for d in FAR:
                rx[d].wait_recv()
            for n in ORDER:
                for d in range(NX):
                    block = held[d, leaving[n]]
                    if n == 0:
                        came[n, d] = block
                    else:
                        packed[n, d] = block
                if n > 0:
                    pz[n] = remote(packed.at[n], came.at[n], z_send.at[n], z_recv.at[n], at_group[n])
                    pz[n].start()
        for d in FAR:
            py[b][d].wait_recv()
        for h in range(EARLY):
            cols = slice(h * D, (h + 1) * D)
            value = quotient(b, h, p, parts, cols)
            for d in range(NX):
                att[b, d, :, cols] = value[d]
        for d in FAR:
            px[b][d] = remote(
                att.at[b, xs[d]], out.at[b, :, mine], x_send.at[b, d], x_recv.at[b, d], at_x[d]
            )
            px[b][d].start()
        px[b][0] = pltpu.make_async_copy(att.at[b, x], out.at[b, :, mine], own.at[b])
        px[b][0].start()

    for n in range(1, len(groups)):
        pz[n].wait_recv()
    for b in range(QB):
        px[b][0].wait()
        for d in FAR:
            px[b][d].wait_recv()
    for s in range(QB):
        n = slot_of(blocks[s], z, c)
        for d in range(NX):
            out[s, :, pl.ds(pl.multiple_of(back[d] * SLICE + FORE, D), REST)] = came[n, d]

    for n in range(1, len(groups)):
        pz[n].wait_send()
    for d in FAR:
        for copy in (ex[d], ty[d], rx[d]):
            copy.wait_send()
        for b in range(QB):
            px[b][d].wait_send()
            py[b][d].wait_send()


def gather(target, p, p_rest, extra):
    slots = pltpu.VMEM((2 * NZ, NX, ROWS, REST), BF16)
    return pl.pallas_call(
        gather_kernel,
        out_shape=jax.ShapeDtypeStruct((QB, ROWS, NX * SLICE), BF16),
        in_specs=[HBM, VMEM, VMEM, VMEM],
        out_specs=VMEM,
        scratch_shapes=[
            pltpu.VMEM((NY, QB, PART, FORE), BF16),
            pltpu.VMEM((NY, QB, PART, REST), BF16),
            pltpu.VMEM((NY, PART, 128), BF16),
            pltpu.VMEM((QB, NX, ROWS, FORE), BF16),
            pltpu.VMEM((NX, QB, ROWS, REST), BF16),
            pltpu.VMEM((NX, QB, ROWS, REST), BF16),
            slots,
            slots,
            pltpu.SMEM(target.shape, I32),
        ]
        + [DMA((NY,))] * 2
        + [DMA((QB, NY))] * 2
        + [DMA((NY,))] * 2
        + [DMA((QB, NX))] * 2
        + [DMA((NX,))] * 2
        + [DMA((2 * NZ,))] * 2
        + [DMA((QB + 1,))],
        compiler_params=pltpu.CompilerParams(
            collective_id=1, has_side_effects=True, vmem_limit_bytes=16 << 20
        ),
        name="gather",
    )(target, p, p_rest, extra)


def hbm(array):
    return pltpu.with_memory_space_constraint(array, pltpu.HBM)


def per_device(queries, key_cache, value_cache, key_scale, value_scale, pattern, target):
    target = hbm(target)
    q_fore, q_rest, keys, values, factors, lists = spread(
        target,
        hbm(queries),
        hbm(key_cache),
        hbm(value_cache),
        hbm(key_scale.T),
        hbm(value_scale.T),
        hbm(jnp.swapaxes(pattern, 1, 2)),
    )
    part, rest, extra = attend(lists, q_fore, q_rest, keys, values, factors)
    return gather(target, part, rest, extra)


def solution(mesh):
    return jax.shard_map(
        per_device,
        mesh=mesh,
        in_specs=(
            P("replica", "ctx", None),
            P("ctx", None),
            P("ctx", None),
            P("ctx", None),
            P("ctx", None),
            P(),
            P(),
        ),
        out_specs=P("replica", "ctx", None),
        check_vma=False,
    )
```

```python
import functools
import math

import jax
import jax.numpy as jnp
from jax import lax
from jax.experimental import pallas as pl
from jax.experimental.pallas import tpu as pltpu
from jax.sharding import PartitionSpec as P

MESH = pl.DeviceIdType.MESH
BF16 = jnp.bfloat16
F32 = jnp.float32
I32 = jnp.int32

NX = 4
NY = 4
NZ = 8
HEADS = 7
D = 128
B = 128
QB = 4
KB = 32
SHARD = 8
SLICE = HEADS * D
EARLY = 6
FORE = EARLY * D
REST = SLICE - FORE
ROWS = B // (NX * NY)
PART = NX * ROWS
KEYS = SHARD * B
PAIRS = 32
SUM_LANE = 64
NEG = -(2.0**100)
STEP = 32
TOGETHER = 2
LANES = 8 * TOGETHER
FIRST = 64
FAR = (1, 3, 2)
ORDER = (8, 9, 6, 7, 10, 11, 4, 5, 12, 13, 2, 3, 14, 15, 1, 0)
TO_LOG2 = math.log2(math.e) / math.sqrt(D)

DMA = pltpu.SemaphoreType.DMA
HBM = pl.BlockSpec(memory_space=pltpu.HBM)
VMEM = pl.BlockSpec(memory_space=pltpu.VMEM)
SMEM = pl.BlockSpec(memory_space=pltpu.SMEM)


def place():
    rep = lax.axis_index("replica")
    ctx = lax.axis_index("ctx")
    return rep, rep // 2, rep % 2, ctx // NY, ctx % NY


def remote(src, dst, send, recv, who):
    return pltpu.make_async_remote_copy(
        src_ref=src, dst_ref=dst, send_sem=send, recv_sem=recv, device_id=who, device_id_type=MESH
    )


def iota(shape, dim):
    return lax.broadcasted_iota(I32, shape, dim)


def block_lists(listed, blocks, rep, y):
    shape = (PAIRS, 128)
    lane, row = iota(shape, 1), iota(shape, 0)
    block = (lane >> 3) * (SHARD * NY) + y * SHARD + (lane & 7)
    hits = jnp.zeros(shape, I32)
    own = jnp.zeros(shape, I32)
    column = iota(listed.shape[1:], 1)
    for s in range(QB):
        own = jnp.where(row >> 3 == s, jnp.where((row & 7) < EARLY, blocks[s], rep * QB + s), own)
        for h in range(HEADS):
            of = blocks[s] if h < EARLY else rep * QB + s
            entry = jnp.max(jnp.where(column == of, listed[h], -1), axis=1, keepdims=True)
            found = (jnp.broadcast_to(entry, shape) == block).astype(I32)
            found = jnp.max(found, axis=0, keepdims=True)
            hits = jnp.where(row == s * 8 + h, found, hits)
    below = FIRST + own - block
    hits = jnp.where(below == 0, 1, hits)
    hits = jnp.where((below >= 0) & (lane < KB) & ((row & 7) < HEADS), hits, 0)
    upto = hits
    for s in (1, 2, 4, 8, 16):
        upto = upto + jnp.where(lane >= s, pltpu.roll(upto, s, 1), 0)
    slot = jnp.where(hits > 0, upto - 1, -1)
    code = lane + KB * below
    packed = jnp.full(shape, -KB * 1024, I32)
    for b in range(KB):
        at = jnp.broadcast_to(slot[:, b : b + 1], shape) == lane
        packed = jnp.where(at, jnp.broadcast_to(code[:, b : b + 1], shape), packed)
    number = jnp.broadcast_to(upto[:, KB - 1 : KB], shape)
    return jnp.where(lane == KB, number, packed)


def near_groups(z, c):
    return [((z + d) % NZ) * 2 + (c + e) % 2 for d in range(NZ) for e in range(2)]


def slot_of(block, z, c):
    source = block >> 2
    return (((z + NZ - (source >> 1)) & (NZ - 1)) << 1) + ((source & 1) ^ c)


def blocks_out(goes, rep, groups):
    goes_to = [goes[rep * QB + b] for b in range(QB)]
    leaving = []
    for group in groups:
        b = jnp.int32(0)
        for other in range(1, QB):
            b = jnp.where(goes_to[other] == group, other, b)
        leaving.append(b)
    return leaving


def blocks_in(goes, rep):
    def look(j, state):
        found, *at = state
        hit = goes[j] == rep
        at = [jnp.where(hit & (found == s), j, a) for s, a in enumerate(at)]
        return (found + hit.astype(I32), *at)

    _, *blocks = lax.fori_loop(0, 2 * NZ * QB, look, (jnp.int32(0),) * (1 + QB))
    return blocks


def spread_kernel(
    target, q, k, v, ks, vs, pattern,
    q_fore, q_rest, keys, values, factors, lists,
    held0, held1, held2, held3, packed, came0, came1, came2, came3,
    v_land, scales, k_loc, v_loc, listed, goes,
    z_send, z_recv, q_send, q_recv, r_send, r_recv, y_send, y_recv, t_send, t_recv, k_send, k_recv, v_send, v_recv, s_send, s_recv,
    kc_send, kc_recv, vc_send, vc_recv, own,
):
    rep, z, c, x, y = place()
    sib = (rep + 1 - 2 * c, x * NY + y)
    xs = [(x + d) % NX for d in range(NX)]
    back = [(x + NX - d) % NX for d in range(NX)]
    at_x = [(rep, xs[d] * NY + y) for d in range(NX)]
    at_y = [(rep, x * NY + (y + d) % NY) for d in range(NY)]
    half = pl.ds(pl.multiple_of(c * (KEYS // 2), KEYS // 2), KEYS // 2)
    groups = near_groups(z, c)
    at_group = [(g, x * NY + y) for g in groups]
    held = (held0, held1, held2, held3)
    came = (came0, came1, came2, came3)

    def cols(d, n):
        return pl.ds(pl.multiple_of(xs[d] * n, n), n)

    def fore(d):
        return q.at[:, :, pl.ds(pl.multiple_of(xs[d] * SLICE, D), FORE)]

    def rest(d):
        return q.at[:, :, pl.ds(pl.multiple_of(xs[d] * SLICE + FORE, D), REST)]

    partners = at_group[1:] + at_x[1:] + at_y[1:]
    barrier = pltpu.get_barrier_semaphore()
    for who in partners:
        pl.semaphore_signal(barrier, inc=1, device_id=who, device_id_type=MESH)
    stay = [
        pltpu.make_async_copy(target, goes, own.at[0]),
        pltpu.make_async_copy(fore(0), held[0], own.at[1]),
        pltpu.make_async_copy(ks, k_loc, own.at[2]),
        pltpu.make_async_copy(vs, v_loc, own.at[3]),
        pltpu.make_async_copy(pattern.at[pl.ds(x * HEADS, HEADS)], listed, own.at[4]),
        pltpu.make_async_copy(k.at[:, cols(0, D)], keys.at[x], own.at[5]),
        pltpu.make_async_copy(v.at[:, cols(0, D)], v_land.at[0], own.at[6]),
        pltpu.make_async_copy(rest(0), q_rest.at[y, x], own.at[7]),
    ]
    for copy in stay:
        copy.start()

    qx, rx, kx, vx, sx, kc, vc = ([None] * NX for _ in range(7))
    qy, ry = ([[None] * NY for _ in range(NX)] for _ in range(2))
    qz = [[None] * len(groups) for _ in range(NX)]

    stay[0].wait()
    leaving = blocks_out(goes, rep, groups)

    def pack(d):
        for n in ORDER:
            block = held[d][leaving[n]]
            if n == 0:
                came[d][n] = block
            else:
                packed[d, n] = block

    def over_z(d):
        for n in ORDER[:-1]:
            qz[d][n] = remote(packed.at[d, n], came[d].at[n], z_send.at[d, n], z_recv.at[d, n], at_group[n])
            qz[d][n].start()

    stay[1].wait()
    pack(0)
    scales[0] = jnp.zeros((2 * NX, 128), F32)
    stay[2].wait()
    stay[3].wait()
    scales[0, 0:NX, 0:SHARD] = k_loc[...]
    scales[0, NX : 2 * NX, 0:SHARD] = v_loc[...]

    pl.semaphore_wait(barrier, len(partners))
    for d in FAR:
        qx[d] = remote(fore(d), held[d], q_send.at[d], q_recv.at[d], at_x[d])
        qx[d].start()
    over_z(0)
    for d in FAR:
        rx[d] = remote(rest(d), q_rest.at[y, x], r_send.at[d], r_recv.at[d], at_x[d])
        rx[d].start()
    for d in FAR:
        sx[d] = remote(scales.at[0], scales.at[d], s_send.at[d], s_recv.at[d], at_x[d])
        sx[d].start()
    for d in FAR:
        kx[d] = remote(k.at[half, cols(d, D)], keys.at[x, half], k_send.at[d], k_recv.at[d], at_x[d])
        vx[d] = remote(v.at[half, cols(d, D)], v_land.at[d, half], v_send.at[d], v_recv.at[d], at_x[d])
        kx[d].start()
        vx[d].start()

    for d in FAR:
        qx[d].wait_recv()
        pack(d)
        over_z(d)
    blocks = blocks_in(goes, rep)

    stay[4].wait()
    lists[...] = block_lists(listed, blocks, rep, y)

    scale_row = iota((2 * NX, 128), 0)

    def pick_row(tile, n):
        return jnp.sum(jnp.where(scale_row == n, tile, 0.0), axis=0, keepdims=True)

    def finish(d):
        tile = scales[d]
        for_keys = pick_row(tile, x) * TO_LOG2
        for_values = pick_row(tile, NX + x)
        for b in range(SHARD):
            at = back[d] * SHARD + b
            factors[at] = jnp.broadcast_to(for_keys[:, b : b + 1], (8, 128))
            rows = slice(b * B, (b + 1) * B)
            scaled = v_land[d, rows].astype(F32) * jnp.broadcast_to(for_values[:, b : b + 1], (B, D))
            values[at] = scaled.astype(BF16).T

    def hand_over(d):
        kx[d].wait_recv()
        piece = keys.at[back[d], half]
        kc[d] = remote(piece, piece, kc_send.at[d], kc_recv.at[d], sib)
        kc[d].start()
        vx[d].wait_recv()
        vc[d] = remote(v_land.at[d, half], v_land.at[d, half], vc_send.at[d], vc_recv.at[d], sib)
        vc[d].start()
        sx[d].wait_recv()

    def whole(d):
        kc[d].wait_recv()
        vc[d].wait_recv()
        finish(d)

    def over_y(d):
        for n in range(1, len(groups)):
            qz[d][n].wait_recv()
        for s in range(QB):
            q_fore[y, back[d], s] = came[d][slot_of(blocks[s], z, c)]
        for e in FAR:
            piece = q_fore.at[y, back[d]]
            qy[d][e] = remote(piece, piece, y_send.at[d, e], y_recv.at[d, e], at_y[e])
            qy[d][e].start()

    stay[7].wait()
    for d in (0, *FAR):
        if d:
            rx[d].wait_recv()
        for e in FAR:
            piece = q_rest.at[y, back[d]]
            ry[d][e] = remote(piece, piece, t_send.at[d, e], t_recv.at[d, e], at_y[e])
            ry[d][e].start()
    for copy in stay[5:7]:
        copy.wait()
    finish(0)
    hand_over(1)
    hand_over(3)
    over_y(0)
    whole(1)
    over_y(1)
    whole(3)
    over_y(3)
    over_y(2)
    hand_over(2)
    whole(2)
    for d in range(NX):
        for e in FAR:
            for copy in (qy[d][e], ry[d][e]):
                copy.wait_recv()
                copy.wait_send()
    for d in FAR:
        for copy in (qx[d], rx[d], kx[d], vx[d], sx[d], kc[d], vc[d]):
            copy.wait_send()
    for copies in qz:
        for copy in copies[1:]:
            copy.wait_send()


def spread(target, q, k, v, ks, vs, pattern):
    slots = pltpu.VMEM((2 * NZ, ROWS, FORE), BF16)
    return pl.pallas_call(
        spread_kernel,
        out_shape=[
            jax.ShapeDtypeStruct((NY, NX, QB, ROWS, FORE), BF16),
            jax.ShapeDtypeStruct((NY, NX, QB, ROWS, REST), BF16),
            jax.ShapeDtypeStruct((NX, KEYS, D), BF16),
            jax.ShapeDtypeStruct((KB, D, B), BF16),
            jax.ShapeDtypeStruct((KB, 8, 128), F32),
            jax.ShapeDtypeStruct((PAIRS, 128), I32),
        ],
        in_specs=[HBM] * 7,
        out_specs=[VMEM] * 6,
        scratch_shapes=[pltpu.VMEM((QB, ROWS, FORE), BF16)] * NX
        + [pltpu.VMEM((NX, 2 * NZ, ROWS, FORE), BF16)]
        + [slots] * NX
        + [
            pltpu.VMEM((NX, KEYS, D), BF16),
            pltpu.VMEM((NX, 2 * NX, 128), F32),
            pltpu.VMEM((NX, SHARD), F32),
            pltpu.VMEM((NX, SHARD), F32),
            pltpu.VMEM((HEADS, *pattern.shape[1:]), I32),
            pltpu.SMEM(target.shape, I32),
        ]
        + [DMA((NX, 2 * NZ))] * 2
        + [DMA((NX,))] * 4
        + [DMA((NX, NY))] * 4
        + [DMA((NX,))] * 10
        + [DMA((8,))],
        compiler_params=pltpu.CompilerParams(
            collective_id=0, has_side_effects=True, vmem_limit_bytes=24 << 20
        ),
        name="spread",
    )(target, q, k, v, ks, vs, pattern)


def attend_kernel(
    ints, q_fore, q_rest, keys, values, factors, out_fore, out_rest, extra_out,
    qs, sc, mx, acc, su, extra, items,
):
    row = iota((B, B), 1)
    row = ((row >> 3) & 3) * PART + (row >> 5) * ROWS + (row & 7)
    ahead = iota((B, B), 0) - row
    extra[...] = jnp.zeros((B, B), F32)
    qs[HEADS] = jnp.zeros((D, B), BF16)

    def tall(tile):
        return jnp.broadcast_to(tile[None], (B // 8, 8, B)).reshape(B, B)

    @pl.loop(0, QB // TOGETHER)
    def _(part_of):
        def add_pair(r, n):
            def add(t, n):
                items[n] = r * 16 + t
                return n + 1

            return lax.fori_loop(0, (ints[part_of * LANES + r, KB] + 1) // 2, add, n)

        n = lax.fori_loop(0, LANES, add_pair, jnp.int32(0))
        for g in range(STEP):
            items[n + g] = HEADS * 16
        count = (n + STEP - 1) // STEP
        for j in range(TOGETHER):
            for q_ref, low, high in ((q_fore, 0, EARLY), (q_rest, EARLY, HEADS)):
                rows = q_ref[:, :, part_of * TOGETHER + j].astype(F32).reshape(B, (high - low) * D)
                rows = rows.astype(BF16)
                for h in range(low, high):
                    qs[j * 8 + h] = rows[:, (h - low) * D : (h - low + 1) * D].T
        mx[...] = jnp.full(mx.shape, NEG, F32)
        acc[...] = jnp.zeros(acc.shape, F32)
        su[...] = jnp.zeros(su.shape, F32)

        def item_at(i, g):
            item = items[i * STEP + g]
            r, t = item >> 4, item & 15
            codes = [ints[part_of * LANES + r, t * 2 + u] for u in range(2)]
            return r, codes, [code & (KB - 1) for code in codes]

        @pl.loop(0, count)
        def _(i):
            for g in range(STEP):
                r, codes, kbs = item_at(i, g)
                both = jnp.dot(
                    jnp.concatenate([keys[kb] for kb in kbs], axis=0), qs[r], preferred_element_type=F32
                )
                top = mx[r]
                for u in range(2):
                    score = both[u * B : (u + 1) * B] * tall(factors[kbs[u]])
                    score = jnp.where(ahead <= (codes[u] >> 5) * B, score, NEG)
                    sc[(i * STEP + g) * 2 + u] = score
                    top = jnp.maximum(top, jnp.max(score.reshape(B // 8, 8, B), axis=0))
                mx[r] = top

        for j in range(TOGETHER):
            for h in range(HEADS):
                top = jnp.max(mx[j * 8 + h], axis=0, keepdims=True)
                mx[j * 8 + h] = jnp.broadcast_to(top, (8, B)).astype(BF16).astype(F32)

        @pl.loop(0, count)
        def _(i):
            for g in range(STEP):
                r, codes, kbs = item_at(i, g)
                top = tall(mx[r])
                weights = [jnp.exp2(sc[(i * STEP + g) * 2 + u] - top) for u in range(2)]
                su[r] += jnp.sum((weights[0] + weights[1]).reshape(B // 8, 8, B), axis=0)
                acc[r] += jnp.dot(
                    jnp.concatenate([values[kb] for kb in kbs], axis=1),
                    jnp.concatenate([w.astype(BF16) for w in weights], axis=0),
                    preferred_element_type=F32,
                )

        for j in range(TOGETHER):
            for h in range(HEADS):
                r = j * 8 + h
                at = part_of * LANES + r
                extra[pl.ds(at, 1), :] = mx[r][0:1]
                extra[pl.ds(SUM_LANE + at, 1), :] = jnp.sum(su[r], axis=0, keepdims=True)
                part = acc[r].astype(BF16).T
                out, i = (out_fore, h) if h < EARLY else (out_rest, h - EARLY)
                for d in range(NY):
                    out[d, part_of * TOGETHER + j, :, i * D : (i + 1) * D] = part[d * PART : (d + 1) * PART]

    turned = extra[...].T
    for d in range(NY):
        extra_out[d] = turned[d * PART : (d + 1) * PART].astype(BF16)


def attend(lists, q_fore, q_rest, keys, values, factors):
    most = TOGETHER * HEADS * KB // 2 + STEP
    return pl.pallas_call(
        attend_kernel,
        out_shape=[
            jax.ShapeDtypeStruct((NY, QB, PART, FORE), BF16),
            jax.ShapeDtypeStruct((NY, QB, PART, REST), BF16),
            jax.ShapeDtypeStruct((NY, PART, 128), BF16),
        ],
        in_specs=[SMEM] + [VMEM] * 5,
        out_specs=[VMEM] * 3,
        scratch_shapes=[
            pltpu.VMEM((LANES, D, B), BF16),
            pltpu.VMEM((2 * most, B, B), F32),
            pltpu.VMEM((LANES, 8, B), F32),
            pltpu.VMEM((LANES, D, B), F32),
            pltpu.VMEM((LANES, 8, B), F32),
            pltpu.VMEM((B, B), F32),
            pltpu.SMEM((most,), I32),
        ],
        compiler_params=pltpu.CompilerParams(vmem_limit_bytes=46 << 20),
        name="attend",
    )(lists, q_fore, q_rest, keys.reshape(KB, B, D), values, factors)


def gather_kernel(
    target, p, p_rest, extra_in, out,
    parts, parts_rest, extra, att, att_rest, held, packed, came, goes,
    e_send, e_recv, y_send, y_recv, t_send, t_recv, x_send, x_recv, r_send, r_recv, z_send, z_recv, own,
):
    rep, z, c, x, y = place()
    xs = [(x + d) % NX for d in range(NX)]
    back = [(x + NX - d) % NX for d in range(NX)]
    ys = [(y + d) % NY for d in range(NY)]
    at_x = [(rep, xs[d] * NY + y) for d in range(NX)]
    at_y = [(rep, x * NY + ys[d]) for d in range(NY)]
    groups = near_groups(z, c)
    at_group = [(g, x * NY + y) for g in groups]
    partners = at_group[1:] + at_x[1:] + at_y[1:]
    barrier = pltpu.get_barrier_semaphore()
    for who in partners:
        pl.semaphore_signal(barrier, inc=1, device_id=who, device_id_type=MESH)
    told = pltpu.make_async_copy(target, goes, own.at[QB])
    told.start()
    pl.semaphore_wait(barrier, len(partners))

    ex, ty, rx = ([None] * NY for _ in range(3))
    py = [[None] * NY for _ in range(QB)]
    px = [[None] * NX for _ in range(QB)]
    pz = [None] * len(groups)
    for d in FAR:
        ex[d] = remote(extra_in.at[ys[d]], extra.at[d], e_send.at[d], e_recv.at[d], at_y[d])
        ex[d].start()
        ty[d] = remote(p_rest.at[ys[d]], parts_rest.at[d], t_send.at[d], t_recv.at[d], at_y[d])
        ty[d].start()
    for b in range(QB):
        for d in FAR:
            py[b][d] = remote(p.at[ys[d], b], parts.at[d, b], y_send.at[b, d], y_recv.at[b, d], at_y[d])
            py[b][d].start()
    told.wait()
    leaving = blocks_out(goes, rep, groups)
    blocks = blocks_in(goes, rep)
    for d in FAR:
        ex[d].wait_recv()
    marks = [extra_in[y].astype(F32)] + [extra[d].astype(F32) for d in range(1, NY)]
    top = functools.reduce(jnp.maximum, marks)
    shift = [jnp.exp2(e - top) for e in marks]
    total = sum(w * pltpu.roll(e, SUM_LANE, 1) for w, e in zip(shift, marks))
    lane = iota((PART, 128), 1)
    total = jnp.where((lane < QB * 8) & ((lane & 7) < HEADS), total, 1.0)
    ratio = [w / total for w in shift]

    def quotient(b, h, mine, theirs, cols):
        at = b * 8 + h
        value = sum(
            jnp.broadcast_to(ratio[d][:, at : at + 1], (PART, D))
            * (theirs[d, b, :, cols] if d else mine[y, b, :, cols]).astype(F32)
            for d in range(NY)
        )
        return value.reshape(NX, ROWS, D).astype(BF16)

    for d in FAR:
        ty[d].wait_recv()
    for b in range(QB):
        for h in range(EARLY, HEADS):
            cols = slice((h - EARLY) * D, (h - EARLY + 1) * D)
            value = quotient(b, h, p_rest, parts_rest, cols)
            for d in range(NX):
                att_rest[d, b, :, cols] = value[d]
    for d in FAR:
        rx[d] = remote(att_rest.at[xs[d]], held.at[d], r_send.at[d], r_recv.at[d], at_x[d])
        rx[d].start()
    held[0] = att_rest[x]
    mine = pl.ds(pl.multiple_of(x * SLICE, D), FORE)
    for b in range(QB):
        if b == 1:
            for d in FAR:
                rx[d].wait_recv()
            for n in ORDER:
                for d in range(NX):
                    block = held[d, leaving[n]]
                    if n == 0:
                        came[n, d] = block
                    else:
                        packed[n, d] = block
                if n > 0:
                    pz[n] = remote(packed.at[n], came.at[n], z_send.at[n], z_recv.at[n], at_group[n])
                    pz[n].start()
        for d in FAR:
            py[b][d].wait_recv()
        for h in range(EARLY):
            cols = slice(h * D, (h + 1) * D)
            value = quotient(b, h, p, parts, cols)
            for d in range(NX):
                att[b, d, :, cols] = value[d]
        for d in FAR:
            px[b][d] = remote(
                att.at[b, xs[d]], out.at[b, :, mine], x_send.at[b, d], x_recv.at[b, d], at_x[d]
            )
            px[b][d].start()
        px[b][0] = pltpu.make_async_copy(att.at[b, x], out.at[b, :, mine], own.at[b])
        px[b][0].start()

    for n in range(1, len(groups)):
        pz[n].wait_recv()
    for b in range(QB):
        px[b][0].wait()
        for d in FAR:
            px[b][d].wait_recv()
    for s in range(QB):
        n = slot_of(blocks[s], z, c)
        for d in range(NX):
            out[s, :, pl.ds(pl.multiple_of(back[d] * SLICE + FORE, D), REST)] = came[n, d]

    for n in range(1, len(groups)):
        pz[n].wait_send()
    for d in FAR:
        for copy in (ex[d], ty[d], rx[d]):
            copy.wait_send()
        for b in range(QB):
            px[b][d].wait_send()
            py[b][d].wait_send()


def gather(target, p, p_rest, extra):
    slots = pltpu.VMEM((2 * NZ, NX, ROWS, REST), BF16)
    return pl.pallas_call(
        gather_kernel,
        out_shape=jax.ShapeDtypeStruct((QB, ROWS, NX * SLICE), BF16),
        in_specs=[HBM, VMEM, VMEM, VMEM],
        out_specs=VMEM,
        scratch_shapes=[
            pltpu.VMEM((NY, QB, PART, FORE), BF16),
            pltpu.VMEM((NY, QB, PART, REST), BF16),
            pltpu.VMEM((NY, PART, 128), BF16),
            pltpu.VMEM((QB, NX, ROWS, FORE), BF16),
            pltpu.VMEM((NX, QB, ROWS, REST), BF16),
            pltpu.VMEM((NX, QB, ROWS, REST), BF16),
            slots,
            slots,
            pltpu.SMEM(target.shape, I32),
        ]
        + [DMA((NY,))] * 2
        + [DMA((QB, NY))] * 2
        + [DMA((NY,))] * 2
        + [DMA((QB, NX))] * 2
        + [DMA((NX,))] * 2
        + [DMA((2 * NZ,))] * 2
        + [DMA((QB + 1,))],
        compiler_params=pltpu.CompilerParams(
            collective_id=1, has_side_effects=True, vmem_limit_bytes=16 << 20
        ),
        name="gather",
    )(target, p, p_rest, extra)


def hbm(array):
    return pltpu.with_memory_space_constraint(array, pltpu.HBM)


def per_device(queries, key_cache, value_cache, key_scale, value_scale, pattern, target):
    target = hbm(target)
    q_fore, q_rest, keys, values, factors, lists = spread(
        target,
        hbm(queries),
        hbm(key_cache),
        hbm(value_cache),
        hbm(key_scale.T),
        hbm(value_scale.T),
        hbm(jnp.swapaxes(pattern, 1, 2)),
    )
    part, rest, extra = attend(lists, q_fore, q_rest, keys, values, factors)
    return gather(target, part, rest, extra)


def solution(mesh):
    return jax.shard_map(
        per_device,
        mesh=mesh,
        in_specs=(
            P("replica", "ctx", None),
            P("ctx", None),
            P("ctx", None),
            P("ctx", None),
            P("ctx", None),
            P(),
            P(),
        ),
        out_specs=P("replica", "ctx", None),
        check_vma=False,
    )
```

```python
import functools
import math

import jax
import jax.numpy as jnp
from jax import lax
from jax.experimental import pallas as pl
from jax.experimental.pallas import tpu as pltpu
from jax.sharding import PartitionSpec as P

MESH = pl.DeviceIdType.MESH
BF16 = jnp.bfloat16
F32 = jnp.float32
I32 = jnp.int32

NX = 4
NY = 4
NZ = 8
HEADS = 7
D = 128
B = 128
QB = 4
KB = 32
SHARD = 8
SLICE = HEADS * D
EARLY = 5
FORE = EARLY * D
REST = SLICE - FORE
ROWS = B // (NX * NY)
PART = NX * ROWS
KEYS = SHARD * B
PAIRS = 32
SUM_LANE = 64
NEG = -(2.0**100)
STEP = 28
TOGETHER = 2
LANES = 8 * TOGETHER
FIRST = 64
FAR = (1, 3, 2)
ORDER = (8, 9, 6, 7, 10, 11, 4, 5, 12, 13, 2, 3, 14, 15, 1, 0)
TO_LOG2 = math.log2(math.e) / math.sqrt(D)

DMA = pltpu.SemaphoreType.DMA
HBM = pl.BlockSpec(memory_space=pltpu.HBM)
VMEM = pl.BlockSpec(memory_space=pltpu.VMEM)
SMEM = pl.BlockSpec(memory_space=pltpu.SMEM)


def place():
    rep = lax.axis_index("replica")
    ctx = lax.axis_index("ctx")
    return rep, rep // 2, rep % 2, ctx // NY, ctx % NY


def remote(src, dst, send, recv, who):
    return pltpu.make_async_remote_copy(
        src_ref=src, dst_ref=dst, send_sem=send, recv_sem=recv, device_id=who, device_id_type=MESH
    )


def iota(shape, dim):
    return lax.broadcasted_iota(I32, shape, dim)


def block_lists(listed, blocks, rep, y):
    shape = (PAIRS, 128)
    lane, row = iota(shape, 1), iota(shape, 0)
    block = (lane >> 3) * (SHARD * NY) + y * SHARD + (lane & 7)
    hits = jnp.zeros(shape, I32)
    own = jnp.zeros(shape, I32)
    column = iota(listed.shape[1:], 1)
    for s in range(QB):
        own = jnp.where(row >> 3 == s, jnp.where((row & 7) < EARLY, blocks[s], rep * QB + s), own)
        for h in range(HEADS):
            of = blocks[s] if h < EARLY else rep * QB + s
            entry = jnp.max(jnp.where(column == of, listed[h], -1), axis=1, keepdims=True)
            found = (jnp.broadcast_to(entry, shape) == block).astype(I32)
            found = jnp.max(found, axis=0, keepdims=True)
            hits = jnp.where(row == s * 8 + h, found, hits)
    below = FIRST + own - block
    hits = jnp.where(below == 0, 1, hits)
    hits = jnp.where((below >= 0) & (lane < KB) & ((row & 7) < HEADS), hits, 0)
    upto = hits
    for s in (1, 2, 4, 8, 16):
        upto = upto + jnp.where(lane >= s, pltpu.roll(upto, s, 1), 0)
    slot = jnp.where(hits > 0, upto - 1, -1)
    code = lane + KB * below
    packed = jnp.full(shape, -KB * 1024, I32)
    for b in range(KB):
        at = jnp.broadcast_to(slot[:, b : b + 1], shape) == lane
        packed = jnp.where(at, jnp.broadcast_to(code[:, b : b + 1], shape), packed)
    number = jnp.broadcast_to(upto[:, KB - 1 : KB], shape)
    return jnp.where(lane == KB, number, packed)


def near_groups(z, c):
    return [((z + d) % NZ) * 2 + (c + e) % 2 for d in range(NZ) for e in range(2)]


def slot_of(block, z, c):
    source = block >> 2
    return (((z + NZ - (source >> 1)) & (NZ - 1)) << 1) + ((source & 1) ^ c)


def blocks_out(goes, rep, groups):
    goes_to = [goes[rep * QB + b] for b in range(QB)]
    leaving = []
    for group in groups:
        b = jnp.int32(0)
        for other in range(1, QB):
            b = jnp.where(goes_to[other] == group, other, b)
        leaving.append(b)
    return leaving


def blocks_in(goes, rep):
    def look(j, state):
        found, *at = state
        hit = goes[j] == rep
        at = [jnp.where(hit & (found == s), j, a) for s, a in enumerate(at)]
        return (found + hit.astype(I32), *at)

    _, *blocks = lax.fori_loop(0, 2 * NZ * QB, look, (jnp.int32(0),) * (1 + QB))
    return blocks


def spread_kernel(
    target, q, k, v, ks, vs, pattern,
    q_fore, q_rest, keys, values, factors, lists,
    held0, held1, held2, held3, packed, came0, came1, came2, came3,
    v_land, scales, k_loc, v_loc, listed, goes,
    z_send, z_recv, q_send, q_recv, r_send, r_recv, y_send, y_recv, t_send, t_recv, k_send, k_recv, v_send, v_recv, s_send, s_recv,
    kc_send, kc_recv, vc_send, vc_recv, own,
):
    rep, z, c, x, y = place()
    sib = (rep + 1 - 2 * c, x * NY + y)
    xs = [(x + d) % NX for d in range(NX)]
    back = [(x + NX - d) % NX for d in range(NX)]
    at_x = [(rep, xs[d] * NY + y) for d in range(NX)]
    at_y = [(rep, x * NY + (y + d) % NY) for d in range(NY)]
    half = pl.ds(pl.multiple_of(c * (KEYS // 2), KEYS // 2), KEYS // 2)
    groups = near_groups(z, c)
    at_group = [(g, x * NY + y) for g in groups]
    held = (held0, held1, held2, held3)
    came = (came0, came1, came2, came3)

    def cols(d, n):
        return pl.ds(pl.multiple_of(xs[d] * n, n), n)

    def fore(d):
        return q.at[:, :, pl.ds(pl.multiple_of(xs[d] * SLICE, D), FORE)]

    def rest(d):
        return q.at[:, :, pl.ds(pl.multiple_of(xs[d] * SLICE + FORE, D), REST)]

    partners = at_group[1:] + at_x[1:] + at_y[1:]
    barrier = pltpu.get_barrier_semaphore()
    for who in partners:
        pl.semaphore_signal(barrier, inc=1, device_id=who, device_id_type=MESH)
    stay = [
        pltpu.make_async_copy(target, goes, own.at[0]),
        pltpu.make_async_copy(fore(0), held[0], own.at[1]),
        pltpu.make_async_copy(ks, k_loc, own.at[2]),
        pltpu.make_async_copy(vs, v_loc, own.at[3]),
        pltpu.make_async_copy(pattern.at[pl.ds(x * HEADS, HEADS)], listed, own.at[4]),
        pltpu.make_async_copy(k.at[:, cols(0, D)], keys.at[x], own.at[5]),
        pltpu.make_async_copy(v.at[:, cols(0, D)], v_land.at[0], own.at[6]),
        pltpu.make_async_copy(rest(0), q_rest.at[y, x], own.at[7]),
    ]
    for copy in stay:
        copy.start()

    qx, rx, kx, vx, sx, kc, vc = ([None] * NX for _ in range(7))
    qy, ry = ([[None] * NY for _ in range(NX)] for _ in range(2))
    qz = [[None] * len(groups) for _ in range(NX)]

    stay[0].wait()
    leaving = blocks_out(goes, rep, groups)

    def pack(d):
        for n in ORDER:
            block = held[d][leaving[n]]
            if n == 0:
                came[d][n] = block
            else:
                packed[d, n] = block

    def over_z(d):
        for n in ORDER[:-1]:
            qz[d][n] = remote(packed.at[d, n], came[d].at[n], z_send.at[d, n], z_recv.at[d, n], at_group[n])
            qz[d][n].start()

    stay[1].wait()
    pack(0)
    scales[0] = jnp.zeros((2 * NX, 128), F32)
    stay[2].wait()
    stay[3].wait()
    scales[0, 0:NX, 0:SHARD] = k_loc[...]
    scales[0, NX : 2 * NX, 0:SHARD] = v_loc[...]

    pl.semaphore_wait(barrier, len(partners))
    for d in FAR:
        qx[d] = remote(fore(d), held[d], q_send.at[d], q_recv.at[d], at_x[d])
        qx[d].start()
    over_z(0)
    for d in FAR:
        rx[d] = remote(rest(d), q_rest.at[y, x], r_send.at[d], r_recv.at[d], at_x[d])
        rx[d].start()
    for d in FAR:
        sx[d] = remote(scales.at[0], scales.at[d], s_send.at[d], s_recv.at[d], at_x[d])
        sx[d].start()
    for d in FAR:
        kx[d] = remote(k.at[half, cols(d, D)], keys.at[x, half], k_send.at[d], k_recv.at[d], at_x[d])
        vx[d] = remote(v.at[half, cols(d, D)], v_land.at[d, half], v_send.at[d], v_recv.at[d], at_x[d])
        kx[d].start()
        vx[d].start()

    for d in FAR:
        qx[d].wait_recv()
        pack(d)
        over_z(d)
    blocks = blocks_in(goes, rep)

    stay[4].wait()
    lists[...] = block_lists(listed, blocks, rep, y)

    scale_row = iota((2 * NX, 128), 0)

    def pick_row(tile, n):
        return jnp.sum(jnp.where(scale_row == n, tile, 0.0), axis=0, keepdims=True)

    def finish(d):
        tile = scales[d]
        for_keys = pick_row(tile, x) * TO_LOG2
        for_values = pick_row(tile, NX + x)
        for b in range(SHARD):
            at = back[d] * SHARD + b
            factors[at] = jnp.broadcast_to(for_keys[:, b : b + 1], (8, 128))
            rows = slice(b * B, (b + 1) * B)
            scaled = v_land[d, rows].astype(F32) * jnp.broadcast_to(for_values[:, b : b + 1], (B, D))
            values[at] = scaled.astype(BF16).T

    def hand_over(d):
        kx[d].wait_recv()
        piece = keys.at[back[d], half]
        kc[d] = remote(piece, piece, kc_send.at[d], kc_recv.at[d], sib)
        kc[d].start()
        vx[d].wait_recv()
        vc[d] = remote(v_land.at[d, half], v_land.at[d, half], vc_send.at[d], vc_recv.at[d], sib)
        vc[d].start()
        sx[d].wait_recv()

    def whole(d):
        kc[d].wait_recv()
        vc[d].wait_recv()
        finish(d)

    def over_y(d):
        for n in range(1, len(groups)):
            qz[d][n].wait_recv()
        for s in range(QB):
            q_fore[y, back[d], s] = came[d][slot_of(blocks[s], z, c)]
        for e in FAR:
            piece = q_fore.at[y, back[d]]
            qy[d][e] = remote(piece, piece, y_send.at[d, e], y_recv.at[d, e], at_y[e])
            qy[d][e].start()

    stay[7].wait()
    for d in (0, *FAR):
        if d:
            rx[d].wait_recv()
        for e in FAR:
            piece = q_rest.at[y, back[d]]
            ry[d][e] = remote(piece, piece, t_send.at[d, e], t_recv.at[d, e], at_y[e])
            ry[d][e].start()
    for copy in stay[5:7]:
        copy.wait()
    finish(0)
    hand_over(1)
    hand_over(3)
    over_y(0)
    whole(1)
    over_y(1)
    whole(3)
    over_y(3)
    over_y(2)
    hand_over(2)
    whole(2)
    for d in range(NX):
        for e in FAR:
            for copy in (qy[d][e], ry[d][e]):
                copy.wait_recv()
                copy.wait_send()
    for d in FAR:
        for copy in (qx[d], rx[d], kx[d], vx[d], sx[d], kc[d], vc[d]):
            copy.wait_send()
    for copies in qz:
        for copy in copies[1:]:
            copy.wait_send()


def spread(target, q, k, v, ks, vs, pattern):
    slots = pltpu.VMEM((2 * NZ, ROWS, FORE), BF16)
    return pl.pallas_call(
        spread_kernel,
        out_shape=[
            jax.ShapeDtypeStruct((NY, NX, QB, ROWS, FORE), BF16),
            jax.ShapeDtypeStruct((NY, NX, QB, ROWS, REST), BF16),
            jax.ShapeDtypeStruct((NX, KEYS, D), BF16),
            jax.ShapeDtypeStruct((KB, D, B), BF16),
            jax.ShapeDtypeStruct((KB, 8, 128), F32),
            jax.ShapeDtypeStruct((PAIRS, 128), I32),
        ],
        in_specs=[HBM] * 7,
        out_specs=[VMEM] * 6,
        scratch_shapes=[pltpu.VMEM((QB, ROWS, FORE), BF16)] * NX
        + [pltpu.VMEM((NX, 2 * NZ, ROWS, FORE), BF16)]
        + [slots] * NX
        + [
            pltpu.VMEM((NX, KEYS, D), BF16),
            pltpu.VMEM((NX, 2 * NX, 128), F32),
            pltpu.VMEM((NX, SHARD), F32),
            pltpu.VMEM((NX, SHARD), F32),
            pltpu.VMEM((HEADS, *pattern.shape[1:]), I32),
            pltpu.SMEM(target.shape, I32),
        ]
        + [DMA((NX, 2 * NZ))] * 2
        + [DMA((NX,))] * 4
        + [DMA((NX, NY))] * 4
        + [DMA((NX,))] * 10
        + [DMA((8,))],
        compiler_params=pltpu.CompilerParams(
            collective_id=0, has_side_effects=True, vmem_limit_bytes=24 << 20
        ),
        name="spread",
    )(target, q, k, v, ks, vs, pattern)


def attend_kernel(
    ints, q_fore, q_rest, keys, values, factors, out_fore, out_rest, extra_out,
    qs, sc, mx, acc, su, extra, items,
):
    row = iota((B, B), 1)
    row = ((row >> 3) & 3) * PART + (row >> 5) * ROWS + (row & 7)
    ahead = iota((B, B), 0) - row
    extra[...] = jnp.zeros((B, B), F32)
    qs[HEADS] = jnp.zeros((D, B), BF16)

    def tall(tile):
        return jnp.broadcast_to(tile[None], (B // 8, 8, B)).reshape(B, B)

    @pl.loop(0, QB // TOGETHER)
    def _(part_of):
        def add_pair(r, n):
            def add(t, n):
                items[n] = r * 16 + t
                return n + 1

            return lax.fori_loop(0, (ints[part_of * LANES + r, KB] + 1) // 2, add, n)

        n = lax.fori_loop(0, LANES, add_pair, jnp.int32(0))
        for g in range(STEP):
            items[n + g] = HEADS * 16
        count = (n + STEP - 1) // STEP
        for j in range(TOGETHER):
            for q_ref, low, high in ((q_fore, 0, EARLY), (q_rest, EARLY, HEADS)):
                rows = q_ref[:, :, part_of * TOGETHER + j].astype(F32).reshape(B, (high - low) * D)
                rows = rows.astype(BF16)
                for h in range(low, high):
                    qs[j * 8 + h] = rows[:, (h - low) * D : (h - low + 1) * D].T
        mx[...] = jnp.full(mx.shape, NEG, F32)
        acc[...] = jnp.zeros(acc.shape, F32)
        su[...] = jnp.zeros(su.shape, F32)

        def item_at(i, g):
            item = items[i * STEP + g]
            r, t = item >> 4, item & 15
            codes = [ints[part_of * LANES + r, t * 2 + u] for u in range(2)]
            return r, codes, [code & (KB - 1) for code in codes]

        @pl.loop(0, count)
        def _(i):
            for g in range(STEP):
                r, codes, kbs = item_at(i, g)
                both = jnp.dot(
                    jnp.concatenate([keys[kb] for kb in kbs], axis=0), qs[r], preferred_element_type=F32
                )
                top = mx[r]
                for u in range(2):
                    score = both[u * B : (u + 1) * B] * tall(factors[kbs[u]])
                    score = jnp.where(ahead <= (codes[u] >> 5) * B, score, NEG)
                    sc[(i * STEP + g) * 2 + u] = score
                    top = jnp.maximum(top, jnp.max(score.reshape(B // 8, 8, B), axis=0))
                mx[r] = top

        for j in range(TOGETHER):
            for h in range(HEADS):
                top = jnp.max(mx[j * 8 + h], axis=0, keepdims=True)
                mx[j * 8 + h] = jnp.broadcast_to(top, (8, B)).astype(BF16).astype(F32)

        @pl.loop(0, count)
        def _(i):
            for g in range(STEP):
                r, codes, kbs = item_at(i, g)
                top = tall(mx[r])
                weights = [jnp.exp2(sc[(i * STEP + g) * 2 + u] - top) for u in range(2)]
                su[r] += jnp.sum((weights[0] + weights[1]).reshape(B // 8, 8, B), axis=0)
                acc[r] += jnp.dot(
                    jnp.concatenate([values[kb] for kb in kbs], axis=1),
                    jnp.concatenate([w.astype(BF16) for w in weights], axis=0),
                    preferred_element_type=F32,
                )

        for j in range(TOGETHER):
            for h in range(HEADS):
                r = j * 8 + h
                at = part_of * LANES + r
                extra[pl.ds(at, 1), :] = mx[r][0:1]
                extra[pl.ds(SUM_LANE + at, 1), :] = jnp.sum(su[r], axis=0, keepdims=True)
                part = acc[r].astype(BF16).T
                out, i = (out_fore, h) if h < EARLY else (out_rest, h - EARLY)
                for d in range(NY):
                    out[d, part_of * TOGETHER + j, :, i * D : (i + 1) * D] = part[d * PART : (d + 1) * PART]

    turned = extra[...].T
    for d in range(NY):
        extra_out[d] = turned[d * PART : (d + 1) * PART].astype(BF16)


def attend(lists, q_fore, q_rest, keys, values, factors):
    most = TOGETHER * HEADS * KB // 2 + STEP
    return pl.pallas_call(
        attend_kernel,
        out_shape=[
            jax.ShapeDtypeStruct((NY, QB, PART, FORE), BF16),
            jax.ShapeDtypeStruct((NY, QB, PART, REST), BF16),
            jax.ShapeDtypeStruct((NY, PART, 128), BF16),
        ],
        in_specs=[SMEM] + [VMEM] * 5,
        out_specs=[VMEM] * 3,
        scratch_shapes=[
            pltpu.VMEM((LANES, D, B), BF16),
            pltpu.VMEM((2 * most, B, B), F32),
            pltpu.VMEM((LANES, 8, B), F32),
            pltpu.VMEM((LANES, D, B), F32),
            pltpu.VMEM((LANES, 8, B), F32),
            pltpu.VMEM((B, B), F32),
            pltpu.SMEM((most,), I32),
        ],
        compiler_params=pltpu.CompilerParams(vmem_limit_bytes=46 << 20),
        name="attend",
    )(lists, q_fore, q_rest, keys.reshape(KB, B, D), values, factors)


def gather_kernel(
    target, p, p_rest, extra_in, out,
    parts, parts_rest, extra, att, att_rest, held, packed, came, goes,
    e_send, e_recv, y_send, y_recv, t_send, t_recv, x_send, x_recv, r_send, r_recv, z_send, z_recv, own,
):
    rep, z, c, x, y = place()
    xs = [(x + d) % NX for d in range(NX)]
    back = [(x + NX - d) % NX for d in range(NX)]
    ys = [(y + d) % NY for d in range(NY)]
    at_x = [(rep, xs[d] * NY + y) for d in range(NX)]
    at_y = [(rep, x * NY + ys[d]) for d in range(NY)]
    groups = near_groups(z, c)
    at_group = [(g, x * NY + y) for g in groups]
    partners = at_group[1:] + at_x[1:] + at_y[1:]
    barrier = pltpu.get_barrier_semaphore()
    for who in partners:
        pl.semaphore_signal(barrier, inc=1, device_id=who, device_id_type=MESH)
    told = pltpu.make_async_copy(target, goes, own.at[QB])
    told.start()
    pl.semaphore_wait(barrier, len(partners))

    ex, ty, rx = ([None] * NY for _ in range(3))
    py = [[None] * NY for _ in range(QB)]
    px = [[None] * NX for _ in range(QB)]
    pz = [None] * len(groups)
    for d in FAR:
        ex[d] = remote(extra_in.at[ys[d]], extra.at[d], e_send.at[d], e_recv.at[d], at_y[d])
        ex[d].start()
        ty[d] = remote(p_rest.at[ys[d]], parts_rest.at[d], t_send.at[d], t_recv.at[d], at_y[d])
        ty[d].start()
    for b in range(QB):
        for d in FAR:
            py[b][d] = remote(p.at[ys[d], b], parts.at[d, b], y_send.at[b, d], y_recv.at[b, d], at_y[d])
            py[b][d].start()
    told.wait()
    leaving = blocks_out(goes, rep, groups)
    blocks = blocks_in(goes, rep)
    for d in FAR:
        ex[d].wait_recv()
    marks = [extra_in[y].astype(F32)] + [extra[d].astype(F32) for d in range(1, NY)]
    top = functools.reduce(jnp.maximum, marks)
    shift = [jnp.exp2(e - top) for e in marks]
    total = sum(w * pltpu.roll(e, SUM_LANE, 1) for w, e in zip(shift, marks))
    lane = iota((PART, 128), 1)
    total = jnp.where((lane < QB * 8) & ((lane & 7) < HEADS), total, 1.0)
    ratio = [w / total for w in shift]

    def quotient(b, h, mine, theirs, cols):
        at = b * 8 + h
        value = sum(
            jnp.broadcast_to(ratio[d][:, at : at + 1], (PART, D))
            * (theirs[d, b, :, cols] if d else mine[y, b, :, cols]).astype(F32)
            for d in range(NY)
        )
        return value.reshape(NX, ROWS, D).astype(BF16)

    for d in FAR:
        ty[d].wait_recv()
    for b in range(QB):
        for h in range(EARLY, HEADS):
            cols = slice((h - EARLY) * D, (h - EARLY + 1) * D)
            value = quotient(b, h, p_rest, parts_rest, cols)
            for d in range(NX):
                att_rest[d, b, :, cols] = value[d]
    for d in FAR:
        rx[d] = remote(att_rest.at[xs[d]], held.at[d], r_send.at[d], r_recv.at[d], at_x[d])
        rx[d].start()
    held[0] = att_rest[x]
    mine = pl.ds(pl.multiple_of(x * SLICE, D), FORE)
    for b in range(QB):
        if b == 1:
            for d in FAR:
                rx[d].wait_recv()
            for n in ORDER:
                for d in range(NX):
                    block = held[d, leaving[n]]
                    if n == 0:
                        came[n, d] = block
                    else:
                        packed[n, d] = block
                if n > 0:
                    pz[n] = remote(packed.at[n], came.at[n], z_send.at[n], z_recv.at[n], at_group[n])
                    pz[n].start()
        for d in FAR:
            py[b][d].wait_recv()
        for h in range(EARLY):
            cols = slice(h * D, (h + 1) * D)
            value = quotient(b, h, p, parts, cols)
            for d in range(NX):
                att[b, d, :, cols] = value[d]
        for d in FAR:
            px[b][d] = remote(
                att.at[b, xs[d]], out.at[b, :, mine], x_send.at[b, d], x_recv.at[b, d], at_x[d]
            )
            px[b][d].start()
        px[b][0] = pltpu.make_async_copy(att.at[b, x], out.at[b, :, mine], own.at[b])
        px[b][0].start()

    for n in range(1, len(groups)):
        pz[n].wait_recv()
    for b in range(QB):
        px[b][0].wait()
        for d in FAR:
            px[b][d].wait_recv()
    for s in range(QB):
        n = slot_of(blocks[s], z, c)
        for d in range(NX):
            out[s, :, pl.ds(pl.multiple_of(back[d] * SLICE + FORE, D), REST)] = came[n, d]

    for n in range(1, len(groups)):
        pz[n].wait_send()
    for d in FAR:
        for copy in (ex[d], ty[d], rx[d]):
            copy.wait_send()
        for b in range(QB):
            px[b][d].wait_send()
            py[b][d].wait_send()


def gather(target, p, p_rest, extra):
    slots = pltpu.VMEM((2 * NZ, NX, ROWS, REST), BF16)
    return pl.pallas_call(
        gather_kernel,
        out_shape=jax.ShapeDtypeStruct((QB, ROWS, NX * SLICE), BF16),
        in_specs=[HBM, VMEM, VMEM, VMEM],
        out_specs=VMEM,
        scratch_shapes=[
            pltpu.VMEM((NY, QB, PART, FORE), BF16),
            pltpu.VMEM((NY, QB, PART, REST), BF16),
            pltpu.VMEM((NY, PART, 128), BF16),
            pltpu.VMEM((QB, NX, ROWS, FORE), BF16),
            pltpu.VMEM((NX, QB, ROWS, REST), BF16),
            pltpu.VMEM((NX, QB, ROWS, REST), BF16),
            slots,
            slots,
            pltpu.SMEM(target.shape, I32),
        ]
        + [DMA((NY,))] * 2
        + [DMA((QB, NY))] * 2
        + [DMA((NY,))] * 2
        + [DMA((QB, NX))] * 2
        + [DMA((NX,))] * 2
        + [DMA((2 * NZ,))] * 2
        + [DMA((QB + 1,))],
        compiler_params=pltpu.CompilerParams(
            collective_id=1, has_side_effects=True, vmem_limit_bytes=16 << 20
        ),
        name="gather",
    )(target, p, p_rest, extra)


def hbm(array):
    return pltpu.with_memory_space_constraint(array, pltpu.HBM)


def per_device(queries, key_cache, value_cache, key_scale, value_scale, pattern, target):
    target = hbm(target)
    q_fore, q_rest, keys, values, factors, lists = spread(
        target,
        hbm(queries),
        hbm(key_cache),
        hbm(value_cache),
        hbm(key_scale.T),
        hbm(value_scale.T),
        hbm(jnp.swapaxes(pattern, 1, 2)),
    )
    part, rest, extra = attend(lists, q_fore, q_rest, keys, values, factors)
    return gather(target, part, rest, extra)


def solution(mesh):
    return jax.shard_map(
        per_device,
        mesh=mesh,
        in_specs=(
            P("replica", "ctx", None),
            P("ctx", None),
            P("ctx", None),
            P("ctx", None),
            P("ctx", None),
            P(),
            P(),
        ),
        out_specs=P("replica", "ctx", None),
        check_vma=False,
    )
```
